256 devices in a mesh: col: 8 (over y_lo, x), row: 32 (over z, y_hi, core).
Axes of the slice: x: 4, y: 4 (y_hi: 2, y_lo: 2; y = y_hi * 2 + y_lo), z: 8, core: 2. Of those that a mesh axis runs over, the one named last changes fastest.
Arguments:
- images: bfloat16 [256, 16, 16, 1536], P(('col', 'row')), may hold values from -6 to 6
- hidden_cot: bfloat16 [256, 256, 3072], P(('col', 'row')), may hold values from -6 to 6
- residual_cot: bfloat16 [256, 16, 16, 1536], P(('col', 'row')), may hold values from -6 to 6
- w_up: bfloat16 [1536, 3072], replicated, may hold values from -0.15625 to 0.15625
- b_up: float32 [3072], replicated, may hold values from -3 to 3
- ln_gain: float32 [1536], replicated, may hold values from 0.1 to 1.9
- ln_bias: float32 [1536], replicated, may hold values from -3 to 3
- dw_weight: float32 [49, 1536], replicated, may hold values from -0.875 to 0.875
- dw_bias: float32 [1536], replicated, may hold values from -3 to 3
Outputs:
- grad_input: bfloat16 [256, 16, 16, 1536], P(('col', 'row'))
- grad_w_up: float32 [1536, 3072], P(('col', 'row'))
- grad_b_up: float32 [3072], replicated
- grad_ln_gain: float32 [1536], replicated
- grad_ln_bias: float32 [1536], replicated
- grad_dw_weight: float32 [49, 1536], replicated
- grad_dw_bias: float32 [1536], replicated
The draws below stay inside these ranges and needn't reach their ends.
All inputs are finite; a program needn't handle non-finite values.
Results may differ from the reference program's by a relative error of at most 0.007.
Values may be sent and summed in bfloat16 or wider, within the bound.
No kernel may reach another device: no remote copies, remote signals or barrier semaphores. Data moves between devices by JAX's collectives and lax.ppermute only.
A program may use at most 128 MiB of HBM per device.

```python
import jax
import jax.numpy as jnp
from jax import lax

C = 1536
HID = 3072
SIDE = 16
IMAGES = 256


def block_levels(own_key, shape, shards, low, largest):
    level, own = 1.0, jax.random.fold_in(own_key, 6)
    for dim, blocks in shards:
        steps = jnp.exp(jax.random.uniform(jax.random.fold_in(own, dim), (blocks,), jnp.float32, low / len(shards), largest / len(shards)))
        level = level * jnp.repeat(steps, shape[dim] // blocks).reshape([-1 if axis == dim else 1 for axis in range(len(shape))])
    return level


def gaussian(stream_key, shape, deviation, limit, pieces=(), held_as=jnp.bfloat16):
    entries = jax.random.normal(stream_key, shape, jnp.float32) * deviation
    if len(pieces) > 0:
        entries = block_levels(stream_key, shape, pieces, -0.22, 0.18) * entries
    return jnp.clip(entries, min=-limit, max=limit).astype(held_as)


def setup_inputs(seed: int = 0) -> dict:
    splits = jax.random.split(jax.random.key(seed), 10)
    return {
        "images": gaussian(splits[0], (IMAGES, SIDE, SIDE, C), 1.0, 6.0, ((0, 256),)),
        "hidden_cot": gaussian(splits[1], (IMAGES, SIDE * SIDE, HID), 1.0, 6.0, ((0, 256),)),
        "residual_cot": gaussian(splits[2], (IMAGES, SIDE, SIDE, C), 1.0, 6.0, ((0, 256),)),
        "w_up": gaussian(splits[3], (C, HID), C ** -0.5, 0.15625),
        "b_up": gaussian(splits[4], (HID,), 0.5, 3.0, (), jnp.float32),
        "ln_gain": jnp.clip(1.0 + 0.18 * jax.random.normal(splits[5], (C,), jnp.float32), 0.1, 1.9),
        "ln_bias": gaussian(splits[6], (C,), 0.5, 3.0, (), jnp.float32),
        "dw_weight": gaussian(splits[7], (49, C), 49 ** -0.5, 0.875, (), jnp.float32),
        "dw_bias": gaussian(splits[8], (C,), 0.5, 3.0, (), jnp.float32),
    }


def depthwise(padded, dw_weight, side_cells):
    running = jnp.zeros(padded.shape[:1] + (side_cells, side_cells, padded.shape[3]), jnp.float32)
    for tap_row in range(7):
        for tap_col in range(7):
            running = running + padded[:, tap_row:tap_row + side_cells, tap_col:tap_col + side_cells, :] * dw_weight[tap_row * 7 + tap_col]
    return running

def local_backward(images, hidden_cot, residual_cot, w_up, b_up, ln_gain, ln_bias, dw_weight, dw_bias):
    side_cells = images.shape[1]
    feat_width = images.shape[3]
    padded = jnp.pad(images.astype(jnp.float32), ((0, 0), (3, 3), (3, 3), (0, 0)))
    conv_out = depthwise(padded, dw_weight, side_cells) + dw_bias
    centred = conv_out - lax.optimization_barrier(jnp.mean(conv_out, axis=-1, keepdims=True))
    inv_sigma = lax.rsqrt(lax.optimization_barrier(jnp.mean(centred * centred, axis=-1, keepdims=True)) + 1e-06)
    unit_vals = centred * inv_sigma
    normed = (unit_vals * ln_gain + ln_bias).astype(jnp.bfloat16).reshape(-1, feat_width)
    pre_act = jnp.dot(normed, w_up, preferred_element_type=jnp.float32) + b_up
    gelu_slope = 0.5 * (1.0 + lax.erf(pre_act * 0.7071067811865476)) + pre_act * jnp.exp(-0.5 * pre_act * pre_act) * 0.3989422804014327
    pre_grad = (hidden_cot.reshape(pre_act.shape).astype(jnp.float32) * gelu_slope).astype(jnp.bfloat16)
    normed_grad = lax.dot_general(pre_grad, w_up, (((1,), (1,)), ((), ())), preferred_element_type=jnp.float32)
    unit_flat = unit_vals.reshape(-1, feat_width)
    grad_gain = lax.optimization_barrier(jnp.sum(normed_grad * unit_flat, axis=0))
    grad_shift = lax.optimization_barrier(jnp.sum(normed_grad, axis=0))
    grad_bias_up = lax.optimization_barrier(jnp.sum(pre_grad.astype(jnp.float32), axis=0))
    unit_grad = (normed_grad * ln_gain).reshape(unit_vals.shape)
    conv_grad = inv_sigma * (unit_grad - lax.optimization_barrier(jnp.mean(unit_grad, axis=-1, keepdims=True)) - unit_vals * lax.optimization_barrier(jnp.mean(unit_grad * unit_vals, axis=-1, keepdims=True)))
    grad_conv_bias = lax.optimization_barrier(jnp.sum(conv_grad, axis=(0, 1, 2)))
    tap_sums = []
    for tap_row in range(7):
        for tap_col in range(7):
            window = padded[:, tap_row:tap_row + side_cells, tap_col:tap_col + side_cells, :]
            tap_sums.append(lax.optimization_barrier(jnp.sum(conv_grad * window, axis=(0, 1, 2))))
    grad_filter = jnp.stack(tap_sums)
    grad_padded = jnp.pad(conv_grad, ((0, 0), (3, 3), (3, 3), (0, 0)))
    input_grad = residual_cot.astype(jnp.float32)
    for tap_row in range(7):
        for tap_col in range(7):
            input_grad = input_grad + grad_padded[:, 6 - tap_row:6 - tap_row + side_cells, 6 - tap_col:6 - tap_col + side_cells, :] * dw_weight[tap_row * 7 + tap_col]
    return (input_grad.astype(jnp.bfloat16), normed, pre_grad, (grad_bias_up, grad_gain, grad_shift, grad_filter, grad_conv_bias))

def reference(images, hidden_cot, residual_cot, w_up, b_up, ln_gain, ln_bias, dw_weight, dw_bias):

    def one_image(running, image_items):
        image, cot_rows, res_rows = image_items
        grad_input, normed, pre_grad, smalls = local_backward(image[None], cot_rows[None], res_rows[None], w_up, b_up, ln_gain, ln_bias, dw_weight, dw_bias)
        rank_term = lax.dot_general(normed, pre_grad, (((0,), (0,)), ((), ())), preferred_element_type=jnp.float32)
        updated = (running[0] + rank_term,) + tuple((left + right for left, right in zip(running[1:], smalls)))
        return (updated, grad_input[0])
    initial = (jnp.zeros((C, HID), jnp.float32), jnp.zeros((HID,), jnp.float32), jnp.zeros((C,), jnp.float32), jnp.zeros((C,), jnp.float32), jnp.zeros((49, C), jnp.float32), jnp.zeros((C,), jnp.float32))
    totals, grad_input = lax.scan(one_image, initial, (images, hidden_cot, residual_cot))
    inverse_count = 1.0 / IMAGES
    return (grad_input, totals[0] * inverse_count, totals[1] * inverse_count, totals[2] * inverse_count, totals[3] * inverse_count, totals[4] * inverse_count, totals[5] * inverse_count)
```

```python
import jax
import jax.numpy as jnp
import numpy as np
from jax import lax
from jax.experimental import pallas as pl
from jax.experimental.pallas import tpu as pltpu
from jax.sharding import Mesh
from jax.sharding import PartitionSpec as P

LANES = 128
EDGE = 8
VMEM_LIMIT = 60 * 1024 * 1024


def conv_norm_kernel(
    image_ref, taps_ref, bias_ref, gain_ref, shift_ref, order_ref,
    unit_ref, sigma_ref, normed_ref, turned_ref, padded, conv,
):
    side, feat = image_ref.shape[1], image_ref.shape[3]
    blank = jnp.zeros((side, EDGE, LANES), jnp.float32)
    padded[:, 0:EDGE, :] = blank
    padded[:, EDGE + side : EDGE + side + EDGE, :] = blank

    @pl.loop(0, feat // LANES)
    def _(block):
        lanes = pl.ds(pl.multiple_of(block * LANES, LANES), LANES)
        padded[:, EDGE : EDGE + side, :] = image_ref[0, :, :, lanes].astype(jnp.float32)
        start = jnp.broadcast_to(bias_ref[:, lanes], (side, LANES))
        sums = [start] * side
        for tap_col in range(7):
            weights = [
                jnp.broadcast_to(taps_ref[pl.ds(7 * tap_row + tap_col, 1), lanes], (side, LANES))
                for tap_row in range(7)
            ]
            for source in range(side):
                cells = padded[source, EDGE - 3 + tap_col : EDGE - 3 + tap_col + side, :]
                for tap_row in range(7):
                    target = source + 3 - tap_row
                    if 0 <= target < side:
                        sums[target] = sums[target] + cells * weights[tap_row]
        for row in range(side):
            conv[row * side : (row + 1) * side, lanes] = sums[row]

    @pl.loop(0, side)
    def _(row):
        cells = pl.ds(pl.multiple_of(row * side, side), side)
        values = conv[cells, :]
        centred = values - jnp.mean(values, axis=-1, keepdims=True)
        inv_sigma = lax.rsqrt(jnp.mean(centred * centred, axis=-1, keepdims=True) + 1e-06)
        unit = centred * inv_sigma
        unit_ref[cells, :] = unit
        sigma_ref[cells, :] = jnp.broadcast_to(inv_sigma, (side, LANES))
        normed_ref[cells, :] = (unit * gain_ref[...] + shift_ref[...]).astype(jnp.bfloat16)

    width = order_ref.shape[0]
    rows = turned_ref.shape[3]
    for group in range(feat // width):
        y_lo, pair = divmod(group, 2)
        turned = lax.dot_general(
            order_ref[...],
            normed_ref[:, group * width : (group + 1) * width],
            (((1,), (1,)), ((), ())),
            preferred_element_type=jnp.float32,
        ).astype(jnp.bfloat16)
        for within in range(2):
            for y_hi in range(2):
                first = (within * 2 + y_hi) * rows
                turned_ref[2 * pair + within, y_hi, y_lo] = turned[first : first + rows]


def channel_order(rows, along_z):
    width = 4 * rows
    owned = rows // along_z
    target = np.arange(width).reshape(2, along_z, 2, owned).transpose(0, 2, 1, 3).reshape(-1)
    return jnp.asarray(np.eye(width, dtype=np.float32)[target], jnp.bfloat16)


def conv_norm(image, taps, bias, gain, shift, along_z):
    side, feat = image.shape[1], image.shape[3]
    cells = side * side
    rows = feat // 16
    order = channel_order(rows, along_z)
    return pl.pallas_call(
        conv_norm_kernel,
        name="conv_norm",
        out_shape=(
            jax.ShapeDtypeStruct((cells, feat), jnp.float32),
            jax.ShapeDtypeStruct((cells, LANES), jnp.float32),
            jax.ShapeDtypeStruct((cells, feat), jnp.bfloat16),
            jax.ShapeDtypeStruct((4, 2, 2, rows, cells), jnp.bfloat16),
        ),
        scratch_shapes=[
            pltpu.VMEM((side, side + 2 * EDGE, LANES), jnp.float32),
            pltpu.VMEM((cells, feat), jnp.float32),
        ],
        compiler_params=pltpu.CompilerParams(vmem_limit_bytes=VMEM_LIMIT),
        cost_estimate=pl.CostEstimate(flops=2 * 49 * cells * feat, bytes_accessed=cells * feat * 8, transcendentals=0),
    )(image, taps, bias.reshape(1, -1), gain.reshape(1, -1), shift.reshape(1, -1), order)


def slope_kernel(half_ref, normed_ref, w_ref, b_ref, cot_ref, grad_ref, sums_ref):
    pre_act = jnp.dot(normed_ref[...], w_ref[...], preferred_element_type=jnp.float32) + b_ref[...]
    slope = 0.5 * (1.0 + lax.erf(pre_act * 0.7071067811865476)) + pre_act * jnp.exp(
        -0.5 * pre_act * pre_act
    ) * 0.3989422804014327
    pre_grad = (cot_ref[0].astype(jnp.float32) * slope).astype(jnp.bfloat16)
    grad_ref[...] = pre_grad
    sums_ref[...] = jnp.sum(pre_grad.astype(jnp.float32), axis=0, keepdims=True)


def gelu_grad(half, normed, w_up, b_up, cot, width=512):
    cells, feat = normed.shape
    hid = w_up.shape[1] // 2
    steps = hid // width

    def block(i, half_ref):
        return half_ref[0] * steps + i

    return pl.pallas_call(
        slope_kernel,
        name="gelu_grad",
        grid_spec=pltpu.PrefetchScalarGridSpec(
            num_scalar_prefetch=1,
            grid=(steps,),
            in_specs=[
                pl.BlockSpec((cells, feat), lambda i, h: (0, 0)),
                pl.BlockSpec((feat, width), lambda i, h: (0, block(i, h))),
                pl.BlockSpec((1, width), lambda i, h: (0, block(i, h))),
                pl.BlockSpec((1, cells, width), lambda i, h: (0, 0, block(i, h))),
            ],
            out_specs=[
                pl.BlockSpec((cells, width), lambda i, h: (0, i)),
                pl.BlockSpec((1, width), lambda i, h: (0, i)),
            ],
        ),
        out_shape=(
            jax.ShapeDtypeStruct((cells, hid), jnp.bfloat16),
            jax.ShapeDtypeStruct((1, hid), jnp.float32),
        ),
        compiler_params=pltpu.CompilerParams(vmem_limit_bytes=VMEM_LIMIT),
        cost_estimate=pl.CostEstimate(
            flops=2 * cells * feat * hid, bytes_accessed=2 * feat * hid, transcendentals=2 * cells * hid
        ),
    )(half, normed, w_up, b_up.reshape(1, -1), cot)


def norm_grad_kernel(
    half_ref, near_ref, far_ref, w_ref, unit_ref, sigma_ref, gain_ref,
    conv_ref, gain_sum_ref, shift_sum_ref, total,
):
    step = pl.program_id(0)
    half_steps = pl.num_programs(0) // 2

    @pl.when(step == 0)
    def _():
        total[...] = jnp.zeros_like(total)

    dims = (((1,), (1,)), ((), ()))

    @pl.when(step < half_steps)
    def _():
        total[...] += lax.dot_general(near_ref[...], w_ref[...], dims, preferred_element_type=jnp.float32)

    @pl.when(step >= half_steps)
    def _():
        total[...] += lax.dot_general(far_ref[...], w_ref[...], dims, preferred_element_type=jnp.float32)

    @pl.when(step == pl.num_programs(0) - 1)
    def _():
        feat = total.shape[1]
        gain_sum_ref[...] = jnp.zeros_like(gain_sum_ref)
        shift_sum_ref[...] = jnp.zeros_like(shift_sum_ref)

        @pl.loop(0, total.shape[0] // 16)
        def _(row):
            cells = pl.ds(pl.multiple_of(row * 16, 16), 16)
            grad = total[cells, :]
            unit = unit_ref[cells, :]
            gain_sum_ref[...] += jnp.sum(grad * unit, axis=0, keepdims=True)
            shift_sum_ref[...] += jnp.sum(grad, axis=0, keepdims=True)
            unit_grad = grad * gain_ref[...]
            first = jnp.sum(unit_grad, axis=-1, keepdims=True) * (1.0 / feat)
            second = jnp.sum(unit_grad * unit, axis=-1, keepdims=True) * (1.0 / feat)
            conv_ref[cells, :] = sigma_ref[cells, 0:1] * (unit_grad - first - unit * second)


def norm_grad(half, near, far, w_up, unit, sigma, gain, width=512):
    cells, feat = unit.shape
    hid = w_up.shape[1]
    steps = hid // width
    hs = steps // 2

    def block(i, half_ref):
        return lax.rem(half_ref[0] * hs + i, steps)

    return pl.pallas_call(
        norm_grad_kernel,
        name="norm_grad",
        grid_spec=pltpu.PrefetchScalarGridSpec(
            num_scalar_prefetch=1,
            grid=(steps,),
            in_specs=[
                pl.BlockSpec((cells, width), lambda i, h: (0, jnp.minimum(i, hs - 1))),
                pl.BlockSpec((cells, width), lambda i, h: (0, jnp.maximum(i - hs, 0))),
                pl.BlockSpec((feat, width), lambda i, h: (0, block(i, h))),
                pl.BlockSpec((cells, feat), lambda i, h: (0, 0)),
                pl.BlockSpec((cells, LANES), lambda i, h: (0, 0)),
                pl.BlockSpec((1, feat), lambda i, h: (0, 0)),
            ],
            out_specs=[
                pl.BlockSpec((cells, feat), lambda i, h: (0, 0)),
                pl.BlockSpec((1, feat), lambda i, h: (0, 0)),
                pl.BlockSpec((1, feat), lambda i, h: (0, 0)),
            ],
            scratch_shapes=[pltpu.VMEM((cells, feat), jnp.float32)],
        ),
        out_shape=(
            jax.ShapeDtypeStruct((cells, feat), jnp.float32),
            jax.ShapeDtypeStruct((1, feat), jnp.float32),
            jax.ShapeDtypeStruct((1, feat), jnp.float32),
        ),
        compiler_params=pltpu.CompilerParams(vmem_limit_bytes=VMEM_LIMIT),
        cost_estimate=pl.CostEstimate(
            flops=2 * cells * feat * hid, bytes_accessed=2 * feat * hid + 8 * cells * feat, transcendentals=0
        ),
    )(half, near, far, w_up, unit, sigma, gain.reshape(1, -1))


def conv_grad_kernel(grad_ref, image_ref, res_ref, taps_ref, out_ref, tap_sum_ref, bias_sum_ref, padded, image):
    side = image_ref.shape[1]
    blank = jnp.zeros((side, EDGE, LANES), jnp.float32)
    padded[:, 0:EDGE, :] = blank
    padded[:, EDGE + side : EDGE + side + EDGE, :] = blank
    image[...] = image_ref[0].astype(jnp.float32)
    bias_sum = jnp.zeros((side, LANES), jnp.float32)
    for row in range(side):
        cells = grad_ref[row * side : (row + 1) * side, :]
        padded[row, EDGE : EDGE + side, :] = cells
        bias_sum = bias_sum + cells
    bias_sum_ref[...] = jnp.sum(bias_sum, axis=0, keepdims=True)
    sums = [res_ref[0, row].astype(jnp.float32) for row in range(side)]
    for turn_col in range(7):
        weights = [
            jnp.broadcast_to(
                taps_ref[pl.ds(7 * (6 - turn_row) + 6 - turn_col, 1), :], (side, LANES)
            )
            for turn_row in range(7)
        ]
        parts = [jnp.zeros((8, LANES), jnp.float32) for _ in range(7)]
        for source in range(side):
            cells = padded[source, EDGE - 3 + turn_col : EDGE - 3 + turn_col + side, :]
            for turn_row in range(7):
                target = source + 3 - turn_row
                if 0 <= target < side:
                    sums[target] = sums[target] + cells * weights[turn_row]
                    product = cells * image[target]
                    parts[turn_row] = parts[turn_row] + (product[:8] + product[8:])
        for turn_row in range(7):
            tap = 7 * (6 - turn_row) + 6 - turn_col
            tap_sum_ref[tap : tap + 1, :] = jnp.sum(parts[turn_row], axis=0, keepdims=True)
    for row in range(side):
        out_ref[0, row] = sums[row].astype(jnp.bfloat16)


def conv_backward(grad, image, residual, taps):
    side, feat = image.shape[1], image.shape[3]
    cells = side * side
    picture = pl.BlockSpec((1, side, side, LANES), lambda i: (0, 0, 0, i))
    return pl.pallas_call(
        conv_grad_kernel,
        name="conv_backward",
        grid=(feat // LANES,),
        in_specs=[
            pl.BlockSpec((cells, LANES), lambda i: (0, i)),
            picture,
            picture,
            pl.BlockSpec((49, LANES), lambda i: (0, i)),
        ],
        out_specs=[
            picture,
            pl.BlockSpec((49, LANES), lambda i: (0, i)),
            pl.BlockSpec((1, LANES), lambda i: (0, i)),
        ],
        out_shape=(
            jax.ShapeDtypeStruct(image.shape, jnp.bfloat16),
            jax.ShapeDtypeStruct((49, feat), jnp.float32),
            jax.ShapeDtypeStruct((1, feat), jnp.float32),
        ),
        scratch_shapes=[
            pltpu.VMEM((side, side + 2 * EDGE, LANES), jnp.float32),
            pltpu.VMEM((side, side, LANES), jnp.float32),
        ],
        compiler_params=pltpu.CompilerParams(vmem_limit_bytes=VMEM_LIMIT),
        cost_estimate=pl.CostEstimate(flops=4 * 49 * cells * feat, bytes_accessed=cells * feat * 10, transcendentals=0),
    )(grad, image, residual, taps)


def product_kernel(near_t_ref, far_t_ref, near_ref, far_ref, out_ref):
    out_ref[0] = (
        jnp.dot(near_t_ref[0], near_ref[...], preferred_element_type=jnp.float32)
        + jnp.dot(far_t_ref[0], far_ref[...], preferred_element_type=jnp.float32)
    ).astype(jnp.bfloat16)


def product(near_t, far_t, near, far):
    blocks, rows, cells = near_t.shape
    columns = near.shape[1]
    left = pl.BlockSpec((1, rows, cells), lambda i: (i, 0, 0))
    right = pl.BlockSpec((cells, columns), lambda i: (0, 0))
    return pl.pallas_call(
        product_kernel,
        name="product",
        grid=(blocks,),
        in_specs=[left, left, right, right],
        out_specs=pl.BlockSpec((1, rows, columns), lambda i: (i, 0, 0)),
        out_shape=jax.ShapeDtypeStruct((blocks, rows, columns), jnp.bfloat16),
        compiler_params=pltpu.CompilerParams(vmem_limit_bytes=VMEM_LIMIT),
        cost_estimate=pl.CostEstimate(
            flops=4 * blocks * rows * cells * columns, bytes_accessed=2 * blocks * rows * columns, transcendentals=0
        ),
    )(near_t, far_t, near, far)


def per_device(images, hidden_cot, residual_cot, w_up, b_up, ln_gain, ln_bias, dw_weight, dw_bias):
    feat, hid = w_up.shape
    everyone = ("y_lo", "x", "z", "y_hi", "core")
    along_z = lax.axis_size("z")
    devices = 1
    for name in everyone:
        devices *= lax.axis_size(name)
    inverse_count = 1.0 / (images.shape[0] * devices)
    mine = lax.axis_index("core").astype(jnp.int32).reshape(1)
    swap = [(0, 1), (1, 0)]

    unit, sigma, normed, turned = conv_norm(images, dw_weight, dw_bias, ln_gain, ln_bias, along_z)
    far_turned = lax.ppermute(turned, "core", swap)
    away, away_sums = gelu_grad(1 - mine, normed, w_up, b_up, hidden_cot)
    far = lax.ppermute(away, "core", swap)
    near, near_sums = gelu_grad(mine, normed, w_up, b_up, hidden_cot)
    cells = normed.shape[0]
    partial = product(turned.reshape(4, -1, cells), far_turned.reshape(4, -1, cells), near, far)

    by_x = lax.psum_scatter(partial.reshape(feat, -1), "x", scatter_dimension=0, tiled=True)
    by_y = lax.psum_scatter(by_x, ("y_hi", "y_lo"), scatter_dimension=0, tiled=True)
    pieces = 2 * along_z
    last = lax.all_to_all(by_y.reshape(pieces, -1, LANES), ("z", "core"), 0, 0, tiled=True)
    last = last.astype(jnp.float32).reshape(along_z, 2, feat // devices, hid // 2)
    owned = jnp.sum(last, axis=0).transpose(1, 0, 2).reshape(feat // devices, hid) * inverse_count

    conv_grad, gain_sum, shift_sum = norm_grad(mine, near, away, w_up, unit, sigma, ln_gain)
    grad_input, tap_sums, bias_sum = conv_backward(conv_grad, images, residual_cot, dw_weight)
    first = jnp.where(mine == 0, near_sums, away_sums)
    second = jnp.where(mine == 0, away_sums, near_sums)
    used = 49 + 3 + hid // feat
    rows = -(-used // 64) * 64
    small = jnp.concatenate(
        [
            tap_sums,
            gain_sum,
            shift_sum,
            bias_sum,
            first.reshape(-1, feat),
            second.reshape(-1, feat),
            jnp.zeros((rows - used, feat), jnp.float32),
        ],
        axis=0,
    )
    small = lax.all_to_all(small.reshape(devices, 1, -1), everyone, 0, 0, tiled=True)
    small = jnp.sum(small, axis=0, keepdims=True) * inverse_count
    small = lax.all_to_all(
        jnp.broadcast_to(small, (devices, 1, small.shape[2])), everyone, 0, 0, tiled=True
    ).reshape(rows, feat)
    return (
        grad_input,
        owned,
        small[52:used].reshape(hid),
        small[49],
        small[50],
        small[:49],
        small[51],
    )


def solution(mesh):
    x, z = 4, mesh.devices.size // 32
    split = Mesh(mesh.devices.reshape(2, x, z, 2, 2), ("y_lo", "x", "z", "y_hi", "core"))
    images = P(("y_lo", "x", "z", "y_hi", "core"))
    return jax.shard_map(
        per_device,
        mesh=split,
        in_specs=(images, images, images, P(), P(), P(), P(), P(), P()),
        out_specs=(images, images, P(), P(), P(), P(), P()),
        check_vma=False,
    )
```

```python
import functools

import jax
import jax.numpy as jnp
import numpy as np
from jax import lax
from jax.experimental import pallas as pl
from jax.experimental.pallas import tpu as pltpu
from jax.sharding import Mesh
from jax.sharding import PartitionSpec as P

LANES = 128
EDGE = 8
VMEM_LIMIT = 60 * 1024 * 1024
SMALL = pl.CostEstimate(flops=1000, bytes_accessed=1000, transcendentals=0)


def conv_norm_kernel(
    image_ref, taps_ref, bias_ref, gain_ref, shift_ref, order_ref,
    unit_ref, sigma_ref, normed_ref, turned_ref, padded, conv,
):
    side, feat = image_ref.shape[1], image_ref.shape[3]
    blank = jnp.zeros((side, EDGE, LANES), jnp.float32)
    padded[:, 0:EDGE, :] = blank
    padded[:, EDGE + side : EDGE + side + EDGE, :] = blank

    @pl.loop(0, feat // LANES)
    def _(block):
        lanes = pl.ds(pl.multiple_of(block * LANES, LANES), LANES)
        padded[:, EDGE : EDGE + side, :] = image_ref[0, :, :, lanes].astype(jnp.float32)
        start = jnp.broadcast_to(bias_ref[:, lanes], (side, LANES))
        sums = [start] * side
        for tap_col in range(7):
            weights = [
                jnp.broadcast_to(taps_ref[pl.ds(7 * tap_row + tap_col, 1), lanes], (side, LANES))
                for tap_row in range(7)
            ]
            for source in range(side):
                cells = padded[source, EDGE - 3 + tap_col : EDGE - 3 + tap_col + side, :]
                for tap_row in range(7):
                    target = source + 3 - tap_row
                    if 0 <= target < side:
                        sums[target] = sums[target] + cells * weights[tap_row]
        for row in range(side):
            conv[row * side : (row + 1) * side, lanes] = sums[row]

    @pl.loop(0, side)
    def _(row):
        cells = pl.ds(pl.multiple_of(row * side, side), side)
        values = conv[cells, :]
        centred = values - jnp.mean(values, axis=-1, keepdims=True)
        inv_sigma = lax.rsqrt(jnp.mean(centred * centred, axis=-1, keepdims=True) + 1e-06)
        unit = centred * inv_sigma
        unit_ref[cells, :] = unit
        sigma_ref[cells, :] = jnp.broadcast_to(inv_sigma, (side, LANES))
        normed_ref[cells, :] = (unit * gain_ref[...] + shift_ref[...]).astype(jnp.bfloat16)

    width = order_ref.shape[0]
    rows = turned_ref.shape[3]
    for group in range(feat // width):
        y_lo, pair = divmod(group, 2)
        turned = lax.dot_general(
            order_ref[...],
            normed_ref[:, group * width : (group + 1) * width],
            (((1,), (1,)), ((), ())),
            preferred_element_type=jnp.float32,
        ).astype(jnp.bfloat16)
        for within in range(2):
            for y_hi in range(2):
                first = (within * 2 + y_hi) * rows
                turned_ref[2 * pair + within, y_hi, y_lo] = turned[first : first + rows]


def channel_order(rows, along_z):
    width = 4 * rows
    owned = rows // along_z
    target = np.arange(width).reshape(2, along_z, 2, owned).transpose(0, 2, 1, 3).reshape(-1)
    return jnp.asarray(np.eye(width, dtype=np.float32)[target], jnp.bfloat16)


def conv_norm(image, taps, bias, gain, shift, along_z):
    side, feat = image.shape[1], image.shape[3]
    cells = side * side
    rows = feat // 16
    order = channel_order(rows, along_z)
    return pl.pallas_call(
        conv_norm_kernel,
        name="conv_norm",
        out_shape=(
            jax.ShapeDtypeStruct((cells, feat), jnp.float32),
            jax.ShapeDtypeStruct((cells, LANES), jnp.float32),
            jax.ShapeDtypeStruct((cells, feat), jnp.bfloat16),
            jax.ShapeDtypeStruct((4, 2, 2, rows, cells), jnp.bfloat16),
        ),
        scratch_shapes=[
            pltpu.VMEM((side, side + 2 * EDGE, LANES), jnp.float32),
            pltpu.VMEM((cells, feat), jnp.float32),
        ],
        compiler_params=pltpu.CompilerParams(vmem_limit_bytes=VMEM_LIMIT),
        cost_estimate=SMALL,
    )(image, taps, bias.reshape(1, -1), gain, shift.reshape(1, -1), order)


def slope_kernel(start_ref, normed_ref, w_ref, b_ref, cot_ref, grad_ref, sums_ref):
    pre_act = jnp.dot(normed_ref[...], w_ref[...], preferred_element_type=jnp.float32) + b_ref[...]
    slope = 0.5 * (1.0 + lax.erf(pre_act * 0.7071067811865476)) + pre_act * jnp.exp(
        -0.5 * pre_act * pre_act
    ) * 0.3989422804014327
    pre_grad = (cot_ref[0].astype(jnp.float32) * slope).astype(jnp.bfloat16)
    grad_ref[...] = pre_grad
    sums_ref[...] = jnp.sum(pre_grad.astype(jnp.float32), axis=0, keepdims=True)


def gelu_grad(start, steps, normed, w_up, b_up, cot, width):
    cells, feat = normed.shape
    hid = steps * width
    return pl.pallas_call(
        slope_kernel,
        name="gelu_grad",
        grid_spec=pltpu.PrefetchScalarGridSpec(
            num_scalar_prefetch=1,
            grid=(steps,),
            in_specs=[
                pl.BlockSpec((cells, feat), lambda i, s: (0, 0)),
                pl.BlockSpec((feat, width), lambda i, s: (0, s[0] + i)),
                pl.BlockSpec((1, width), lambda i, s: (0, s[0] + i)),
                pl.BlockSpec((1, cells, width), lambda i, s: (0, 0, s[0] + i)),
            ],
            out_specs=[
                pl.BlockSpec((cells, width), lambda i, s: (0, i)),
                pl.BlockSpec((1, width), lambda i, s: (0, i)),
            ],
        ),
        out_shape=(
            jax.ShapeDtypeStruct((cells, hid), jnp.bfloat16),
            jax.ShapeDtypeStruct((1, hid), jnp.float32),
        ),
        compiler_params=pltpu.CompilerParams(vmem_limit_bytes=VMEM_LIMIT),
        cost_estimate=SMALL,
    )(start, normed, w_up, b_up, cot)


def norm_grad_kernel(
    start_ref, first_ref, second_ref, away_ref, w_ref, unit_ref, sigma_ref, gain_ref,
    conv_ref, gain_sum_ref, shift_sum_ref, total,
):
    step = pl.program_id(0)
    quarter = pl.num_programs(0) // 4

    @pl.when(step == 0)
    def _():
        total[...] = jnp.zeros_like(total)

    def add(grad_ref):
        total[...] += lax.dot_general(
            grad_ref[...], w_ref[...], (((1,), (1,)), ((), ())), preferred_element_type=jnp.float32
        )

    @pl.when(step < quarter)
    def _():
        add(first_ref)

    @pl.when((step >= quarter) & (step < 2 * quarter))
    def _():
        add(second_ref)

    @pl.when(step >= 2 * quarter)
    def _():
        add(away_ref)

    @pl.when(step == pl.num_programs(0) - 1)
    def _():
        feat = total.shape[1]
        gain_sum_ref[...] = jnp.zeros_like(gain_sum_ref)
        shift_sum_ref[...] = jnp.zeros_like(shift_sum_ref)

        @pl.loop(0, total.shape[0] // 16)
        def _(row):
            cells = pl.ds(pl.multiple_of(row * 16, 16), 16)
            grad = total[cells, :]
            unit = unit_ref[cells, :]
            gain_sum_ref[...] += jnp.sum(grad * unit, axis=0, keepdims=True)
            shift_sum_ref[...] += jnp.sum(grad, axis=0, keepdims=True)
            unit_grad = grad * gain_ref[...]
            first = jnp.sum(unit_grad, axis=-1, keepdims=True) * (1.0 / feat)
            second = jnp.sum(unit_grad * unit, axis=-1, keepdims=True) * (1.0 / feat)
            conv_ref[cells, :] = sigma_ref[cells, 0:1] * (unit_grad - first - unit * second)


def norm_grad(start, first, second, away, w_up, unit, sigma, gain, width):
    cells, feat = unit.shape
    hid = w_up.shape[1]
    steps = hid // width
    quarter = steps // 4
    return pl.pallas_call(
        norm_grad_kernel,
        name="norm_grad",
        grid_spec=pltpu.PrefetchScalarGridSpec(
            num_scalar_prefetch=1,
            grid=(steps,),
            in_specs=[
                pl.BlockSpec((cells, width), lambda i, s: (0, jnp.minimum(i, quarter - 1))),
                pl.BlockSpec((cells, width), lambda i, s: (0, jnp.clip(i - quarter, 0, quarter - 1))),
                pl.BlockSpec((cells, width), lambda i, s: (0, jnp.maximum(i - 2 * quarter, 0))),
                pl.BlockSpec((feat, width), lambda i, s: (0, lax.rem(s[0] + i, steps))),
                pl.BlockSpec((cells, feat), lambda i, s: (0, 0)),
                pl.BlockSpec((cells, LANES), lambda i, s: (0, 0)),
                pl.BlockSpec((1, feat), lambda i, s: (0, 0)),
            ],
            out_specs=[
                pl.BlockSpec((cells, feat), lambda i, s: (0, 0)),
                pl.BlockSpec((1, feat), lambda i, s: (0, 0)),
                pl.BlockSpec((1, feat), lambda i, s: (0, 0)),
            ],
            scratch_shapes=[pltpu.VMEM((cells, feat), jnp.float32)],
        ),
        out_shape=(
            jax.ShapeDtypeStruct((cells, feat), jnp.float32),
            jax.ShapeDtypeStruct((1, feat), jnp.float32),
            jax.ShapeDtypeStruct((1, feat), jnp.float32),
        ),
        compiler_params=pltpu.CompilerParams(vmem_limit_bytes=VMEM_LIMIT),
        cost_estimate=SMALL,
    )(start, first, second, away, w_up, unit, sigma, gain)


def conv_grad_kernel(grad_ref, image_ref, res_ref, taps_ref, out_ref, tap_sum_ref, bias_sum_ref, padded, image):
    side = image_ref.shape[1]
    blank = jnp.zeros((side, EDGE, LANES), jnp.float32)
    padded[:, 0:EDGE, :] = blank
    padded[:, EDGE + side : EDGE + side + EDGE, :] = blank
    image[...] = image_ref[0].astype(jnp.float32)
    bias_sum = jnp.zeros((side, LANES), jnp.float32)
    for row in range(side):
        cells = grad_ref[row * side : (row + 1) * side, :]
        padded[row, EDGE : EDGE + side, :] = cells
        bias_sum = bias_sum + cells
    bias_sum_ref[...] = jnp.sum(bias_sum, axis=0, keepdims=True)
    sums = [res_ref[0, row].astype(jnp.float32) for row in range(side)]
    for turn_col in range(7):
        weights = [
            jnp.broadcast_to(
                taps_ref[pl.ds(7 * (6 - turn_row) + 6 - turn_col, 1), :], (side, LANES)
            )
            for turn_row in range(7)
        ]
        parts = [jnp.zeros((8, LANES), jnp.float32) for _ in range(7)]
        for source in range(side):
            cells = padded[source, EDGE - 3 + turn_col : EDGE - 3 + turn_col + side, :]
            for turn_row in range(7):
                target = source + 3 - turn_row
                if 0 <= target < side:
                    sums[target] = sums[target] + cells * weights[turn_row]
                    product = cells * image[target]
                    parts[turn_row] = parts[turn_row] + (product[:8] + product[8:])
        for turn_row in range(7):
            tap = 7 * (6 - turn_row) + 6 - turn_col
            tap_sum_ref[tap : tap + 1, :] = jnp.sum(parts[turn_row], axis=0, keepdims=True)
    for row in range(side):
        out_ref[0, row] = sums[row].astype(jnp.bfloat16)


def conv_backward(grad, image, residual, taps):
    side, feat = image.shape[1], image.shape[3]
    cells = side * side
    picture = pl.BlockSpec((1, side, side, LANES), lambda i: (0, 0, 0, i))
    return pl.pallas_call(
        conv_grad_kernel,
        name="conv_backward",
        grid=(feat // LANES,),
        in_specs=[
            pl.BlockSpec((cells, LANES), lambda i: (0, i)),
            picture,
            picture,
            pl.BlockSpec((49, LANES), lambda i: (0, i)),
        ],
        out_specs=[
            picture,
            pl.BlockSpec((49, LANES), lambda i: (0, i)),
            pl.BlockSpec((1, LANES), lambda i: (0, i)),
        ],
        out_shape=(
            jax.ShapeDtypeStruct(image.shape, jnp.bfloat16),
            jax.ShapeDtypeStruct((49, feat), jnp.float32),
            jax.ShapeDtypeStruct((1, feat), jnp.float32),
        ),
        scratch_shapes=[
            pltpu.VMEM((side, side + 2 * EDGE, LANES), jnp.float32),
            pltpu.VMEM((side, side, LANES), jnp.float32),
        ],
        compiler_params=pltpu.CompilerParams(vmem_limit_bytes=VMEM_LIMIT),
        cost_estimate=SMALL,
    )(grad, image, residual, taps)


def product_kernel(x_first, place_ref, near_t_ref, far_t_ref, near_ref, far_ref, *out_refs):
    rows = near_t_ref.shape[2]
    cells = near_t_ref.shape[3]
    block = (
        jnp.dot(near_t_ref[...].reshape(4 * rows, cells), near_ref[...], preferred_element_type=jnp.float32)
        + jnp.dot(far_t_ref[...].reshape(4 * rows, cells), far_ref[...], preferred_element_type=jnp.float32)
    ).astype(jnp.bfloat16)
    inner = place_ref[1] if x_first else place_ref[0]
    for away in range(4):

        @pl.when(pl.program_id(0) == away)
        def _():
            for index in range(4):
                out_refs[away][lax.rem(index - inner + 4, 4)] = block[index * rows : (index + 1) * rows]


def product(place, near_t, far_t, near, far, part, columns, x_first):
    _, _, rows, cells = near_t.shape
    if x_first:
        left = pl.BlockSpec((1, 4, rows, cells), lambda i, p: (lax.rem(p[0] + i, 4), 0, 0, 0))
    else:
        left = pl.BlockSpec((4, 1, rows, cells), lambda i, p: (0, lax.rem(p[1] + i, 4), 0, 0))
    return pl.pallas_call(
        functools.partial(product_kernel, x_first),
        name="product",
        grid_spec=pltpu.PrefetchScalarGridSpec(
            num_scalar_prefetch=1,
            grid=(4,),
            in_specs=[
                left,
                left,
                pl.BlockSpec((cells, columns), lambda i, p: (0, 0)),
                pl.BlockSpec((cells, columns), lambda i, p: (0, part)),
            ],
            out_specs=[pl.BlockSpec((4, rows, columns), lambda i, p: (0, 0, 0))] * 4,
        ),
        out_shape=[jax.ShapeDtypeStruct((4, rows, columns), jnp.bfloat16)] * 4,
        compiler_params=pltpu.CompilerParams(vmem_limit_bytes=VMEM_LIMIT),
        cost_estimate=SMALL,
    )(place, near_t, far_t, near, far)


def sum_kernel(*refs):
    for index in range(4):
        total = refs[0][index].astype(jnp.float32)
        for ref in refs[1:4]:
            total = total + ref[index].astype(jnp.float32)
        refs[4 + index][...] = total.astype(jnp.bfloat16)


def sum_pieces(pieces):
    _, rows, columns = pieces[0].shape
    return pl.pallas_call(
        sum_kernel,
        name="sum_pieces",
        out_shape=[jax.ShapeDtypeStruct((rows, columns), jnp.bfloat16)] * 4,
        compiler_params=pltpu.CompilerParams(vmem_limit_bytes=VMEM_LIMIT),
        cost_estimate=SMALL,
    )(*pieces)


def to_owners(pieces, axes):
    named = range(4) if axes == "x" else [0, 2, 1, 3]
    moved = [
        lax.ppermute(piece, axes, [(named[i], named[(i + d) % 4]) for i in range(4)])
        for d, piece in enumerate(pieces)
        if d
    ]
    return [pieces[0]] + moved


def swap_pieces(values, axes):
    return lax.all_to_all(values, axes, 0, 0, tiled=True)


def total_of(received):
    return jnp.sum(received.astype(jnp.float32), axis=0)


def per_device(images, hidden_cot, residual_cot, w_up, b_up, ln_gain, ln_bias, dw_weight, dw_bias):
    feat, hid = w_up.shape
    y_axes = ("y_lo", "y_hi")
    plane = ("x", "y_hi", "y_lo")
    along_z = lax.axis_size("z")
    devices = 32 * along_z
    inverse_count = 1.0 / (images.shape[0] * devices)
    core = lax.axis_index("core")
    mine = core.astype(jnp.int32).reshape(1)
    swap = [(0, 1), (1, 0)]
    width = hid // 8

    b_row, gain_row = b_up.reshape(1, -1), ln_gain.reshape(1, -1)
    unit, sigma, normed, turned = conv_norm(images, dw_weight, dw_bias, gain_row, ln_bias, along_z)
    cells = normed.shape[0]
    far_turned = lax.ppermute(turned, "core", swap)
    away, away_sums = gelu_grad(4 - 4 * mine, 4, normed, w_up, b_row, hidden_cot, width)
    far = lax.ppermute(away, "core", swap)
    y_index = 2 * lax.axis_index("y_hi") + lax.axis_index("y_lo")
    place = jnp.stack([lax.axis_index("x"), y_index]).astype(jnp.int32)
    near_t, far_t = turned.reshape(4, 4, -1, cells), far_turned.reshape(4, 4, -1, cells)
    near_a, sums_a = gelu_grad(4 * mine, 2, normed, w_up, b_row, hidden_cot, width)
    part_a = to_owners(product(place, near_t, far_t, near_a, far, 0, 2 * width, True), "x")
    near_b, sums_b = gelu_grad(4 * mine + 2, 2, normed, w_up, b_row, hidden_cot, width)
    part_b = product(place, near_t, far_t, near_b, far, 1, 2 * width, False)
    part_b, unit = lax.optimization_barrier((part_b, unit))
    part_b = to_owners(part_b, y_axes)

    conv_grad, gain_sum, shift_sum = norm_grad(
        4 * mine, near_a, near_b, away, w_up, unit, sigma, gain_row, width
    )
    grad_input, tap_sums, bias_sum = conv_backward(conv_grad, images, residual_cot, dw_weight)
    near_sums = jnp.concatenate([sums_a, sums_b], axis=1)
    used = 49 + 3 + hid // feat
    rows = 2 * (-(-used // 4) * 2)
    small = jnp.concatenate(
        [
            tap_sums,
            gain_sum,
            shift_sum,
            bias_sum,
            jnp.where(core == 0, near_sums, away_sums).reshape(-1, feat),
            jnp.where(core == 0, away_sums, near_sums).reshape(-1, feat),
            jnp.zeros((rows - used, feat), jnp.float32),
        ],
        axis=0,
    ).reshape(2, 16, 1, -1)
    part_a, part_b, small = lax.optimization_barrier((part_a, part_b, small))

    part_a = to_owners(sum_pieces(part_a), y_axes)
    part_b = to_owners(sum_pieces(part_b), "x")

    kept = jnp.where(core == 0, small[0], small[1])
    small = kept + lax.ppermute(jnp.where(core == 0, small[1], small[0]), "core", swap)
    small = jnp.sum(swap_pieces(small, plane), axis=0, keepdims=True)
    small = jnp.broadcast_to(small, (along_z,) + small.shape[1:])
    small = jnp.sum(swap_pieces(small, "z"), axis=0, keepdims=True) * inverse_count
    small = swap_pieces(jnp.broadcast_to(small, (16,) + small.shape[1:]), plane)
    other = lax.ppermute(small, "core", swap)
    small = jnp.stack([jnp.where(core == 0, small, other), jnp.where(core == 0, other, small)])
    small = small.reshape(rows, feat)

    last = jnp.concatenate([total_of(jnp.stack(part_a)), total_of(jnp.stack(part_b))], axis=1).astype(jnp.bfloat16)
    last = swap_pieces(last.reshape(2 * along_z, -1, LANES), ("z", "core"))
    last = total_of(last.reshape(along_z, 2, feat // devices, hid // 2))
    owned = last.transpose(1, 0, 2).reshape(feat // devices, hid) * inverse_count
    return (
        grad_input,
        owned,
        small[52:used].reshape(hid),
        small[49],
        small[50],
        small[:49],
        small[51],
    )


def solution(mesh):
    x, z = 4, mesh.devices.size // 32
    split = Mesh(mesh.devices.reshape(2, x, z, 2, 2), ("y_lo", "x", "z", "y_hi", "core"))
    images = P(("y_lo", "x", "z", "y_hi", "core"))
    return jax.shard_map(
        per_device,
        mesh=split,
        in_specs=(images, images, images, P(), P(), P(), P(), P(), P()),
        out_specs=(images, images, P(), P(), P(), P(), P()),
        check_vma=False,
    )
```

```python
import jax
import jax.numpy as jnp
import numpy as np
from jax import lax
from jax.experimental import pallas as pl
from jax.experimental.pallas import tpu as pltpu
from jax.sharding import Mesh
from jax.sharding import PartitionSpec as P

LANES = 128
EDGE = 8
VMEM_LIMIT = 60 * 1024 * 1024
SMALL = pl.CostEstimate(flops=1000, bytes_accessed=1000, transcendentals=0)
SMALL_ROWS = 64


def front_kernel(
    core_ref, image_ref, taps_ref, bias_ref, gain_ref, shift_ref, order_ref, b_ref, w_hbm, cot_hbm,
    unit_out, sigma_ref, turned_ref, away_out, near_out, sums_ref,
    padded, conv, unit, normed, weights, cots, grads, in_sems, out_sems,
):
    side, feat = image_ref.shape[1], image_ref.shape[3]
    parts, _, width = weights.shape
    half = parts // 2
    core = core_ref[0]

    def column(part):
        owner = 1 - core if part < half else core
        return pl.multiple_of((owner * half + part % half) * width, width)

    loads = []
    for part in range(parts):
        columns = pl.ds(column(part), width)
        loads.append(
            (
                pltpu.make_async_copy(w_hbm.at[:, columns], weights.at[part], in_sems.at[2 * part]),
                pltpu.make_async_copy(cot_hbm.at[0, :, columns], cots.at[part], in_sems.at[2 * part + 1]),
            )
        )
    for pair in loads:
        pair[0].start()
        pair[1].start()

    blank = jnp.zeros((side, EDGE, LANES), jnp.float32)
    padded[:, 0:EDGE, :] = blank
    padded[:, EDGE + side : EDGE + side + EDGE, :] = blank

    @pl.loop(0, feat // LANES)
    def _(block):
        lanes = pl.ds(pl.multiple_of(block * LANES, LANES), LANES)
        padded[:, EDGE : EDGE + side, :] = image_ref[0, :, :, lanes].astype(jnp.float32)
        start = jnp.broadcast_to(bias_ref[lanes].reshape(1, LANES), (side, LANES))
        sums = [start] * side
        for tap_col in range(7):
            taps = [
                jnp.broadcast_to(taps_ref[pl.ds(7 * tap_row + tap_col, 1), lanes], (side, LANES))
                for tap_row in range(7)
            ]
            for source in range(side):
                cells = padded[source, EDGE - 3 + tap_col : EDGE - 3 + tap_col + side, :]
                for tap_row in range(7):
                    target = source + 3 - tap_row
                    if 0 <= target < side:
                        sums[target] = sums[target] + cells * taps[tap_row]
        for row in range(side):
            conv[row * side : (row + 1) * side, lanes] = sums[row]

    gain = gain_ref[...].reshape(1, feat)
    shift = shift_ref[...].reshape(1, feat)

    @pl.loop(0, side)
    def _(row):
        cells = pl.ds(pl.multiple_of(row * side, side), side)
        values = conv[cells, :]
        centred = values - jnp.mean(values, axis=-1, keepdims=True)
        inv_sigma = lax.rsqrt(jnp.mean(centred * centred, axis=-1, keepdims=True) + 1e-06)
        scaled = centred * inv_sigma
        unit[cells, :] = scaled
        sigma_ref[cells, :] = jnp.broadcast_to(inv_sigma, (side, LANES))
        normed[cells, :] = (scaled * gain + shift).astype(jnp.bfloat16)

    unit_copy = pltpu.make_async_copy(unit, unit_out, out_sems.at[0])
    unit_copy.start()

    group = order_ref.shape[0]
    rows = turned_ref.shape[3]
    for index in range(feat // group):
        y_lo, pair = divmod(index, 2)
        turned = lax.dot_general(
            order_ref[...],
            normed[:, index * group : (index + 1) * group],
            (((1,), (1,)), ((), ())),
            preferred_element_type=jnp.float32,
        ).astype(jnp.bfloat16)
        for within in range(2):
            for y_hi in range(2):
                first = (within * 2 + y_hi) * rows
                turned_ref[2 * pair + within, y_hi, y_lo] = turned[first : first + rows]

    stores = [unit_copy]
    for part in range(parts):
        loads[part][0].wait()
        loads[part][1].wait()
        columns = pl.ds(column(part), width)
        pre_act = jnp.dot(normed[...], weights[part], preferred_element_type=jnp.float32)
        pre_act = pre_act + b_ref[:, columns]
        slope = 0.5 * (1.0 + lax.erf(pre_act * 0.7071067811865476)) + pre_act * jnp.exp(
            -0.5 * pre_act * pre_act
        ) * 0.3989422804014327
        grad = (cots[part].astype(jnp.float32) * slope).astype(jnp.bfloat16)
        grads[part] = grad
        sums_ref[:, columns] = jnp.sum(grad.astype(jnp.float32), axis=0, keepdims=True)
        target = away_out if part < half else near_out
        copy = pltpu.make_async_copy(
            grads.at[part], target.at[:, (part % half) * width : (part % half + 1) * width], out_sems.at[1 + part]
        )
        copy.start()
        stores.append(copy)
    for copy in stores:
        copy.wait()


def channel_order(rows, along_z):
    width = 4 * rows
    owned = rows // along_z
    target = np.arange(width).reshape(2, along_z, 2, owned).transpose(0, 2, 1, 3).reshape(-1)
    return jnp.asarray(np.eye(width, dtype=np.float32)[target], jnp.bfloat16)


def front(core, image, taps, bias, gain, shift, w_up, b_row, cot, along_z, parts=4):
    side, feat = image.shape[1], image.shape[3]
    cells = side * side
    hid = w_up.shape[1]
    rows = feat // 16
    width = hid // parts
    whole = pl.BlockSpec(memory_space=pltpu.VMEM)
    remain = pl.BlockSpec(memory_space=pl.ANY)
    return pl.pallas_call(
        front_kernel,
        name="front",
        in_specs=[pl.BlockSpec(memory_space=pltpu.SMEM)] + [whole] * 7 + [remain] * 2,
        out_specs=[remain, whole, whole, remain, remain, whole],
        out_shape=(
            jax.ShapeDtypeStruct((cells, feat), jnp.float32),
            jax.ShapeDtypeStruct((cells, LANES), jnp.float32),
            jax.ShapeDtypeStruct((4, 2, 2, rows, cells), jnp.bfloat16),
            jax.ShapeDtypeStruct((cells, hid // 2), jnp.bfloat16),
            jax.ShapeDtypeStruct((cells, hid // 2), jnp.bfloat16),
            jax.ShapeDtypeStruct((1, hid), jnp.float32),
        ),
        scratch_shapes=[
            pltpu.VMEM((side, side + 2 * EDGE, LANES), jnp.float32),
            pltpu.VMEM((cells, feat), jnp.float32),
            pltpu.VMEM((cells, feat), jnp.float32),
            pltpu.VMEM((cells, feat), jnp.bfloat16),
            pltpu.VMEM((parts, feat, width), jnp.bfloat16),
            pltpu.VMEM((parts, cells, width), jnp.bfloat16),
            pltpu.VMEM((parts, cells, width), jnp.bfloat16),
            pltpu.SemaphoreType.DMA((2 * parts,)),
            pltpu.SemaphoreType.DMA((1 + parts,)),
        ],
        compiler_params=pltpu.CompilerParams(vmem_limit_bytes=VMEM_LIMIT),
        cost_estimate=SMALL,
    )(core, image, taps, bias, gain, shift, channel_order(rows, along_z), b_row, w_up, cot)


def finish_rows(total, unit_ref, sigma_ref, gain_ref, conv_ref, gain_sum_ref, shift_sum_ref):
    feat = total.shape[1]
    gain = gain_ref[...].reshape(1, feat)

    def body(row, carry):
        gain_sum, shift_sum = carry
        cells = pl.ds(pl.multiple_of(row * 8, 8), 8)
        grad = total[cells, :]
        unit = unit_ref[cells, :]
        gain_sum = gain_sum + grad * unit
        shift_sum = shift_sum + grad
        unit_grad = grad * gain
        first = jnp.sum(unit_grad, axis=-1, keepdims=True) * (1.0 / feat)
        second = jnp.sum(unit_grad * unit, axis=-1, keepdims=True) * (1.0 / feat)
        conv_ref[cells, :] = sigma_ref[cells, 0:1] * (unit_grad - first - unit * second)
        return gain_sum, shift_sum

    zero = jnp.zeros((8, feat), jnp.float32)
    gain_sum, shift_sum = lax.fori_loop(0, total.shape[0] // 8, body, (zero, zero))
    gain_sum_ref[...] = jnp.sum(gain_sum, axis=0, keepdims=True)
    shift_sum_ref[...] = jnp.sum(shift_sum, axis=0, keepdims=True)


def norm_grad_kernel(
    core_ref, away_ref, near_ref, unit_ref, sigma_ref, gain_ref, w_hbm,
    conv_ref, gain_sum_ref, shift_sum_ref, weights, total, sems,
):
    parts, feat, width = weights.shape
    half = parts // 2
    core = core_ref[0]
    loads = []
    for part in range(parts):
        owner = 1 - core if part < half else core
        columns = pl.ds(pl.multiple_of((owner * half + part % half) * width, width), width)
        loads.append(pltpu.make_async_copy(w_hbm.at[:, columns], weights.at[part], sems.at[part]))
        loads[-1].start()
    for part in range(parts):
        loads[part].wait()
        grad_ref = away_ref if part < half else near_ref
        grad = grad_ref[:, (part % half) * width : (part % half + 1) * width]
        value = lax.dot_general(grad, weights[part], (((1,), (1,)), ((), ())), preferred_element_type=jnp.float32)
        if part:
            total[...] += value
        else:
            total[...] = value
    finish_rows(total, unit_ref, sigma_ref, gain_ref, conv_ref, gain_sum_ref, shift_sum_ref)


def norm_grad(core, away, near, w_up, unit, sigma, gain, parts=4):
    cells, feat = unit.shape
    width = w_up.shape[1] // parts
    whole = pl.BlockSpec(memory_space=pltpu.VMEM)
    return pl.pallas_call(
        norm_grad_kernel,
        name="norm_grad",
        in_specs=[pl.BlockSpec(memory_space=pltpu.SMEM)] + [whole] * 5 + [pl.BlockSpec(memory_space=pl.ANY)],
        out_specs=[whole] * 3,
        out_shape=(
            jax.ShapeDtypeStruct((cells, feat), jnp.float32),
            jax.ShapeDtypeStruct((1, feat), jnp.float32),
            jax.ShapeDtypeStruct((1, feat), jnp.float32),
        ),
        scratch_shapes=[
            pltpu.VMEM((parts, feat, width), jnp.bfloat16),
            pltpu.VMEM((cells, feat), jnp.float32),
            pltpu.SemaphoreType.DMA((parts,)),
        ],
        compiler_params=pltpu.CompilerParams(vmem_limit_bytes=VMEM_LIMIT),
        cost_estimate=SMALL,
    )(core, away, near, unit, sigma, gain, w_up)


def product_kernel(near_t_ref, far_t_ref, near_ref, far_ref, *out_refs):
    block = (
        jnp.dot(near_t_ref[0], near_ref[...], preferred_element_type=jnp.float32)
        + jnp.dot(far_t_ref[0], far_ref[...], preferred_element_type=jnp.float32)
    ).astype(jnp.bfloat16)
    first = 0
    for out_ref in out_refs:
        columns = out_ref.shape[-1]
        out_ref[...] = block[:, first : first + columns].reshape(out_ref.shape)
        first += columns


def product(near_t, far_t, near, far, splits):
    blocks, rows, cells = near_t.shape
    left = pl.BlockSpec((1, rows, cells), lambda i: (i, 0, 0))
    right = pl.BlockSpec((cells, near.shape[1]), lambda i: (0, 0))
    return pl.pallas_call(
        product_kernel,
        name="product",
        grid=(blocks,),
        in_specs=[left, left, right, right],
        out_specs=[pl.BlockSpec((1, rows, n), lambda i: (i, 0, 0)) for n in splits],
        out_shape=[jax.ShapeDtypeStruct((blocks, rows, n), jnp.bfloat16) for n in splits],
        compiler_params=pltpu.CompilerParams(vmem_limit_bytes=VMEM_LIMIT),
        cost_estimate=SMALL,
    )(near_t, far_t, near, far)


def conv_grad_kernel(
    grad_ref, image_ref, res_ref, taps_ref, gain_sum_ref, shift_sum_ref, up_first_ref, up_second_ref,
    out_ref, sums_ref, padded, image,
):
    side = image_ref.shape[1]
    blank = jnp.zeros((side, EDGE, LANES), jnp.float32)
    padded[:, 0:EDGE, :] = blank
    padded[:, EDGE + side : EDGE + side + EDGE, :] = blank
    image[...] = image_ref[0].astype(jnp.float32)
    bias_sum = jnp.zeros((side, LANES), jnp.float32)
    for row in range(side):
        cells = grad_ref[row * side : (row + 1) * side, :]
        padded[row, EDGE : EDGE + side, :] = cells
        bias_sum = bias_sum + cells
    sums_ref[49:50, :] = gain_sum_ref[...]
    sums_ref[50:51, :] = shift_sum_ref[...]
    sums_ref[51:52, :] = jnp.sum(bias_sum, axis=0, keepdims=True)
    sums_ref[52:53, :] = up_first_ref[...]
    sums_ref[53:54, :] = up_second_ref[...]
    sums_ref[54:, :] = jnp.zeros((SMALL_ROWS - 54, LANES), jnp.float32)
    sums = [res_ref[0, row].astype(jnp.float32) for row in range(side)]
    for turn_col in range(7):
        weights = [
            jnp.broadcast_to(
                taps_ref[pl.ds(7 * (6 - turn_row) + 6 - turn_col, 1), :], (side, LANES)
            )
            for turn_row in range(7)
        ]
        parts = [jnp.zeros((8, LANES), jnp.float32) for _ in range(7)]
        for source in range(side):
            cells = padded[source, EDGE - 3 + turn_col : EDGE - 3 + turn_col + side, :]
            for turn_row in range(7):
                target = source + 3 - turn_row
                if 0 <= target < side:
                    sums[target] = sums[target] + cells * weights[turn_row]
                    product = cells * image[target]
                    parts[turn_row] = parts[turn_row] + (product[:8] + product[8:])
        for turn_row in range(7):
            tap = 7 * (6 - turn_row) + 6 - turn_col
            sums_ref[tap : tap + 1, :] = jnp.sum(parts[turn_row], axis=0, keepdims=True)
    for row in range(side):
        out_ref[0, row] = sums[row].astype(jnp.bfloat16)


def conv_backward(grad, image, residual, taps, gain_sum, shift_sum, up_sums):
    side, feat = image.shape[1], image.shape[3]
    cells = side * side
    picture = pl.BlockSpec((1, side, side, LANES), lambda i: (0, 0, 0, i))
    return pl.pallas_call(
        conv_grad_kernel,
        name="conv_backward",
        grid=(feat // LANES,),
        in_specs=[
            pl.BlockSpec((cells, LANES), lambda i: (0, i)),
            picture,
            picture,
            pl.BlockSpec((49, LANES), lambda i: (0, i)),
            pl.BlockSpec((1, LANES), lambda i: (0, i)),
            pl.BlockSpec((1, LANES), lambda i: (0, i)),
            pl.BlockSpec((1, LANES), lambda i: (0, i)),
            pl.BlockSpec((1, LANES), lambda i: (0, i + feat // LANES)),
        ],
        out_specs=[
            picture,
            pl.BlockSpec((SMALL_ROWS, LANES), lambda i: (0, i)),
        ],
        out_shape=(
            jax.ShapeDtypeStruct(image.shape, jnp.bfloat16),
            jax.ShapeDtypeStruct((SMALL_ROWS, feat), jnp.float32),
        ),
        scratch_shapes=[
            pltpu.VMEM((side, side + 2 * EDGE, LANES), jnp.float32),
            pltpu.VMEM((side, side, LANES), jnp.float32),
        ],
        compiler_params=pltpu.CompilerParams(vmem_limit_bytes=VMEM_LIMIT),
        cost_estimate=SMALL,
    )(grad, image, residual, taps, gain_sum, shift_sum, up_sums, up_sums)


def swap_pieces(values, axes):
    return lax.all_to_all(values, axes, 0, 0, tiled=True)


def total_of(received):
    return jnp.sum(received.astype(jnp.float32), axis=0)


def per_device(images, hidden_cot, residual_cot, w_up, b_up, ln_gain, ln_bias, dw_weight, dw_bias):
    feat, hid = w_up.shape
    plane = ("x", "y_hi", "y_lo")
    others = ("y_lo", "x", "z", "y_hi")
    along_z = lax.axis_size("z")
    chips = 16 * along_z
    owned_rows = feat // (2 * chips)
    inverse_count = 1.0 / (images.shape[0] * 2 * chips)
    core = lax.axis_index("core")
    mine = core.astype(jnp.int32).reshape(1)
    swap = [(0, 1), (1, 0)]

    unit, sigma, turned, away, near, up_sums = front(
        mine, images, dw_weight, dw_bias, ln_gain, ln_bias, w_up, b_up.reshape(1, -1), hidden_cot, along_z
    )
    far = lax.ppermute(away, "core", swap)
    far_turned = lax.ppermute(turned, "core", swap)
    cells = unit.shape[0]
    ringed = hid // 4
    part_a, part_b = product(
        turned.reshape(4, -1, cells), far_turned.reshape(4, -1, cells), near, far, (ringed, hid // 2 - ringed)
    )
    part_b, unit = lax.optimization_barrier((part_b, unit))
    part_a = lax.psum_scatter(part_a.reshape(feat, -1), "x", scatter_dimension=0, tiled=True)
    part_b = swap_pieces(part_b.reshape(16, feat // 16, -1), plane)

    conv_grad, gain_sum, shift_sum = norm_grad(mine, away, near, w_up, unit, sigma, ln_gain)
    grad_input, small = conv_backward(
        conv_grad, images, residual_cot, dw_weight, gain_sum, shift_sum, up_sums
    )
    part_a, part_b, small = lax.optimization_barrier((part_a, part_b, small))
    part_a = lax.psum_scatter(part_a, ("y_hi", "y_lo"), scatter_dimension=0, tiled=True)
    part_b = total_of(part_b).astype(jnp.bfloat16)

    small = small.reshape(2, chips, 1, -1)
    kept = jnp.where(core == 0, small[0], small[1])
    small = kept + lax.ppermute(jnp.where(core == 0, small[1], small[0]), "core", swap)
    small = jnp.sum(swap_pieces(small, others), axis=0, keepdims=True) * inverse_count
    small = swap_pieces(jnp.broadcast_to(small, (chips,) + small.shape[1:]), others)
    other = lax.ppermute(small, "core", swap)
    part_a, small, other = lax.optimization_barrier((part_a, small, other))

    last = jnp.concatenate([part_a, part_b], axis=1)
    last = swap_pieces(last.reshape(2 * along_z, -1, LANES), ("z", "core"))
    last = total_of(last.reshape(along_z, 2, owned_rows, hid // 2))
    owned = last.transpose(1, 0, 2).reshape(owned_rows, hid) * inverse_count
    small = jnp.stack([jnp.where(core == 0, small, other), jnp.where(core == 0, other, small)])
    small = small.reshape(SMALL_ROWS, feat)
    return (
        grad_input,
        owned,
        small[52:54].reshape(hid),
        small[49],
        small[50],
        small[:49],
        small[51],
    )


def solution(mesh):
    x, z = 4, mesh.devices.size // 32
    split = Mesh(mesh.devices.reshape(2, x, z, 2, 2), ("y_lo", "x", "z", "y_hi", "core"))
    images = P(("y_lo", "x", "z", "y_hi", "core"))
    return jax.shard_map(
        per_device,
        mesh=split,
        in_specs=(images, images, images, P(), P(), P(), P(), P(), P()),
        out_specs=(images, images, P(), P(), P(), P(), P()),
        check_vma=False,
    )
```

```python
import jax
import jax.numpy as jnp
import numpy as np
from jax import lax
from jax.experimental import pallas as pl
from jax.experimental.pallas import tpu as pltpu
from jax.sharding import Mesh
from jax.sharding import PartitionSpec as P

LANES = 128
EDGE = 8
VMEM_LIMIT = 60 * 1024 * 1024
SMALL = pl.CostEstimate(flops=1000, bytes_accessed=1000, transcendentals=0)
SMALL_ROWS = 56


def front_kernel(
    core_ref, image_ref, taps_ref, bias_ref, gain_ref, shift_ref, order_ref, b_ref, w_hbm, cot_hbm,
    unit_out, sigma_ref, turned_ref, away_out, near_out, sums_ref,
    padded, conv, unit, normed, weights, cots, grads, in_sems, out_sems,
):
    side, feat = image_ref.shape[1], image_ref.shape[3]
    parts, _, width = weights.shape
    half = parts // 2
    core = core_ref[0]

    def column(part):
        owner = 1 - core if part < half else core
        return pl.multiple_of((owner * half + part % half) * width, width)

    loads = []
    for part in range(parts):
        columns = pl.ds(column(part), width)
        loads.append(
            (
                pltpu.make_async_copy(w_hbm.at[:, columns], weights.at[part], in_sems.at[2 * part]),
                pltpu.make_async_copy(cot_hbm.at[0, :, columns], cots.at[part], in_sems.at[2 * part + 1]),
            )
        )
    for pair in loads:
        pair[0].start()
        pair[1].start()

    blank = jnp.zeros((side, EDGE, LANES), jnp.float32)
    padded[:, 0:EDGE, :] = blank
    padded[:, EDGE + side : EDGE + side + EDGE, :] = blank

    @pl.loop(0, feat // LANES)
    def _(block):
        lanes = pl.ds(pl.multiple_of(block * LANES, LANES), LANES)
        padded[:, EDGE : EDGE + side, :] = image_ref[0, :, :, lanes].astype(jnp.float32)
        start = jnp.broadcast_to(bias_ref[lanes].reshape(1, LANES), (side, LANES))
        sums = [start] * side
        for tap_col in range(7):
            taps = [
                jnp.broadcast_to(taps_ref[pl.ds(7 * tap_row + tap_col, 1), lanes], (side, LANES))
                for tap_row in range(7)
            ]
            for source in range(side):
                cells = padded[source, EDGE - 3 + tap_col : EDGE - 3 + tap_col + side, :]
                for tap_row in range(7):
                    target = source + 3 - tap_row
                    if 0 <= target < side:
                        sums[target] = sums[target] + cells * taps[tap_row]
        for row in range(side):
            conv[row * side : (row + 1) * side, lanes] = sums[row]

    gain = gain_ref[...].reshape(1, feat)
    shift = shift_ref[...].reshape(1, feat)

    @pl.loop(0, side)
    def _(row):
        cells = pl.ds(pl.multiple_of(row * side, side), side)
        values = conv[cells, :]
        centred = values - jnp.mean(values, axis=-1, keepdims=True)
        inv_sigma = lax.rsqrt(jnp.mean(centred * centred, axis=-1, keepdims=True) + 1e-06)
        scaled = centred * inv_sigma
        unit[cells, :] = scaled
        sigma_ref[cells, :] = jnp.broadcast_to(inv_sigma, (side, LANES))
        normed[cells, :] = (scaled * gain + shift).astype(jnp.bfloat16)

    unit_copy = pltpu.make_async_copy(unit, unit_out, out_sems.at[0])
    unit_copy.start()

    group = order_ref.shape[0]
    rows = turned_ref.shape[3]
    for index in range(feat // group):
        y_lo, pair = divmod(index, 2)
        turned = lax.dot_general(
            order_ref[...],
            normed[:, index * group : (index + 1) * group],
            (((1,), (1,)), ((), ())),
            preferred_element_type=jnp.float32,
        ).astype(jnp.bfloat16)
        for within in range(2):
            for y_hi in range(2):
                first = (within * 2 + y_hi) * rows
                turned_ref[2 * pair + within, y_hi, y_lo] = turned[first : first + rows]

    stores = [unit_copy]
    for part in range(parts):
        loads[part][0].wait()
        loads[part][1].wait()
        columns = pl.ds(column(part), width)
        pre_act = jnp.dot(normed[...], weights[part], preferred_element_type=jnp.float32)
        pre_act = pre_act + b_ref[:, columns]
        slope = 0.5 * (1.0 + lax.erf(pre_act * 0.7071067811865476)) + pre_act * jnp.exp(
            -0.5 * pre_act * pre_act
        ) * 0.3989422804014327
        grad = (cots[part].astype(jnp.float32) * slope).astype(jnp.bfloat16)
        grads[part] = grad
        sums_ref[:, columns] = jnp.sum(grad.astype(jnp.float32), axis=0, keepdims=True)
        target = away_out if part < half else near_out
        copy = pltpu.make_async_copy(
            grads.at[part], target.at[:, (part % half) * width : (part % half + 1) * width], out_sems.at[1 + part]
        )
        copy.start()
        stores.append(copy)
    for copy in stores:
        copy.wait()


def channel_order(rows, along_z):
    width = 4 * rows
    owned = rows // along_z
    target = np.arange(width).reshape(2, along_z, 2, owned).transpose(0, 2, 1, 3).reshape(-1)
    return jnp.asarray(np.eye(width, dtype=np.float32)[target], jnp.bfloat16)


def front(core, image, taps, bias, gain, shift, w_up, b_row, cot, along_z, parts=4):
    side, feat = image.shape[1], image.shape[3]
    cells = side * side
    hid = w_up.shape[1]
    rows = feat // 16
    width = hid // parts
    whole = pl.BlockSpec(memory_space=pltpu.VMEM)
    remain = pl.BlockSpec(memory_space=pl.ANY)
    return pl.pallas_call(
        front_kernel,
        name="front",
        in_specs=[pl.BlockSpec(memory_space=pltpu.SMEM)] + [whole] * 7 + [remain] * 2,
        out_specs=[remain, whole, whole, remain, remain, whole],
        out_shape=(
            jax.ShapeDtypeStruct((cells, feat), jnp.float32),
            jax.ShapeDtypeStruct((cells, LANES), jnp.float32),
            jax.ShapeDtypeStruct((4, 2, 2, rows, cells), jnp.bfloat16),
            jax.ShapeDtypeStruct((cells, hid // 2), jnp.bfloat16),
            jax.ShapeDtypeStruct((cells, hid // 2), jnp.bfloat16),
            jax.ShapeDtypeStruct((1, hid), jnp.float32),
        ),
        scratch_shapes=[
            pltpu.VMEM((side, side + 2 * EDGE, LANES), jnp.float32),
            pltpu.VMEM((cells, feat), jnp.float32),
            pltpu.VMEM((cells, feat), jnp.float32),
            pltpu.VMEM((cells, feat), jnp.bfloat16),
            pltpu.VMEM((parts, feat, width), jnp.bfloat16),
            pltpu.VMEM((parts, cells, width), jnp.bfloat16),
            pltpu.VMEM((parts, cells, width), jnp.bfloat16),
            pltpu.SemaphoreType.DMA((2 * parts,)),
            pltpu.SemaphoreType.DMA((1 + parts,)),
        ],
        compiler_params=pltpu.CompilerParams(vmem_limit_bytes=VMEM_LIMIT),
        cost_estimate=SMALL,
    )(core, image, taps, bias, gain, shift, channel_order(rows, along_z), b_row, w_up, cot)


def finish_rows(total, unit_ref, sigma_ref, gain_ref, conv_ref, gain_sum_ref, shift_sum_ref):
    feat = total.shape[1]
    gain = gain_ref[...].reshape(1, feat)

    def body(row, carry):
        gain_sum, shift_sum = carry
        cells = pl.ds(pl.multiple_of(row * 8, 8), 8)
        grad = total[cells, :]
        unit = unit_ref[cells, :]
        gain_sum = gain_sum + grad * unit
        shift_sum = shift_sum + grad
        unit_grad = grad * gain
        first = jnp.sum(unit_grad, axis=-1, keepdims=True) * (1.0 / feat)
        second = jnp.sum(unit_grad * unit, axis=-1, keepdims=True) * (1.0 / feat)
        conv_ref[cells, :] = sigma_ref[cells, 0:1] * (unit_grad - first - unit * second)
        return gain_sum, shift_sum

    zero = jnp.zeros((8, feat), jnp.float32)
    gain_sum, shift_sum = lax.fori_loop(0, total.shape[0] // 8, body, (zero, zero))
    gain_sum_ref[...] = jnp.sum(gain_sum, axis=0, keepdims=True)
    shift_sum_ref[...] = jnp.sum(shift_sum, axis=0, keepdims=True)


def norm_grad_kernel(
    core_ref, away_ref, near_ref, unit_ref, sigma_ref, gain_ref, w_hbm,
    conv_ref, gain_sum_ref, shift_sum_ref, weights, total, sems,
):
    parts, feat, width = weights.shape
    half = parts // 2
    core = core_ref[0]
    loads = []
    for part in range(parts):
        owner = 1 - core if part < half else core
        columns = pl.ds(pl.multiple_of((owner * half + part % half) * width, width), width)
        loads.append(pltpu.make_async_copy(w_hbm.at[:, columns], weights.at[part], sems.at[part]))
        loads[-1].start()
    for part in range(parts):
        loads[part].wait()
        grad_ref = away_ref if part < half else near_ref
        grad = grad_ref[:, (part % half) * width : (part % half + 1) * width]
        value = lax.dot_general(grad, weights[part], (((1,), (1,)), ((), ())), preferred_element_type=jnp.float32)
        if part:
            total[...] += value
        else:
            total[...] = value
    finish_rows(total, unit_ref, sigma_ref, gain_ref, conv_ref, gain_sum_ref, shift_sum_ref)


def norm_grad(core, away, near, w_up, unit, sigma, gain, parts=4):
    cells, feat = unit.shape
    width = w_up.shape[1] // parts
    whole = pl.BlockSpec(memory_space=pltpu.VMEM)
    return pl.pallas_call(
        norm_grad_kernel,
        name="norm_grad",
        in_specs=[pl.BlockSpec(memory_space=pltpu.SMEM)] + [whole] * 5 + [pl.BlockSpec(memory_space=pl.ANY)],
        out_specs=[whole] * 3,
        out_shape=(
            jax.ShapeDtypeStruct((cells, feat), jnp.float32),
            jax.ShapeDtypeStruct((1, feat), jnp.float32),
            jax.ShapeDtypeStruct((1, feat), jnp.float32),
        ),
        scratch_shapes=[
            pltpu.VMEM((parts, feat, width), jnp.bfloat16),
            pltpu.VMEM((cells, feat), jnp.float32),
            pltpu.SemaphoreType.DMA((parts,)),
        ],
        compiler_params=pltpu.CompilerParams(vmem_limit_bytes=VMEM_LIMIT),
        cost_estimate=SMALL,
    )(core, away, near, unit, sigma, gain, w_up)


def product_kernel(place_ref, near_t_ref, far_t_ref, near_ref, far_ref, *out_refs):
    _, along_y, rows, cells = near_t_ref.shape
    block = (
        jnp.dot(near_t_ref[...].reshape(along_y * rows, cells), near_ref[...], preferred_element_type=jnp.float32)
        + jnp.dot(far_t_ref[...].reshape(along_y * rows, cells), far_ref[...], preferred_element_type=jnp.float32)
    ).astype(jnp.bfloat16)
    columns = out_refs[0].shape[2]
    out_refs[4][...] = block[:, columns:].reshape(out_refs[4].shape)
    for steps in range(4):

        @pl.when(pl.program_id(0) == steps)
        def _():
            for y in range(along_y):
                out_refs[steps][lax.rem(y - place_ref[1] + 4, 4)] = block[y * rows : (y + 1) * rows, :columns]


def product(place, near_t, far_t, near, far, columns):
    _, _, rows, cells = near_t.shape
    others = near.shape[1] - columns
    left = pl.BlockSpec((1, 4, rows, cells), lambda i, p: (lax.rem(p[0] + i, 4), 0, 0, 0))
    right = pl.BlockSpec((cells, near.shape[1]), lambda i, p: (0, 0))
    return pl.pallas_call(
        product_kernel,
        name="product",
        grid_spec=pltpu.PrefetchScalarGridSpec(
            num_scalar_prefetch=1,
            grid=(4,),
            in_specs=[left, left, right, right],
            out_specs=[pl.BlockSpec((4, rows, columns), lambda i, p: (0, 0, 0))] * 4
            + [pl.BlockSpec((4, 1, rows, others), lambda i, p: (0, lax.rem(p[0] + i, 4), 0, 0))],
        ),
        out_shape=[jax.ShapeDtypeStruct((4, rows, columns), jnp.bfloat16)] * 4
        + [jax.ShapeDtypeStruct((4, 4, rows, others), jnp.bfloat16)],
        compiler_params=pltpu.CompilerParams(vmem_limit_bytes=VMEM_LIMIT),
        cost_estimate=SMALL,
    )(place, near_t, far_t, near, far)


def sum_kernel(*refs):
    for index in range(4):
        total = refs[0][index].astype(jnp.float32)
        for ref in refs[1:4]:
            total = total + ref[index].astype(jnp.float32)
        refs[4 + index][...] = total.astype(jnp.bfloat16)


def sum_pieces(pieces):
    _, rows, columns = pieces[0].shape
    return pl.pallas_call(
        sum_kernel,
        name="sum_pieces",
        out_shape=[jax.ShapeDtypeStruct((rows, columns), jnp.bfloat16)] * 4,
        compiler_params=pltpu.CompilerParams(vmem_limit_bytes=VMEM_LIMIT),
        cost_estimate=SMALL,
    )(*pieces)


def to_owners(pieces, axes):
    named = range(4) if axes == "x" else [0, 2, 1, 3]
    moved = [
        lax.ppermute(piece, axes, [(named[i], named[(i + d) % 4]) for i in range(4)])
        for d, piece in enumerate(pieces)
        if d
    ]
    return [pieces[0]] + moved


def conv_grad_kernel(
    grad_ref, image_ref, res_ref, taps_ref, gain_sum_ref, shift_sum_ref, up_first_ref, up_second_ref,
    out_ref, sums_ref, padded, image,
):
    side = image_ref.shape[1]
    blank = jnp.zeros((side, EDGE, LANES), jnp.float32)
    padded[:, 0:EDGE, :] = blank
    padded[:, EDGE + side : EDGE + side + EDGE, :] = blank
    image[...] = image_ref[0].astype(jnp.float32)
    bias_sum = jnp.zeros((side, LANES), jnp.float32)
    for row in range(side):
        cells = grad_ref[row * side : (row + 1) * side, :]
        padded[row, EDGE : EDGE + side, :] = cells
        bias_sum = bias_sum + cells
    sums_ref[49:50, :] = gain_sum_ref[...]
    sums_ref[50:51, :] = shift_sum_ref[...]
    sums_ref[51:52, :] = jnp.sum(bias_sum, axis=0, keepdims=True)
    sums_ref[52:53, :] = up_first_ref[...]
    sums_ref[53:54, :] = up_second_ref[...]
    sums_ref[54:, :] = jnp.zeros((SMALL_ROWS - 54, LANES), jnp.float32)
    sums = [res_ref[0, row].astype(jnp.float32) for row in range(side)]
    for turn_col in range(7):
        weights = [
            jnp.broadcast_to(
                taps_ref[pl.ds(7 * (6 - turn_row) + 6 - turn_col, 1), :], (side, LANES)
            )
            for turn_row in range(7)
        ]
        parts = [jnp.zeros((8, LANES), jnp.float32) for _ in range(7)]
        for source in range(side):
            cells = padded[source, EDGE - 3 + turn_col : EDGE - 3 + turn_col + side, :]
            for turn_row in range(7):
                target = source + 3 - turn_row
                if 0 <= target < side:
                    sums[target] = sums[target] + cells * weights[turn_row]
                    product = cells * image[target]
                    parts[turn_row] = parts[turn_row] + (product[:8] + product[8:])
        for turn_row in range(7):
            tap = 7 * (6 - turn_row) + 6 - turn_col
            sums_ref[tap : tap + 1, :] = jnp.sum(parts[turn_row], axis=0, keepdims=True)
    for row in range(side):
        out_ref[0, row] = sums[row].astype(jnp.bfloat16)


def conv_backward(grad, image, residual, taps, gain_sum, shift_sum, up_sums):
    side, feat = image.shape[1], image.shape[3]
    cells = side * side
    picture = pl.BlockSpec((1, side, side, LANES), lambda i: (0, 0, 0, i))
    return pl.pallas_call(
        conv_grad_kernel,
        name="conv_backward",
        grid=(feat // LANES,),
        in_specs=[
            pl.BlockSpec((cells, LANES), lambda i: (0, i)),
            picture,
            picture,
            pl.BlockSpec((49, LANES), lambda i: (0, i)),
            pl.BlockSpec((1, LANES), lambda i: (0, i)),
            pl.BlockSpec((1, LANES), lambda i: (0, i)),
            pl.BlockSpec((1, LANES), lambda i: (0, i)),
            pl.BlockSpec((1, LANES), lambda i: (0, i + feat // LANES)),
        ],
        out_specs=[
            picture,
            pl.BlockSpec((SMALL_ROWS, LANES), lambda i: (0, i)),
        ],
        out_shape=(
            jax.ShapeDtypeStruct(image.shape, jnp.bfloat16),
            jax.ShapeDtypeStruct((SMALL_ROWS, feat), jnp.float32),
        ),
        scratch_shapes=[
            pltpu.VMEM((side, side + 2 * EDGE, LANES), jnp.float32),
            pltpu.VMEM((side, side, LANES), jnp.float32),
        ],
        compiler_params=pltpu.CompilerParams(vmem_limit_bytes=VMEM_LIMIT),
        cost_estimate=SMALL,
    )(grad, image, residual, taps, gain_sum, shift_sum, up_sums, up_sums)


def swap_pieces(values, axes):
    return lax.all_to_all(values, axes, 0, 0, tiled=True)


def total_of(received):
    return jnp.sum(received.astype(jnp.float32), axis=0)


def per_device(images, hidden_cot, residual_cot, w_up, b_up, ln_gain, ln_bias, dw_weight, dw_bias):
    feat, hid = w_up.shape
    plane = ("x", "y_hi", "y_lo")
    along_z = lax.axis_size("z")
    owned_rows = feat // (32 * along_z)
    inverse_count = 1.0 / (images.shape[0] * 32 * along_z)
    mine = lax.axis_index("core").astype(jnp.int32).reshape(1)
    y_index = 2 * lax.axis_index("y_hi") + lax.axis_index("y_lo")
    place = jnp.stack([lax.axis_index("x"), y_index]).astype(jnp.int32)
    swap = [(0, 1), (1, 0)]

    unit, sigma, turned, away, near, up_sums = front(
        mine, images, dw_weight, dw_bias, ln_gain, ln_bias, w_up, b_up.reshape(1, -1), hidden_cot, along_z
    )
    far = lax.ppermute(away, "core", swap)
    far_turned = lax.ppermute(turned, "core", swap)
    cells = unit.shape[0]
    *part_a, part_b = product(
        place, turned.reshape(4, 4, -1, cells), far_turned.reshape(4, 4, -1, cells), near, far, hid // 4
    )
    part_b, unit = lax.optimization_barrier((part_b, unit))
    part_a = to_owners(part_a, "x")
    part_b = swap_pieces(part_b, ("y_hi", "y_lo"))

    conv_grad, gain_sum, shift_sum = norm_grad(mine, away, near, w_up, unit, sigma, ln_gain)
    grad_input, small = conv_backward(
        conv_grad, images, residual_cot, dw_weight, gain_sum, shift_sum, up_sums
    )
    part_a, part_b, small = lax.optimization_barrier((part_a, part_b, small))
    part_a = to_owners(sum_pieces(part_a), ("y_lo", "y_hi"))
    part_b = swap_pieces(total_of(part_b).astype(jnp.bfloat16), "x")
    small = total_of(swap_pieces(small.reshape(16, -1, LANES), plane)).astype(jnp.bfloat16)

    last = jnp.concatenate([total_of(jnp.stack(part_a)), total_of(part_b)], axis=1).astype(jnp.bfloat16)
    last = last.reshape(2 * along_z, -1, LANES)
    height = last.shape[1]
    small = jnp.broadcast_to(small, (2 * along_z,) + small.shape)
    last = swap_pieces(jnp.concatenate([last, small], axis=1), ("z", "core"))
    small = total_of(last[:, height:]) * inverse_count
    small = swap_pieces(jnp.broadcast_to(small, (16,) + small.shape), plane).reshape(SMALL_ROWS, feat)
    last = total_of(last[:, :height].reshape(along_z, 2, owned_rows, hid // 2))
    owned = last.transpose(1, 0, 2).reshape(owned_rows, hid) * inverse_count
    return (
        grad_input,
        owned,
        small[52:54].reshape(hid),
        small[49],
        small[50],
        small[:49],
        small[51],
    )


def solution(mesh):
    x, z = 4, mesh.devices.size // 32
    split = Mesh(mesh.devices.reshape(2, x, z, 2, 2), ("y_lo", "x", "z", "y_hi", "core"))
    images = P(("y_lo", "x", "z", "y_hi", "core"))
    return jax.shard_map(
        per_device,
        mesh=split,
        in_specs=(images, images, images, P(), P(), P(), P(), P(), P()),
        out_specs=(images, images, P(), P(), P(), P(), P()),
        check_vma=False,
    )
```

```python
import jax
import jax.numpy as jnp
import numpy as np
from jax import lax
from jax.experimental import pallas as pl
from jax.experimental.pallas import tpu as pltpu
from jax.sharding import Mesh
from jax.sharding import PartitionSpec as P

LANES = 128
EDGE = 8
VMEM_LIMIT = 60 * 1024 * 1024
SMALL = pl.CostEstimate(flops=1000, bytes_accessed=1000, transcendentals=0)
SMALL_ROWS = 64


def front_kernel(
    core_ref, image_ref, taps_ref, bias_ref, gain_ref, shift_ref, order_ref, b_ref, w_hbm, cot_hbm,
    unit_out, sigma_ref, turned_ref, away_out, near_out, sums_ref,
    padded, conv, unit, normed, weights, cots, grads, in_sems, out_sems,
):
    side, feat = image_ref.shape[1], image_ref.shape[3]
    parts, _, width = weights.shape
    half = parts // 2
    core = core_ref[0]

    def column(part):
        owner = 1 - core if part < half else core
        return pl.multiple_of((owner * half + part % half) * width, width)

    loads = []
    for part in range(parts):
        columns = pl.ds(column(part), width)
        loads.append(
            (
                pltpu.make_async_copy(w_hbm.at[:, columns], weights.at[part], in_sems.at[2 * part]),
                pltpu.make_async_copy(cot_hbm.at[0, :, columns], cots.at[part], in_sems.at[2 * part + 1]),
            )
        )
    for pair in loads:
        pair[0].start()
        pair[1].start()

    blank = jnp.zeros((side, EDGE, LANES), jnp.float32)
    padded[:, 0:EDGE, :] = blank
    padded[:, EDGE + side : EDGE + side + EDGE, :] = blank

    @pl.loop(0, feat // LANES)
    def _(block):
        lanes = pl.ds(pl.multiple_of(block * LANES, LANES), LANES)
        padded[:, EDGE : EDGE + side, :] = image_ref[0, :, :, lanes].astype(jnp.float32)
        start = jnp.broadcast_to(bias_ref[lanes].reshape(1, LANES), (side, LANES))
        sums = [start] * side
        for tap_col in range(7):
            taps = [
                jnp.broadcast_to(taps_ref[pl.ds(7 * tap_row + tap_col, 1), lanes], (side, LANES))
                for tap_row in range(7)
            ]
            for source in range(side):
                cells = padded[source, EDGE - 3 + tap_col : EDGE - 3 + tap_col + side, :]
                for tap_row in range(7):
                    target = source + 3 - tap_row
                    if 0 <= target < side:
                        sums[target] = sums[target] + cells * taps[tap_row]
        for row in range(side):
            conv[row * side : (row + 1) * side, lanes] = sums[row]

    gain = gain_ref[...].reshape(1, feat)
    shift = shift_ref[...].reshape(1, feat)

    @pl.loop(0, side, unroll=4)
    def _(row):
        cells = pl.ds(pl.multiple_of(row * side, side), side)
        values = conv[cells, :]
        centred = values - jnp.mean(values, axis=-1, keepdims=True)
        inv_sigma = lax.rsqrt(jnp.mean(centred * centred, axis=-1, keepdims=True) + 1e-06)
        scaled = centred * inv_sigma
        unit[cells, :] = scaled
        sigma_ref[cells, :] = jnp.broadcast_to(inv_sigma, (side, LANES))
        normed[cells, :] = (scaled * gain + shift).astype(jnp.bfloat16)

    unit_copy = pltpu.make_async_copy(unit, unit_out, out_sems.at[0])
    unit_copy.start()

    group = order_ref.shape[0]
    rows = turned_ref.shape[3]
    for index in range(feat // group):
        y_lo, pair = divmod(index, 2)
        turned = lax.dot_general(
            order_ref[...],
            normed[:, index * group : (index + 1) * group],
            (((1,), (1,)), ((), ())),
            preferred_element_type=jnp.float32,
        ).astype(jnp.bfloat16)
        for within in range(2):
            for y_hi in range(2):
                first = (within * 2 + y_hi) * rows
                turned_ref[2 * pair + within, y_hi, y_lo] = turned[first : first + rows]

    stores = [unit_copy]
    for part in range(parts):
        loads[part][0].wait()
        loads[part][1].wait()
        columns = pl.ds(column(part), width)
        pre_act = jnp.dot(normed[...], weights[part], preferred_element_type=jnp.float32)
        pre_act = pre_act + b_ref[:, columns]
        slope = 0.5 * (1.0 + lax.erf(pre_act * 0.7071067811865476)) + pre_act * jnp.exp(
            -0.5 * pre_act * pre_act
        ) * 0.3989422804014327
        grad = (cots[part].astype(jnp.float32) * slope).astype(jnp.bfloat16)
        grads[part] = grad
        sums_ref[:, columns] = jnp.sum(grad.astype(jnp.float32), axis=0, keepdims=True)
        target = away_out if part < half else near_out
        copy = pltpu.make_async_copy(
            grads.at[part], target.at[:, (part % half) * width : (part % half + 1) * width], out_sems.at[1 + part]
        )
        copy.start()
        stores.append(copy)
    for copy in stores:
        copy.wait()


def channel_order(rows, along_z):
    width = 4 * rows
    owned = rows // along_z
    target = np.arange(width).reshape(2, along_z, 2, owned).transpose(0, 2, 1, 3).reshape(-1)
    return jnp.asarray(np.eye(width, dtype=np.float32)[target], jnp.bfloat16)


def front(core, image, taps, bias, gain, shift, w_up, b_row, cot, along_z, parts=4):
    side, feat = image.shape[1], image.shape[3]
    cells = side * side
    hid = w_up.shape[1]
    rows = feat // 16
    width = hid // parts
    whole = pl.BlockSpec(memory_space=pltpu.VMEM)
    remain = pl.BlockSpec(memory_space=pl.ANY)
    return pl.pallas_call(
        front_kernel,
        name="front",
        in_specs=[pl.BlockSpec(memory_space=pltpu.SMEM)] + [whole] * 7 + [remain] * 2,
        out_specs=[remain, whole, whole, remain, remain, whole],
        out_shape=(
            jax.ShapeDtypeStruct((cells, feat), jnp.float32),
            jax.ShapeDtypeStruct((cells, LANES), jnp.float32),
            jax.ShapeDtypeStruct((4, 2, 2, rows, cells), jnp.bfloat16),
            jax.ShapeDtypeStruct((cells, hid // 2), jnp.bfloat16),
            jax.ShapeDtypeStruct((cells, hid // 2), jnp.bfloat16),
            jax.ShapeDtypeStruct((1, hid), jnp.float32),
        ),
        scratch_shapes=[
            pltpu.VMEM((side, side + 2 * EDGE, LANES), jnp.float32),
            pltpu.VMEM((cells, feat), jnp.float32),
            pltpu.VMEM((cells, feat), jnp.float32),
            pltpu.VMEM((cells, feat), jnp.bfloat16),
            pltpu.VMEM((parts, feat, width), jnp.bfloat16),
            pltpu.VMEM((parts, cells, width), jnp.bfloat16),
            pltpu.VMEM((parts, cells, width), jnp.bfloat16),
            pltpu.SemaphoreType.DMA((2 * parts,)),
            pltpu.SemaphoreType.DMA((1 + parts,)),
        ],
        compiler_params=pltpu.CompilerParams(vmem_limit_bytes=VMEM_LIMIT),
        cost_estimate=SMALL,
    )(core, image, taps, bias, gain, shift, channel_order(rows, along_z), b_row, w_up, cot)


def product_kernel(place_ref, near_t_ref, far_t_ref, near_ref, far_ref, *out_refs):
    _, along_y, rows, cells = near_t_ref.shape
    block = (
        jnp.dot(near_t_ref[...].reshape(along_y * rows, cells), near_ref[...], preferred_element_type=jnp.float32)
        + jnp.dot(far_t_ref[...].reshape(along_y * rows, cells), far_ref[...], preferred_element_type=jnp.float32)
    ).astype(jnp.bfloat16)
    columns = out_refs[0].shape[2]
    out_refs[4][...] = block[:, columns:].reshape(out_refs[4].shape)
    for steps in range(4):

        @pl.when(pl.program_id(0) == steps)
        def _():
            for y in range(along_y):
                out_refs[steps][lax.rem(y - place_ref[1] + 4, 4)] = block[y * rows : (y + 1) * rows, :columns]


def product(place, near_t, far_t, near, far, columns):
    _, _, rows, cells = near_t.shape
    others = near.shape[1] - columns
    left = pl.BlockSpec((1, 4, rows, cells), lambda i, p: (lax.rem(p[0] + i, 4), 0, 0, 0))
    right = pl.BlockSpec((cells, near.shape[1]), lambda i, p: (0, 0))
    return pl.pallas_call(
        product_kernel,
        name="product",
        grid_spec=pltpu.PrefetchScalarGridSpec(
            num_scalar_prefetch=1,
            grid=(4,),
            in_specs=[left, left, right, right],
            out_specs=[pl.BlockSpec((4, rows, columns), lambda i, p: (0, 0, 0))] * 4
            + [pl.BlockSpec((4, 1, rows, others), lambda i, p: (0, i, 0, 0))],
        ),
        out_shape=[jax.ShapeDtypeStruct((4, rows, columns), jnp.bfloat16)] * 4
        + [jax.ShapeDtypeStruct((4, 4, rows, others), jnp.bfloat16)],
        compiler_params=pltpu.CompilerParams(vmem_limit_bytes=VMEM_LIMIT),
        cost_estimate=SMALL,
    )(place, near_t, far_t, near, far)


def sum_kernel(*refs):
    ins, outs = refs[:-4], refs[-4:]
    for index in range(4):
        if len(ins) == 1:
            parts = [ins[0][source, index] for source in range(4)]
        else:
            parts = [ref[index] for ref in ins]
        total = parts[0].astype(jnp.float32)
        for part in parts[1:]:
            total = total + part.astype(jnp.float32)
        outs[index][...] = total.astype(jnp.bfloat16)


def sum_pieces(pieces):
    rows, columns = pieces[0].shape[-2:]
    return pl.pallas_call(
        sum_kernel,
        name="sum_pieces",
        out_shape=[jax.ShapeDtypeStruct((rows, columns), jnp.bfloat16)] * 4,
        compiler_params=pltpu.CompilerParams(vmem_limit_bytes=VMEM_LIMIT),
        cost_estimate=SMALL,
    )(*pieces)


def to_owners(pieces, axes):
    named = range(4) if axes == "x" else [0, 2, 1, 3]
    moved = [
        lax.ppermute(piece, axes, [(named[i], named[(i + d) % 4]) for i in range(4)])
        for d, piece in enumerate(pieces)
        if d
    ]
    return [pieces[0]] + moved


def back_kernel(
    core_ref, away_ref, near_ref, sigma_ref, gain_ref, up_first_ref, up_second_ref, image_ref, res_ref, taps_ref,
    unit_hbm, w_hbm, out_ref, sums_ref, weights, unit, total, norm_sums, padded, image, small, sems,
):
    side = image_ref.shape[1]
    feat = total.shape[1]

    @pl.when(pl.program_id(0) == 0)
    def _():
        parts, _, width = weights.shape
        half = parts // 2
        core = core_ref[0]
        loads = []
        for part in range(parts):
            owner = 1 - core if part < half else core
            columns = pl.ds(pl.multiple_of((owner * half + part % half) * width, width), width)
            loads.append(pltpu.make_async_copy(w_hbm.at[:, columns], weights.at[part], sems.at[part]))
        loads.append(pltpu.make_async_copy(unit_hbm, unit, sems.at[parts]))
        for load in loads:
            load.start()
        blank = jnp.zeros((side, EDGE, LANES), jnp.float32)
        padded[:, 0:EDGE, :] = blank
        padded[:, EDGE + side : EDGE + side + EDGE, :] = blank
        for part in range(parts):
            loads[part].wait()
            grad_ref = away_ref if part < half else near_ref
            grad = grad_ref[:, (part % half) * width : (part % half + 1) * width]
            value = lax.dot_general(
                grad, weights[part], (((1,), (1,)), ((), ())), preferred_element_type=jnp.float32
            )
            if part:
                total[...] += value
            else:
                total[...] = value
        loads[parts].wait()
        gain = gain_ref[...].reshape(1, feat)

        def finish(row, carry):
            gain_sum, shift_sum = carry
            cells = pl.ds(pl.multiple_of(row * 32, 32), 32)
            grad = total[cells, :]
            scaled = unit[cells, :]
            gain_sum = gain_sum + jnp.sum((grad * scaled).reshape(4, 8, feat), axis=0)
            shift_sum = shift_sum + jnp.sum(grad.reshape(4, 8, feat), axis=0)
            unit_grad = grad * gain
            first = jnp.sum(unit_grad, axis=-1, keepdims=True) * (1.0 / feat)
            second = jnp.sum(unit_grad * scaled, axis=-1, keepdims=True) * (1.0 / feat)
            total[cells, :] = sigma_ref[cells, 0:1] * (unit_grad - first - scaled * second)
            return gain_sum, shift_sum

        zero = jnp.zeros((8, feat), jnp.float32)
        gain_sum, shift_sum = lax.fori_loop(0, total.shape[0] // 32, finish, (zero, zero))
        norm_sums[0:1, :] = jnp.sum(gain_sum, axis=0, keepdims=True)
        norm_sums[1:2, :] = jnp.sum(shift_sum, axis=0, keepdims=True)

    lanes = pl.ds(pl.multiple_of(pl.program_id(0) * LANES, LANES), LANES)
    image[...] = image_ref[0].astype(jnp.float32)
    bias_sum = jnp.zeros((side, LANES), jnp.float32)
    for row in range(side):
        cells = total[row * side : (row + 1) * side, lanes]
        padded[row, EDGE : EDGE + side, :] = cells
        bias_sum = bias_sum + cells
    tap_sums = [None] * 49
    sums = [res_ref[0, row].astype(jnp.float32) for row in range(side)]
    for turn_col in range(7):
        weights_here = [
            jnp.broadcast_to(taps_ref[pl.ds(7 * (6 - turn_row) + 6 - turn_col, 1), :], (side, LANES))
            for turn_row in range(7)
        ]
        parts_here = [jnp.zeros((8, LANES), jnp.float32) for _ in range(7)]
        for source in range(side):
            cells = padded[source, EDGE - 3 + turn_col : EDGE - 3 + turn_col + side, :]
            for turn_row in range(7):
                target = source + 3 - turn_row
                if 0 <= target < side:
                    sums[target] = sums[target] + cells * weights_here[turn_row]
                    product = cells * image[target]
                    parts_here[turn_row] = parts_here[turn_row] + (product[:8] + product[8:])
        for turn_row in range(7):
            tap = 7 * (6 - turn_row) + 6 - turn_col
            small[tap : tap + 1, :] = jnp.sum(parts_here[turn_row], axis=0, keepdims=True)
    small[49:51, :] = norm_sums[0:2, lanes]
    small[51:52, :] = jnp.sum(bias_sum, axis=0, keepdims=True)
    small[52:53, :] = up_first_ref[...]
    small[53:54, :] = up_second_ref[...]
    small[54:, :] = jnp.zeros((SMALL_ROWS - 54, LANES), jnp.float32)
    sums_ref[0] = small[...].astype(jnp.bfloat16)
    for row in range(side):
        out_ref[0, row] = sums[row].astype(jnp.bfloat16)


def back(core, away, near, w_up, unit, sigma, gain, up_sums, image, residual, taps, parts=4):
    cells, feat = unit.shape
    side = image.shape[1]
    width = w_up.shape[1] // parts
    whole = pl.BlockSpec(memory_space=pltpu.VMEM)
    remain = pl.BlockSpec(memory_space=pl.ANY)
    picture = pl.BlockSpec((1, side, side, LANES), lambda i: (0, 0, 0, i))
    return pl.pallas_call(
        back_kernel,
        name="back",
        grid=(feat // LANES,),
        in_specs=[pl.BlockSpec(memory_space=pltpu.SMEM)]
        + [whole] * 4
        + [
            pl.BlockSpec((1, LANES), lambda i: (0, i)),
            pl.BlockSpec((1, LANES), lambda i: (0, i + feat // LANES)),
            picture,
            picture,
            pl.BlockSpec((49, LANES), lambda i: (0, i)),
            remain,
            remain,
        ],
        out_specs=[picture, pl.BlockSpec((1, SMALL_ROWS, LANES), lambda i: (i, 0, 0))],
        out_shape=(
            jax.ShapeDtypeStruct(image.shape, jnp.bfloat16),
            jax.ShapeDtypeStruct((feat // LANES, SMALL_ROWS, LANES), jnp.bfloat16),
        ),
        scratch_shapes=[
            pltpu.VMEM((parts, feat, width), jnp.bfloat16),
            pltpu.VMEM((cells, feat), jnp.float32),
            pltpu.VMEM((cells, feat), jnp.float32),
            pltpu.VMEM((8, feat), jnp.float32),
            pltpu.VMEM((side, side + 2 * EDGE, LANES), jnp.float32),
            pltpu.VMEM((side, side, LANES), jnp.float32),
            pltpu.VMEM((SMALL_ROWS, LANES), jnp.float32),
            pltpu.SemaphoreType.DMA((1 + parts,)),
        ],
        compiler_params=pltpu.CompilerParams(vmem_limit_bytes=VMEM_LIMIT),
        cost_estimate=SMALL,
    )(core, away, near, sigma, gain, up_sums, up_sums, image, residual, taps, unit, w_up)


def unpack_kernel(small_ref, up_ref, gain_ref, shift_ref, taps_ref, bias_ref):
    blocks = small_ref.shape[0]
    for block in range(blocks):
        values = small_ref[block].astype(jnp.float32)
        lanes = slice(block * LANES, (block + 1) * LANES)
        taps_ref[:, lanes] = values[:49]
        gain_ref[lanes] = values[49]
        shift_ref[lanes] = values[50]
        bias_ref[lanes] = values[51]
        up_ref[lanes] = values[52]
        up_ref[blocks * LANES + block * LANES : blocks * LANES + (block + 1) * LANES] = values[53]


def unpack(small):
    feat = small.shape[0] * LANES
    row = jax.ShapeDtypeStruct((feat,), jnp.float32)
    return pl.pallas_call(
        unpack_kernel,
        name="unpack",
        out_shape=(
            jax.ShapeDtypeStruct((2 * feat,), jnp.float32),
            row,
            row,
            jax.ShapeDtypeStruct((49, feat), jnp.float32),
            row,
        ),
        compiler_params=pltpu.CompilerParams(vmem_limit_bytes=VMEM_LIMIT),
        cost_estimate=SMALL,
    )(small)


def swap_pieces(values, axes):
    return lax.all_to_all(values, axes, 0, 0, tiled=True)


def total_of(received):
    return jnp.sum(received.astype(jnp.float32), axis=0)


def per_device(images, hidden_cot, residual_cot, w_up, b_up, ln_gain, ln_bias, dw_weight, dw_bias):
    feat, hid = w_up.shape
    plane = ("x", "y_hi", "y_lo")
    along_z = lax.axis_size("z")
    owned_rows = feat // (32 * along_z)
    inverse_count = 1.0 / (images.shape[0] * 32 * along_z)
    mine = lax.axis_index("core").astype(jnp.int32).reshape(1)
    y_index = 2 * lax.axis_index("y_hi") + lax.axis_index("y_lo")
    place = jnp.stack([lax.axis_index("x"), y_index]).astype(jnp.int32)
    swap = [(0, 1), (1, 0)]

    unit, sigma, turned, away, near, up_sums = front(
        mine, images, dw_weight, dw_bias, ln_gain, ln_bias, w_up, b_up.reshape(1, -1), hidden_cot, along_z
    )
    far = lax.ppermute(away, "core", swap)
    far_turned = lax.ppermute(turned, "core", swap)
    cells = unit.shape[0]
    *part_a, part_b = product(
        place, turned.reshape(4, 4, -1, cells), far_turned.reshape(4, 4, -1, cells), near, far, hid // 4
    )
    part_b, unit = lax.optimization_barrier((part_b, unit))
    part_a = to_owners(part_a, "x")
    part_b = swap_pieces(part_b, ("y_hi", "y_lo"))

    grad_input, small = back(
        mine, away, near, w_up, unit, sigma, ln_gain, up_sums, images, residual_cot, dw_weight
    )
    part_a, part_b, small = lax.optimization_barrier((part_a, part_b, small))
    small = total_of(swap_pieces(small.reshape(16, -1, LANES), plane)).astype(jnp.bfloat16)
    part_a = to_owners(sum_pieces(part_a), ("y_lo", "y_hi"))
    part_b = to_owners(sum_pieces([part_b]), "x")

    last = jnp.concatenate([total_of(jnp.stack(part_a)), total_of(jnp.stack(part_b))], axis=1)
    last = last.astype(jnp.bfloat16).reshape(2 * along_z, -1, LANES)
    height = last.shape[1]
    small = jnp.broadcast_to(small, (2 * along_z,) + small.shape)
    last = swap_pieces(jnp.concatenate([last, small], axis=1), ("z", "core"))
    small = (total_of(last[:, height:]) * inverse_count).astype(jnp.bfloat16)
    small = swap_pieces(jnp.broadcast_to(small, (16,) + small.shape), plane)
    small = small.reshape(-1, SMALL_ROWS, LANES)
    last = total_of(last[:, :height].reshape(along_z, 2, owned_rows, hid // 2))
    owned = last.transpose(1, 0, 2).reshape(owned_rows, hid) * inverse_count
    return (grad_input, owned, *unpack(small))


def solution(mesh):
    x, z = 4, mesh.devices.size // 32
    split = Mesh(mesh.devices.reshape(2, x, z, 2, 2), ("y_lo", "x", "z", "y_hi", "core"))
    images = P(("y_lo", "x", "z", "y_hi", "core"))
    return jax.shard_map(
        per_device,
        mesh=split,
        in_specs=(images, images, images, P(), P(), P(), P(), P(), P()),
        out_specs=(images, images, P(), P(), P(), P(), P()),
        check_vma=False,
    )
```

```python
import jax
import jax.numpy as jnp
import numpy as np
from jax import lax
from jax.experimental import pallas as pl
from jax.experimental.pallas import tpu as pltpu
from jax.sharding import Mesh
from jax.sharding import PartitionSpec as P

LANES = 128
EDGE = 8
VMEM_LIMIT = 60 * 1024 * 1024
SMALL = pl.CostEstimate(flops=1000, bytes_accessed=1000, transcendentals=0)
SMALL_ROWS = 64


def front_kernel(
    core_ref, image_ref, taps_ref, bias_ref, gain_ref, shift_ref, order_ref, b_ref, w_hbm, cot_hbm,
    unit_out, sigma_ref, turned_ref, away_out, near_out, sums_ref,
    padded, conv, unit, normed, weights, cots, grads, in_sems, out_sems,
):
    side, feat = image_ref.shape[1], image_ref.shape[3]
    parts, _, width = weights.shape
    half = parts // 2
    core = core_ref[0]

    def column(part):
        owner = 1 - core if part < half else core
        return pl.multiple_of((owner * half + part % half) * width, width)

    loads = []
    for part in range(parts):
        columns = pl.ds(column(part), width)
        loads.append(
            (
                pltpu.make_async_copy(w_hbm.at[:, columns], weights.at[part], in_sems.at[2 * part]),
                pltpu.make_async_copy(cot_hbm.at[0, :, columns], cots.at[part], in_sems.at[2 * part + 1]),
            )
        )
    for pair in loads:
        pair[0].start()
        pair[1].start()

    blank = jnp.zeros((side, EDGE, LANES), jnp.float32)
    padded[:, 0:EDGE, :] = blank
    padded[:, EDGE + side : EDGE + side + EDGE, :] = blank

    @pl.loop(0, feat // LANES)
    def _(block):
        lanes = pl.ds(pl.multiple_of(block * LANES, LANES), LANES)
        padded[:, EDGE : EDGE + side, :] = image_ref[0, :, :, lanes].astype(jnp.float32)
        start = jnp.broadcast_to(bias_ref[lanes].reshape(1, LANES), (side, LANES))
        sums = [start] * side
        for tap_col in range(7):
            taps = [
                jnp.broadcast_to(taps_ref[pl.ds(7 * tap_row + tap_col, 1), lanes], (side, LANES))
                for tap_row in range(7)
            ]
            for source in range(side):
                cells = padded[source, EDGE - 3 + tap_col : EDGE - 3 + tap_col + side, :]
                for tap_row in range(7):
                    target = source + 3 - tap_row
                    if 0 <= target < side:
                        sums[target] = sums[target] + cells * taps[tap_row]
        for row in range(side):
            conv[row * side : (row + 1) * side, lanes] = sums[row]

    gain = gain_ref[...].reshape(1, feat)
    shift = shift_ref[...].reshape(1, feat)

    @pl.loop(0, side, unroll=4)
    def _(row):
        cells = pl.ds(pl.multiple_of(row * side, side), side)
        values = conv[cells, :]
        centred = values - jnp.mean(values, axis=-1, keepdims=True)
        inv_sigma = lax.rsqrt(jnp.mean(centred * centred, axis=-1, keepdims=True) + 1e-06)
        scaled = centred * inv_sigma
        unit[cells, :] = scaled
        sigma_ref[cells, :] = jnp.broadcast_to(inv_sigma, (side, LANES))
        normed[cells, :] = (scaled * gain + shift).astype(jnp.bfloat16)

    unit_copy = pltpu.make_async_copy(unit, unit_out, out_sems.at[0])
    unit_copy.start()

    group = order_ref.shape[0]
    rows = turned_ref.shape[3]
    for index in range(feat // group):
        y_lo, pair = divmod(index, 2)
        turned = lax.dot_general(
            order_ref[...],
            normed[:, index * group : (index + 1) * group],
            (((1,), (1,)), ((), ())),
            preferred_element_type=jnp.float32,
        ).astype(jnp.bfloat16)
        for within in range(2):
            for y_hi in range(2):
                first = (within * 2 + y_hi) * rows
                turned_ref[2 * pair + within, y_hi, y_lo] = turned[first : first + rows]

    stores = [unit_copy]
    for part in range(parts):
        loads[part][0].wait()
        loads[part][1].wait()
        columns = pl.ds(column(part), width)
        pre_act = jnp.dot(normed[...], weights[part], preferred_element_type=jnp.float32)
        pre_act = pre_act + b_ref[:, columns]
        slope = 0.5 * (1.0 + lax.erf(pre_act * 0.7071067811865476)) + pre_act * jnp.exp(
            -0.5 * pre_act * pre_act
        ) * 0.3989422804014327
        grad = (cots[part].astype(jnp.float32) * slope).astype(jnp.bfloat16)
        grads[part] = grad
        sums_ref[:, columns] = jnp.sum(grad.astype(jnp.float32), axis=0, keepdims=True)
        target = away_out if part < half else near_out
        copy = pltpu.make_async_copy(
            grads.at[part], target.at[:, (part % half) * width : (part % half + 1) * width], out_sems.at[1 + part]
        )
        copy.start()
        stores.append(copy)
    for copy in stores:
        copy.wait()


def channel_order(rows, along_z):
    width = 4 * rows
    owned = rows // along_z
    target = np.arange(width).reshape(2, along_z, 2, owned).transpose(0, 2, 1, 3).reshape(-1)
    return jnp.asarray(np.eye(width, dtype=np.float32)[target], jnp.bfloat16)


def front(core, image, taps, bias, gain, shift, w_up, b_row, cot, along_z, parts=4):
    side, feat = image.shape[1], image.shape[3]
    cells = side * side
    hid = w_up.shape[1]
    rows = feat // 16
    width = hid // parts
    whole = pl.BlockSpec(memory_space=pltpu.VMEM)
    remain = pl.BlockSpec(memory_space=pl.ANY)
    return pl.pallas_call(
        front_kernel,
        name="front",
        in_specs=[pl.BlockSpec(memory_space=pltpu.SMEM)] + [whole] * 7 + [remain] * 2,
        out_specs=[remain, whole, whole, remain, remain, whole],
        out_shape=(
            jax.ShapeDtypeStruct((cells, feat), jnp.float32),
            jax.ShapeDtypeStruct((cells, LANES), jnp.float32),
            jax.ShapeDtypeStruct((4, 2, 2, rows, cells), jnp.bfloat16),
            jax.ShapeDtypeStruct((cells, hid // 2), jnp.bfloat16),
            jax.ShapeDtypeStruct((cells, hid // 2), jnp.bfloat16),
            jax.ShapeDtypeStruct((1, hid), jnp.float32),
        ),
        scratch_shapes=[
            pltpu.VMEM((side, side + 2 * EDGE, LANES), jnp.float32),
            pltpu.VMEM((cells, feat), jnp.float32),
            pltpu.VMEM((cells, feat), jnp.float32),
            pltpu.VMEM((cells, feat), jnp.bfloat16),
            pltpu.VMEM((parts, feat, width), jnp.bfloat16),
            pltpu.VMEM((parts, cells, width), jnp.bfloat16),
            pltpu.VMEM((parts, cells, width), jnp.bfloat16),
            pltpu.SemaphoreType.DMA((2 * parts,)),
            pltpu.SemaphoreType.DMA((1 + parts,)),
        ],
        compiler_params=pltpu.CompilerParams(vmem_limit_bytes=VMEM_LIMIT),
        cost_estimate=SMALL,
    )(core, image, taps, bias, gain, shift, channel_order(rows, along_z), b_row, w_up, cot)


def product_kernel(place_ref, near_t_ref, far_t_ref, near_ref, far_ref, *out_refs):
    _, along_y, rows, cells = near_t_ref.shape
    block = (
        jnp.dot(near_t_ref[...].reshape(along_y * rows, cells), near_ref[...], preferred_element_type=jnp.float32)
        + jnp.dot(far_t_ref[...].reshape(along_y * rows, cells), far_ref[...], preferred_element_type=jnp.float32)
    ).astype(jnp.bfloat16)
    columns = out_refs[0].shape[2]
    out_refs[4][...] = block[:, columns:].reshape(out_refs[4].shape)
    for steps in range(4):

        @pl.when(pl.program_id(0) == steps)
        def _():
            for y in range(along_y):
                out_refs[steps][lax.rem(y - place_ref[1] + 4, 4)] = block[y * rows : (y + 1) * rows, :columns]


def product(place, near_t, far_t, near, far, columns):
    _, _, rows, cells = near_t.shape
    others = near.shape[1] - columns
    left = pl.BlockSpec((1, 4, rows, cells), lambda i, p: (lax.rem(p[0] + i, 4), 0, 0, 0))
    right = pl.BlockSpec((cells, near.shape[1]), lambda i, p: (0, 0))
    return pl.pallas_call(
        product_kernel,
        name="product",
        grid_spec=pltpu.PrefetchScalarGridSpec(
            num_scalar_prefetch=1,
            grid=(4,),
            in_specs=[left, left, right, right],
            out_specs=[pl.BlockSpec((4, rows, columns), lambda i, p: (0, 0, 0))] * 4
            + [pl.BlockSpec((4, 1, rows, others), lambda i, p: (0, i, 0, 0))],
        ),
        out_shape=[jax.ShapeDtypeStruct((4, rows, columns), jnp.bfloat16)] * 4
        + [jax.ShapeDtypeStruct((4, 4, rows, others), jnp.bfloat16)],
        compiler_params=pltpu.CompilerParams(vmem_limit_bytes=VMEM_LIMIT),
        cost_estimate=SMALL,
    )(place, near_t, far_t, near, far)


def sum_kernel(*refs):
    ins, outs = refs[:-4], refs[-4:]
    for index in range(4):
        if len(ins) == 1:
            parts = [ins[0][source, index] for source in range(4)]
        else:
            parts = [ref[index] for ref in ins]
        total = parts[0].astype(jnp.float32)
        for part in parts[1:]:
            total = total + part.astype(jnp.float32)
        outs[index][...] = total.astype(jnp.bfloat16)


def sum_pieces(pieces):
    rows, columns = pieces[0].shape[-2:]
    return pl.pallas_call(
        sum_kernel,
        name="sum_pieces",
        out_shape=[jax.ShapeDtypeStruct((rows, columns), jnp.bfloat16)] * 4,
        compiler_params=pltpu.CompilerParams(vmem_limit_bytes=VMEM_LIMIT),
        cost_estimate=SMALL,
    )(*pieces)


def to_owners(pieces, axes):
    named = range(4) if axes == "x" else [0, 2, 1, 3]
    moved = [
        lax.ppermute(piece, axes, [(named[i], named[(i + d) % 4]) for i in range(4)])
        for d, piece in enumerate(pieces)
        if d
    ]
    return [pieces[0]] + moved


def back_kernel(
    core_ref, away_ref, near_ref, sigma_ref, gain_ref, up_first_ref, up_second_ref, image_ref, res_ref, taps_ref,
    unit_hbm, w_hbm, out_ref, sums_ref, weights, unit, total, norm_sums, padded, image, small, sems,
):
    side = image_ref.shape[1]
    feat = total.shape[1]

    @pl.when(pl.program_id(0) == 0)
    def _():
        parts, _, width = weights.shape
        half = parts // 2
        core = core_ref[0]
        loads = []
        for part in range(parts):
            owner = 1 - core if part < half else core
            columns = pl.ds(pl.multiple_of((owner * half + part % half) * width, width), width)
            loads.append(pltpu.make_async_copy(w_hbm.at[:, columns], weights.at[part], sems.at[part]))
        loads.append(pltpu.make_async_copy(unit_hbm, unit, sems.at[parts]))
        for load in loads:
            load.start()
        blank = jnp.zeros((side, EDGE, LANES), jnp.float32)
        padded[:, 0:EDGE, :] = blank
        padded[:, EDGE + side : EDGE + side + EDGE, :] = blank
        for part in range(parts):
            loads[part].wait()
            grad_ref = away_ref if part < half else near_ref
            grad = grad_ref[:, (part % half) * width : (part % half + 1) * width]
            value = lax.dot_general(
                grad, weights[part], (((1,), (1,)), ((), ())), preferred_element_type=jnp.float32
            )
            if part:
                total[...] += value
            else:
                total[...] = value
        loads[parts].wait()
        gain = gain_ref[...].reshape(1, feat)

        def finish(row, carry):
            gain_sum, shift_sum = carry
            cells = pl.ds(pl.multiple_of(row * 32, 32), 32)
            grad = total[cells, :]
            scaled = unit[cells, :]
            gain_sum = gain_sum + jnp.sum((grad * scaled).reshape(4, 8, feat), axis=0)
            shift_sum = shift_sum + jnp.sum(grad.reshape(4, 8, feat), axis=0)
            unit_grad = grad * gain
            first = jnp.sum(unit_grad, axis=-1, keepdims=True) * (1.0 / feat)
            second = jnp.sum(unit_grad * scaled, axis=-1, keepdims=True) * (1.0 / feat)
            total[cells, :] = sigma_ref[cells, 0:1] * (unit_grad - first - scaled * second)
            return gain_sum, shift_sum

        zero = jnp.zeros((8, feat), jnp.float32)
        gain_sum, shift_sum = lax.fori_loop(0, total.shape[0] // 32, finish, (zero, zero))
        norm_sums[0:1, :] = jnp.sum(gain_sum, axis=0, keepdims=True)
        norm_sums[1:2, :] = jnp.sum(shift_sum, axis=0, keepdims=True)

    lanes = pl.ds(pl.multiple_of(pl.program_id(0) * LANES, LANES), LANES)
    image[...] = image_ref[0].astype(jnp.float32)
    bias_sum = jnp.zeros((side, LANES), jnp.float32)
    for row in range(side):
        cells = total[row * side : (row + 1) * side, lanes]
        padded[row, EDGE : EDGE + side, :] = cells
        bias_sum = bias_sum + cells
    tap_sums = [None] * 49
    sums = [res_ref[0, row].astype(jnp.float32) for row in range(side)]
    for turn_col in range(7):
        weights_here = [
            jnp.broadcast_to(taps_ref[pl.ds(7 * (6 - turn_row) + 6 - turn_col, 1), :], (side, LANES))
            for turn_row in range(7)
        ]
        parts_here = [jnp.zeros((8, LANES), jnp.float32) for _ in range(7)]
        for source in range(side):
            cells = padded[source, EDGE - 3 + turn_col : EDGE - 3 + turn_col + side, :]
            for turn_row in range(7):
                target = source + 3 - turn_row
                if 0 <= target < side:
                    sums[target] = sums[target] + cells * weights_here[turn_row]
                    product = cells * image[target]
                    parts_here[turn_row] = parts_here[turn_row] + (product[:8] + product[8:])
        for turn_row in range(7):
            tap = 7 * (6 - turn_row) + 6 - turn_col
            small[tap : tap + 1, :] = jnp.sum(parts_here[turn_row], axis=0, keepdims=True)
    small[49:51, :] = norm_sums[0:2, lanes]
    small[51:52, :] = jnp.sum(bias_sum, axis=0, keepdims=True)
    small[52:53, :] = up_first_ref[...]
    small[53:54, :] = up_second_ref[...]
    small[54:, :] = jnp.zeros((SMALL_ROWS - 54, LANES), jnp.float32)
    sums_ref[0] = small[...].astype(jnp.bfloat16)
    for row in range(side):
        out_ref[0, row] = sums[row].astype(jnp.bfloat16)


def back(core, away, near, w_up, unit, sigma, gain, up_sums, image, residual, taps, parts=4):
    cells, feat = unit.shape
    side = image.shape[1]
    width = w_up.shape[1] // parts
    whole = pl.BlockSpec(memory_space=pltpu.VMEM)
    remain = pl.BlockSpec(memory_space=pl.ANY)
    picture = pl.BlockSpec((1, side, side, LANES), lambda i: (0, 0, 0, i))
    return pl.pallas_call(
        back_kernel,
        name="back",
        grid=(feat // LANES,),
        in_specs=[pl.BlockSpec(memory_space=pltpu.SMEM)]
        + [whole] * 4
        + [
            pl.BlockSpec((1, LANES), lambda i: (0, i)),
            pl.BlockSpec((1, LANES), lambda i: (0, i + feat // LANES)),
            picture,
            picture,
            pl.BlockSpec((49, LANES), lambda i: (0, i)),
            remain,
            remain,
        ],
        out_specs=[picture, pl.BlockSpec((1, SMALL_ROWS, LANES), lambda i: (i, 0, 0))],
        out_shape=(
            jax.ShapeDtypeStruct(image.shape, jnp.bfloat16),
            jax.ShapeDtypeStruct((feat // LANES, SMALL_ROWS, LANES), jnp.bfloat16),
        ),
        scratch_shapes=[
            pltpu.VMEM((parts, feat, width), jnp.bfloat16),
            pltpu.VMEM((cells, feat), jnp.float32),
            pltpu.VMEM((cells, feat), jnp.float32),
            pltpu.VMEM((8, feat), jnp.float32),
            pltpu.VMEM((side, side + 2 * EDGE, LANES), jnp.float32),
            pltpu.VMEM((side, side, LANES), jnp.float32),
            pltpu.VMEM((SMALL_ROWS, LANES), jnp.float32),
            pltpu.SemaphoreType.DMA((1 + parts,)),
        ],
        compiler_params=pltpu.CompilerParams(vmem_limit_bytes=VMEM_LIMIT),
        cost_estimate=SMALL,
    )(core, away, near, sigma, gain, up_sums, up_sums, image, residual, taps, unit, w_up)


def unpack_kernel(small_ref, up_ref, gain_ref, shift_ref, taps_ref, bias_ref):
    blocks = small_ref.shape[0]
    for block in range(blocks):
        values = small_ref[block].astype(jnp.float32)
        lanes = slice(block * LANES, (block + 1) * LANES)
        taps_ref[:, lanes] = values[:49]
        gain_ref[lanes] = values[49]
        shift_ref[lanes] = values[50]
        bias_ref[lanes] = values[51]
        up_ref[lanes] = values[52]
        up_ref[blocks * LANES + block * LANES : blocks * LANES + (block + 1) * LANES] = values[53]


def unpack(small):
    feat = small.shape[0] * LANES
    row = jax.ShapeDtypeStruct((feat,), jnp.float32)
    return pl.pallas_call(
        unpack_kernel,
        name="unpack",
        out_shape=(
            jax.ShapeDtypeStruct((2 * feat,), jnp.float32),
            row,
            row,
            jax.ShapeDtypeStruct((49, feat), jnp.float32),
            row,
        ),
        compiler_params=pltpu.CompilerParams(vmem_limit_bytes=VMEM_LIMIT),
        cost_estimate=SMALL,
    )(small)


def swap_pieces(values, axes):
    return lax.all_to_all(values, axes, 0, 0, tiled=True)


def total_of(received):
    return jnp.sum(received.astype(jnp.float32), axis=0)


def per_device(images, hidden_cot, residual_cot, w_up, b_up, ln_gain, ln_bias, dw_weight, dw_bias):
    feat, hid = w_up.shape
    plane = ("x", "y_hi", "y_lo")
    along_z = lax.axis_size("z")
    owned_rows = feat // (32 * along_z)
    inverse_count = 1.0 / (images.shape[0] * 32 * along_z)
    mine = lax.axis_index("core").astype(jnp.int32).reshape(1)
    y_index = 2 * lax.axis_index("y_hi") + lax.axis_index("y_lo")
    place = jnp.stack([lax.axis_index("x"), y_index]).astype(jnp.int32)
    swap = [(0, 1), (1, 0)]

    unit, sigma, turned, away, near, up_sums = front(
        mine, images, dw_weight, dw_bias, ln_gain, ln_bias, w_up, b_up.reshape(1, -1), hidden_cot, along_z
    )
    far = lax.ppermute(away, "core", swap)
    far_turned = lax.ppermute(turned, "core", swap)
    cells = unit.shape[0]
    *part_a, part_b = product(
        place, turned.reshape(4, 4, -1, cells), far_turned.reshape(4, 4, -1, cells), near, far, 7 * hid // 24
    )
    part_b, unit = lax.optimization_barrier((part_b, unit))
    part_a = to_owners(part_a, "x")
    part_b = swap_pieces(part_b, ("y_hi", "y_lo"))

    grad_input, small = back(
        mine, away, near, w_up, unit, sigma, ln_gain, up_sums, images, residual_cot, dw_weight
    )
    part_b, small = lax.optimization_barrier((part_b, small))

    around = ("z", "core")
    small = total_of(swap_pieces(small.reshape(16, -1, LANES), plane)).astype(jnp.bfloat16)
    part_a, small = lax.optimization_barrier((part_a, small))
    small = swap_pieces(jnp.broadcast_to(small, (2 * along_z,) + small.shape), around)
    small = (total_of(small) * inverse_count).astype(jnp.bfloat16)
    small = swap_pieces(jnp.broadcast_to(small, (16,) + small.shape), plane)
    small = small.reshape(-1, SMALL_ROWS, LANES)

    part_a = to_owners(sum_pieces(part_a), ("y_lo", "y_hi"))
    part_b = to_owners(sum_pieces([part_b]), "x")
    last = jnp.concatenate([total_of(jnp.stack(part_a)), total_of(jnp.stack(part_b))], axis=1)
    last = last.astype(jnp.bfloat16).reshape(2 * along_z, -1, LANES)
    last, small = lax.optimization_barrier((last, small))
    last = total_of(swap_pieces(last, around).reshape(along_z, 2, owned_rows, hid // 2))
    owned = last.transpose(1, 0, 2).reshape(owned_rows, hid) * inverse_count
    return (grad_input, owned, *unpack(small))


def solution(mesh):
    x, z = 4, mesh.devices.size // 32
    split = Mesh(mesh.devices.reshape(2, x, z, 2, 2), ("y_lo", "x", "z", "y_hi", "core"))
    images = P(("y_lo", "x", "z", "y_hi", "core"))
    return jax.shard_map(
        per_device,
        mesh=split,
        in_specs=(images, images, images, P(), P(), P(), P(), P(), P()),
        out_specs=(images, images, P(), P(), P(), P(), P()),
        check_vma=False,
    )
```

```python
import functools

import jax
import jax.numpy as jnp
import numpy as np
from jax import lax
from jax.experimental import pallas as pl
from jax.experimental.pallas import tpu as pltpu
from jax.sharding import Mesh
from jax.sharding import PartitionSpec as P

LANES = 128
EDGE = 8
VMEM_LIMIT = 60 * 1024 * 1024
SMALL = pl.CostEstimate(flops=1000, bytes_accessed=1000, transcendentals=0)
SMALL_ROWS = 64


def front_kernel(
    core_ref, image_ref, taps_ref, bias_ref, gain_ref, shift_ref, order_ref, b_ref, w_hbm, cot_hbm,
    unit_out, sigma_ref, turned_ref, away_out, near_out, sums_ref,
    padded, conv, unit, normed, weights, cots, grads, in_sems, out_sems,
):
    side, feat = image_ref.shape[1], image_ref.shape[3]
    parts, _, width = weights.shape
    half = parts // 2
    core = core_ref[0]

    def column(part):
        owner = 1 - core if part < half else core
        return pl.multiple_of((owner * half + part % half) * width, width)

    loads = []
    for part in range(parts):
        columns = pl.ds(column(part), width)
        loads.append(
            (
                pltpu.make_async_copy(w_hbm.at[:, columns], weights.at[part], in_sems.at[2 * part]),
                pltpu.make_async_copy(cot_hbm.at[0, :, columns], cots.at[part], in_sems.at[2 * part + 1]),
            )
        )
    for pair in loads:
        pair[0].start()
        pair[1].start()

    blank = jnp.zeros((side, EDGE, LANES), jnp.float32)
    padded[:, 0:EDGE, :] = blank
    padded[:, EDGE + side : EDGE + side + EDGE, :] = blank

    @pl.loop(0, feat // LANES)
    def _(block):
        lanes = pl.ds(pl.multiple_of(block * LANES, LANES), LANES)
        padded[:, EDGE : EDGE + side, :] = image_ref[0, :, :, lanes].astype(jnp.float32)
        start = jnp.broadcast_to(bias_ref[lanes].reshape(1, LANES), (side, LANES))
        sums = [start] * side
        for tap_col in range(7):
            taps = [
                jnp.broadcast_to(taps_ref[pl.ds(7 * tap_row + tap_col, 1), lanes], (side, LANES))
                for tap_row in range(7)
            ]
            for source in range(side):
                cells = padded[source, EDGE - 3 + tap_col : EDGE - 3 + tap_col + side, :]
                for tap_row in range(7):
                    target = source + 3 - tap_row
                    if 0 <= target < side:
                        sums[target] = sums[target] + cells * taps[tap_row]
        for row in range(side):
            conv[row * side : (row + 1) * side, lanes] = sums[row]

    gain = gain_ref[...].reshape(1, feat)
    shift = shift_ref[...].reshape(1, feat)

    @pl.loop(0, side, unroll=4)
    def _(row):
        cells = pl.ds(pl.multiple_of(row * side, side), side)
        values = conv[cells, :]
        centred = values - jnp.mean(values, axis=-1, keepdims=True)
        inv_sigma = lax.rsqrt(jnp.mean(centred * centred, axis=-1, keepdims=True) + 1e-06)
        scaled = centred * inv_sigma
        unit[cells, :] = scaled
        sigma_ref[cells, :] = jnp.broadcast_to(inv_sigma, (side, LANES))
        normed[cells, :] = (scaled * gain + shift).astype(jnp.bfloat16)

    unit_copy = pltpu.make_async_copy(unit, unit_out, out_sems.at[0])
    unit_copy.start()

    group = order_ref.shape[0]
    rows = turned_ref.shape[3]
    for index in range(feat // group):
        y_lo, pair = divmod(index, 2)
        turned = lax.dot_general(
            order_ref[...],
            normed[:, index * group : (index + 1) * group],
            (((1,), (1,)), ((), ())),
            preferred_element_type=jnp.float32,
        ).astype(jnp.bfloat16)
        for within in range(2):
            for y_hi in range(2):
                first = (within * 2 + y_hi) * rows
                turned_ref[2 * pair + within, y_hi, y_lo] = turned[first : first + rows]

    stores = [unit_copy]
    for part in range(parts):
        loads[part][0].wait()
        loads[part][1].wait()
        columns = pl.ds(column(part), width)
        pre_act = jnp.dot(normed[...], weights[part], preferred_element_type=jnp.float32)
        pre_act = pre_act + b_ref[:, columns]
        slope = 0.5 * (1.0 + lax.erf(pre_act * 0.7071067811865476)) + pre_act * jnp.exp(
            -0.5 * pre_act * pre_act
        ) * 0.3989422804014327
        grad = (cots[part].astype(jnp.float32) * slope).astype(jnp.bfloat16)
        grads[part] = grad
        sums_ref[:, columns] = jnp.sum(grad.astype(jnp.float32), axis=0, keepdims=True)
        target = away_out if part < half else near_out
        copy = pltpu.make_async_copy(
            grads.at[part], target.at[:, (part % half) * width : (part % half + 1) * width], out_sems.at[1 + part]
        )
        copy.start()
        stores.append(copy)
    for copy in stores:
        copy.wait()


def channel_order(rows, along_z):
    width = 4 * rows
    owned = rows // along_z
    target = np.arange(width).reshape(2, along_z, 2, owned).transpose(0, 2, 1, 3).reshape(-1)
    return jnp.asarray(np.eye(width, dtype=np.float32)[target], jnp.bfloat16)


def front(core, image, taps, bias, gain, shift, w_up, b_row, cot, along_z, parts=4):
    side, feat = image.shape[1], image.shape[3]
    cells = side * side
    hid = w_up.shape[1]
    rows = feat // 16
    width = hid // parts
    whole = pl.BlockSpec(memory_space=pltpu.VMEM)
    remain = pl.BlockSpec(memory_space=pl.ANY)
    return pl.pallas_call(
        front_kernel,
        name="front",
        in_specs=[pl.BlockSpec(memory_space=pltpu.SMEM)] + [whole] * 7 + [remain] * 2,
        out_specs=[remain, whole, whole, remain, remain, whole],
        out_shape=(
            jax.ShapeDtypeStruct((cells, feat), jnp.float32),
            jax.ShapeDtypeStruct((cells, LANES), jnp.float32),
            jax.ShapeDtypeStruct((4, 2, 2, rows, cells), jnp.bfloat16),
            jax.ShapeDtypeStruct((cells, hid // 2), jnp.bfloat16),
            jax.ShapeDtypeStruct((cells, hid // 2), jnp.bfloat16),
            jax.ShapeDtypeStruct((1, hid), jnp.float32),
        ),
        scratch_shapes=[
            pltpu.VMEM((side, side + 2 * EDGE, LANES), jnp.float32),
            pltpu.VMEM((cells, feat), jnp.float32),
            pltpu.VMEM((cells, feat), jnp.float32),
            pltpu.VMEM((cells, feat), jnp.bfloat16),
            pltpu.VMEM((parts, feat, width), jnp.bfloat16),
            pltpu.VMEM((parts, cells, width), jnp.bfloat16),
            pltpu.VMEM((parts, cells, width), jnp.bfloat16),
            pltpu.SemaphoreType.DMA((2 * parts,)),
            pltpu.SemaphoreType.DMA((1 + parts,)),
        ],
        compiler_params=pltpu.CompilerParams(vmem_limit_bytes=VMEM_LIMIT),
        cost_estimate=SMALL,
    )(core, image, taps, bias, gain, shift, channel_order(rows, along_z), b_row, w_up, cot)


def product_kernel(place_ref, near_t_ref, far_t_ref, near_ref, far_ref, *out_refs):
    _, along_y, rows, cells = near_t_ref.shape
    block = (
        jnp.dot(near_t_ref[...].reshape(along_y * rows, cells), near_ref[...], preferred_element_type=jnp.float32)
        + jnp.dot(far_t_ref[...].reshape(along_y * rows, cells), far_ref[...], preferred_element_type=jnp.float32)
    ).astype(jnp.bfloat16)
    columns = out_refs[0].shape[2]
    out_refs[4][...] = block[:, columns:].reshape(out_refs[4].shape)
    for steps in range(4):

        @pl.when(pl.program_id(0) == steps)
        def _():
            for y in range(along_y):
                out_refs[steps][lax.rem(y - place_ref[1] + 4, 4)] = block[y * rows : (y + 1) * rows, :columns]


def product(place, near_t, far_t, near, far, columns):
    _, _, rows, cells = near_t.shape
    others = near.shape[1] - columns
    left = pl.BlockSpec((1, 4, rows, cells), lambda i, p: (lax.rem(p[0] + i, 4), 0, 0, 0))
    right = pl.BlockSpec((cells, near.shape[1]), lambda i, p: (0, 0))
    return pl.pallas_call(
        product_kernel,
        name="product",
        grid_spec=pltpu.PrefetchScalarGridSpec(
            num_scalar_prefetch=1,
            grid=(4,),
            in_specs=[left, left, right, right],
            out_specs=[pl.BlockSpec((4, rows, columns), lambda i, p: (0, 0, 0))] * 4
            + [pl.BlockSpec((4, 1, rows, others), lambda i, p: (0, i, 0, 0))],
        ),
        out_shape=[jax.ShapeDtypeStruct((4, rows, columns), jnp.bfloat16)] * 4
        + [jax.ShapeDtypeStruct((4, 4, rows, others), jnp.bfloat16)],
        compiler_params=pltpu.CompilerParams(vmem_limit_bytes=VMEM_LIMIT),
        cost_estimate=SMALL,
    )(place, near_t, far_t, near, far)


def sum_kernel(*refs):
    ins, outs = refs[:-4], refs[-4:]
    for index in range(4):
        if len(ins) == 1:
            parts = [ins[0][source, index] for source in range(4)]
        else:
            parts = [ref[index] for ref in ins]
        total = parts[0].astype(jnp.float32)
        for part in parts[1:]:
            total = total + part.astype(jnp.float32)
        outs[index][...] = total.astype(jnp.bfloat16)


def sum_pieces(pieces):
    rows, columns = pieces[0].shape[-2:]
    return pl.pallas_call(
        sum_kernel,
        name="sum_pieces",
        out_shape=[jax.ShapeDtypeStruct((rows, columns), jnp.bfloat16)] * 4,
        compiler_params=pltpu.CompilerParams(vmem_limit_bytes=VMEM_LIMIT),
        cost_estimate=SMALL,
    )(*pieces)


def to_owners(pieces, axes):
    named = range(4) if axes == "x" else [0, 2, 1, 3]
    moved = [
        lax.ppermute(piece, axes, [(named[i], named[(i + d) % 4]) for i in range(4)])
        for d, piece in enumerate(pieces)
        if d
    ]
    return [pieces[0]] + moved


def back_kernel(
    core_ref, away_ref, near_ref, sigma_ref, gain_ref, up_first_ref, up_second_ref, image_ref, res_ref, taps_ref,
    unit_hbm, w_hbm, out_ref, sums_ref, weights, unit, total, norm_sums, padded, image, small, sems,
):
    side = image_ref.shape[1]
    feat = total.shape[1]

    @pl.when(pl.program_id(0) == 0)
    def _():
        parts, _, width = weights.shape
        half = parts // 2
        core = core_ref[0]
        loads = []
        for part in range(parts):
            owner = 1 - core if part < half else core
            columns = pl.ds(pl.multiple_of((owner * half + part % half) * width, width), width)
            loads.append(pltpu.make_async_copy(w_hbm.at[:, columns], weights.at[part], sems.at[part]))
        loads.append(pltpu.make_async_copy(unit_hbm, unit, sems.at[parts]))
        for load in loads:
            load.start()
        blank = jnp.zeros((side, EDGE, LANES), jnp.float32)
        padded[:, 0:EDGE, :] = blank
        padded[:, EDGE + side : EDGE + side + EDGE, :] = blank
        for part in range(parts):
            loads[part].wait()
            grad_ref = away_ref if part < half else near_ref
            grad = grad_ref[:, (part % half) * width : (part % half + 1) * width]
            value = lax.dot_general(
                grad, weights[part], (((1,), (1,)), ((), ())), preferred_element_type=jnp.float32
            )
            if part:
                total[...] += value
            else:
                total[...] = value
        loads[parts].wait()
        gain = gain_ref[...].reshape(1, feat)

        def finish(row, carry):
            gain_sum, shift_sum = carry
            cells = pl.ds(pl.multiple_of(row * 32, 32), 32)
            grad = total[cells, :]
            scaled = unit[cells, :]
            gain_sum = gain_sum + jnp.sum((grad * scaled).reshape(4, 8, feat), axis=0)
            shift_sum = shift_sum + jnp.sum(grad.reshape(4, 8, feat), axis=0)
            unit_grad = grad * gain
            first = jnp.sum(unit_grad, axis=-1, keepdims=True) * (1.0 / feat)
            second = jnp.sum(unit_grad * scaled, axis=-1, keepdims=True) * (1.0 / feat)
            total[cells, :] = sigma_ref[cells, 0:1] * (unit_grad - first - scaled * second)
            return gain_sum, shift_sum

        zero = jnp.zeros((8, feat), jnp.float32)
        gain_sum, shift_sum = lax.fori_loop(0, total.shape[0] // 32, finish, (zero, zero))
        norm_sums[0:1, :] = jnp.sum(gain_sum, axis=0, keepdims=True)
        norm_sums[1:2, :] = jnp.sum(shift_sum, axis=0, keepdims=True)

    lanes = pl.ds(pl.multiple_of(pl.program_id(0) * LANES, LANES), LANES)
    image[...] = image_ref[0].astype(jnp.float32)
    bias_sum = jnp.zeros((side, LANES), jnp.float32)
    for row in range(side):
        cells = total[row * side : (row + 1) * side, lanes]
        padded[row, EDGE : EDGE + side, :] = cells
        bias_sum = bias_sum + cells
    tap_sums = [None] * 49
    sums = [res_ref[0, row].astype(jnp.float32) for row in range(side)]
    for turn_col in range(7):
        weights_here = [
            jnp.broadcast_to(taps_ref[pl.ds(7 * (6 - turn_row) + 6 - turn_col, 1), :], (side, LANES))
            for turn_row in range(7)
        ]
        parts_here = [jnp.zeros((8, LANES), jnp.float32) for _ in range(7)]
        for source in range(side):
            cells = padded[source, EDGE - 3 + turn_col : EDGE - 3 + turn_col + side, :]
            for turn_row in range(7):
                target = source + 3 - turn_row
                if 0 <= target < side:
                    sums[target] = sums[target] + cells * weights_here[turn_row]
                    product = cells * image[target]
                    parts_here[turn_row] = parts_here[turn_row] + (product[:8] + product[8:])
        for turn_row in range(7):
            tap = 7 * (6 - turn_row) + 6 - turn_col
            small[tap : tap + 1, :] = jnp.sum(parts_here[turn_row], axis=0, keepdims=True)
    small[49:51, :] = norm_sums[0:2, lanes]
    small[51:52, :] = jnp.sum(bias_sum, axis=0, keepdims=True)
    small[52:53, :] = up_first_ref[...]
    small[53:54, :] = up_second_ref[...]
    small[54:, :] = jnp.zeros((SMALL_ROWS - 54, LANES), jnp.float32)
    sums_ref[0] = small[...].astype(jnp.bfloat16)
    for row in range(side):
        out_ref[0, row] = sums[row].astype(jnp.bfloat16)


def back(core, away, near, w_up, unit, sigma, gain, up_sums, image, residual, taps, parts=4):
    cells, feat = unit.shape
    side = image.shape[1]
    width = w_up.shape[1] // parts
    whole = pl.BlockSpec(memory_space=pltpu.VMEM)
    remain = pl.BlockSpec(memory_space=pl.ANY)
    picture = pl.BlockSpec((1, side, side, LANES), lambda i: (0, 0, 0, i))
    return pl.pallas_call(
        back_kernel,
        name="back",
        grid=(feat // LANES,),
        in_specs=[pl.BlockSpec(memory_space=pltpu.SMEM)]
        + [whole] * 4
        + [
            pl.BlockSpec((1, LANES), lambda i: (0, i)),
            pl.BlockSpec((1, LANES), lambda i: (0, i + feat // LANES)),
            picture,
            picture,
            pl.BlockSpec((49, LANES), lambda i: (0, i)),
            remain,
            remain,
        ],
        out_specs=[picture, pl.BlockSpec((1, SMALL_ROWS, LANES), lambda i: (i, 0, 0))],
        out_shape=(
            jax.ShapeDtypeStruct(image.shape, jnp.bfloat16),
            jax.ShapeDtypeStruct((feat // LANES, SMALL_ROWS, LANES), jnp.bfloat16),
        ),
        scratch_shapes=[
            pltpu.VMEM((parts, feat, width), jnp.bfloat16),
            pltpu.VMEM((cells, feat), jnp.float32),
            pltpu.VMEM((cells, feat), jnp.float32),
            pltpu.VMEM((8, feat), jnp.float32),
            pltpu.VMEM((side, side + 2 * EDGE, LANES), jnp.float32),
            pltpu.VMEM((side, side, LANES), jnp.float32),
            pltpu.VMEM((SMALL_ROWS, LANES), jnp.float32),
            pltpu.SemaphoreType.DMA((1 + parts,)),
        ],
        compiler_params=pltpu.CompilerParams(vmem_limit_bytes=VMEM_LIMIT),
        cost_estimate=SMALL,
    )(core, away, near, sigma, gain, up_sums, up_sums, image, residual, taps, unit, w_up)


def finish_kernel(inverse_count, received_ref, owned_ref, up_ref, gain_ref, shift_ref, taps_ref, bias_ref):
    pieces, height, _ = received_ref.shape
    owned_rows, hid = owned_ref.shape
    blocks = hid // 2 // LANES
    share = height - owned_rows * blocks
    for core in range(2):
        total = received_ref[core, share:, :].astype(jnp.float32)
        for z in range(1, pieces // 2):
            total = total + received_ref[2 * z + core, share:, :].astype(jnp.float32)
        total = total * inverse_count
        for row in range(owned_rows):
            for block in range(blocks):
                first = (core * blocks + block) * LANES
                index = row * blocks + block
                owned_ref[row : row + 1, first : first + LANES] = total[index : index + 1]
    feat = gain_ref.shape[0]
    for block in range(feat // LANES):
        parts = []
        row, end = block * SMALL_ROWS, (block + 1) * SMALL_ROWS
        while row < end:
            stop = min(end, (row // share + 1) * share)
            first = row % share
            parts.append(received_ref[row // share, first : first + stop - row, :].astype(jnp.float32))
            row = stop
        values = jnp.concatenate(parts, axis=0)
        lanes = slice(block * LANES, (block + 1) * LANES)
        taps_ref[:, lanes] = values[:49]
        gain_ref[lanes] = values[49]
        shift_ref[lanes] = values[50]
        bias_ref[lanes] = values[51]
        up_ref[lanes] = values[52]
        up_ref[feat + block * LANES : feat + (block + 1) * LANES] = values[53]


def finish(received, owned_rows, feat, hid, inverse_count):
    row = jax.ShapeDtypeStruct((feat,), jnp.float32)
    return pl.pallas_call(
        functools.partial(finish_kernel, inverse_count),
        name="finish",
        out_shape=(
            jax.ShapeDtypeStruct((owned_rows, hid), jnp.float32),
            jax.ShapeDtypeStruct((hid,), jnp.float32),
            row,
            row,
            jax.ShapeDtypeStruct((49, feat), jnp.float32),
            row,
        ),
        compiler_params=pltpu.CompilerParams(vmem_limit_bytes=VMEM_LIMIT),
        cost_estimate=SMALL,
    )(received)


def swap_pieces(values, axes):
    return lax.all_to_all(values, axes, 0, 0, tiled=True)


def total_of(received):
    return jnp.sum(received.astype(jnp.float32), axis=0)


def per_device(images, hidden_cot, residual_cot, w_up, b_up, ln_gain, ln_bias, dw_weight, dw_bias):
    feat, hid = w_up.shape
    plane = ("x", "y_hi", "y_lo")
    along_z = lax.axis_size("z")
    owned_rows = feat // (32 * along_z)
    inverse_count = 1.0 / (images.shape[0] * 32 * along_z)
    mine = lax.axis_index("core").astype(jnp.int32).reshape(1)
    y_index = 2 * lax.axis_index("y_hi") + lax.axis_index("y_lo")
    place = jnp.stack([lax.axis_index("x"), y_index]).astype(jnp.int32)
    swap = [(0, 1), (1, 0)]

    unit, sigma, turned, away, near, up_sums = front(
        mine, images, dw_weight, dw_bias, ln_gain, ln_bias, w_up, b_up.reshape(1, -1), hidden_cot, along_z
    )
    far = lax.ppermute(away, "core", swap)
    far_turned = lax.ppermute(turned, "core", swap)
    cells = unit.shape[0]
    *part_a, part_b = product(
        place, turned.reshape(4, 4, -1, cells), far_turned.reshape(4, 4, -1, cells), near, far, 7 * hid // 24
    )
    part_b, unit = lax.optimization_barrier((part_b, unit))
    part_a = to_owners(part_a, "x")
    part_b = swap_pieces(part_b, ("y_hi", "y_lo"))

    grad_input, small = back(
        mine, away, near, w_up, unit, sigma, ln_gain, up_sums, images, residual_cot, dw_weight
    )
    part_b, small = lax.optimization_barrier((part_b, small))

    around = ("z", "core")
    small = swap_pieces(small.reshape(2 * along_z, -1, LANES), around)
    small = total_of(small).astype(jnp.bfloat16)
    part_a, small = lax.optimization_barrier((part_a, small))
    small = swap_pieces(jnp.broadcast_to(small, (16,) + small.shape), plane)

    part_b = to_owners(sum_pieces([part_b]), "x")
    part_a, part_b = lax.optimization_barrier((part_a, part_b))
    part_a = to_owners(sum_pieces(part_a), ("y_lo", "y_hi"))
    last = jnp.concatenate([total_of(jnp.stack(part_a)), total_of(jnp.stack(part_b))], axis=1)
    last = last.astype(jnp.bfloat16).reshape(2 * along_z, -1, LANES)
    small = (total_of(small) * inverse_count).astype(jnp.bfloat16)
    small = jnp.broadcast_to(small, (2 * along_z,) + small.shape)
    last = swap_pieces(jnp.concatenate([small, last], axis=1), around)
    return (grad_input, *finish(last, owned_rows, feat, hid, inverse_count))


def solution(mesh):
    x, z = 4, mesh.devices.size // 32
    split = Mesh(mesh.devices.reshape(2, x, z, 2, 2), ("y_lo", "x", "z", "y_hi", "core"))
    images = P(("y_lo", "x", "z", "y_hi", "core"))
    return jax.shard_map(
        per_device,
        mesh=split,
        in_specs=(images, images, images, P(), P(), P(), P(), P(), P()),
        out_specs=(images, images, P(), P(), P(), P(), P()),
        check_vma=False,
    )
```

```python
import functools

import jax
import jax.numpy as jnp
import numpy as np
from jax import lax
from jax.experimental import pallas as pl
from jax.experimental.pallas import tpu as pltpu
from jax.sharding import Mesh
from jax.sharding import PartitionSpec as P

LANES = 128
EDGE = 8
VMEM_LIMIT = 60 * 1024 * 1024
SMALL = pl.CostEstimate(flops=1000, bytes_accessed=1000, transcendentals=0)
SMALL_ROWS = 64


def hidden_grads(first, normed, b_ref, sums_ref, loads, weights, cots, grads, target, sems):
    parts, _, width = weights.shape
    stores = []
    for part in range(parts):
        for load in loads[part]:
            load.wait()
        pre_act = jnp.dot(normed[...], weights[part], preferred_element_type=jnp.float32)
        pre_act = pre_act + b_ref[:, pl.ds(pl.multiple_of(first + part * width, width), width)]
        slope = 0.5 * (1.0 + lax.erf(pre_act * 0.7071067811865476)) + pre_act * jnp.exp(
            -0.5 * pre_act * pre_act
        ) * 0.3989422804014327
        grad = (cots[part].astype(jnp.float32) * slope).astype(jnp.bfloat16)
        grads[part] = grad
        here = slice(part * width, (part + 1) * width)
        sums_ref[:, here] = jnp.sum(grad.astype(jnp.float32), axis=0, keepdims=True)
        stores.append(pltpu.make_async_copy(grads.at[part], target.at[:, here], sems.at[part]))
        stores[-1].start()
    return stores


def start_loads(first, w_hbm, cot_hbm, weights, cots, sems):
    parts, _, width = weights.shape
    loads = []
    for part in range(parts):
        columns = pl.ds(pl.multiple_of(first + part * width, width), width)
        loads.append(
            (
                pltpu.make_async_copy(w_hbm.at[:, columns], weights.at[part], sems.at[2 * part]),
                pltpu.make_async_copy(cot_hbm.at[0, :, columns], cots.at[part], sems.at[2 * part + 1]),
            )
        )
    for pair in loads:
        pair[0].start()
        pair[1].start()
    return loads


def near_kernel(
    core_ref, normed_ref, b_ref, w_hbm, cot_hbm, near_out, sums_ref, weights, cots, grads, in_sems, out_sems
):
    parts, _, width = weights.shape
    first = core_ref[0] * (parts * width)
    loads = start_loads(first, w_hbm, cot_hbm, weights, cots, in_sems)
    for copy in hidden_grads(first, normed_ref, b_ref, sums_ref, loads, weights, cots, grads, near_out, out_sems):
        copy.wait()


def near_half(core, normed, b_row, w_up, cot, parts=4):
    cells, feat = normed.shape
    hid = w_up.shape[1]
    width = hid // 2 // parts
    whole = pl.BlockSpec(memory_space=pltpu.VMEM)
    remain = pl.BlockSpec(memory_space=pl.ANY)
    return pl.pallas_call(
        near_kernel,
        name="near_half",
        in_specs=[pl.BlockSpec(memory_space=pltpu.SMEM), whole, whole, remain, remain],
        out_specs=[remain, whole],
        out_shape=(
            jax.ShapeDtypeStruct((cells, hid // 2), jnp.bfloat16),
            jax.ShapeDtypeStruct((1, hid // 2), jnp.float32),
        ),
        scratch_shapes=[
            pltpu.VMEM((parts, feat, width), jnp.bfloat16),
            pltpu.VMEM((parts, cells, width), jnp.bfloat16),
            pltpu.VMEM((parts, cells, width), jnp.bfloat16),
            pltpu.SemaphoreType.DMA((2 * parts,)),
            pltpu.SemaphoreType.DMA((parts,)),
        ],
        compiler_params=pltpu.CompilerParams(vmem_limit_bytes=VMEM_LIMIT),
        cost_estimate=SMALL,
    )(core, normed, b_row, w_up, cot)


def front_kernel(
    core_ref, image_ref, taps_ref, bias_ref, gain_ref, shift_ref, order_ref, b_ref, w_hbm, cot_hbm,
    unit_out, sigma_ref, turned_ref, normed_out, away_out, sums_ref,
    padded, conv, unit, normed, weights, cots, grads, in_sems, out_sems, grad_sems,
):
    side, feat = image_ref.shape[1], image_ref.shape[3]
    parts, _, width = weights.shape
    first_unit = (1 - core_ref[0]) * (parts * width)
    loads = start_loads(first_unit, w_hbm, cot_hbm, weights, cots, in_sems)

    blank = jnp.zeros((side, EDGE, LANES), jnp.float32)
    padded[:, 0:EDGE, :] = blank
    padded[:, EDGE + side : EDGE + side + EDGE, :] = blank

    @pl.loop(0, feat // LANES)
    def _(block):
        lanes = pl.ds(pl.multiple_of(block * LANES, LANES), LANES)
        padded[:, EDGE : EDGE + side, :] = image_ref[0, :, :, lanes].astype(jnp.float32)
        start = jnp.broadcast_to(bias_ref[lanes].reshape(1, LANES), (side, LANES))
        sums = [start] * side
        for tap_col in range(7):
            taps = [
                jnp.broadcast_to(taps_ref[pl.ds(7 * tap_row + tap_col, 1), lanes], (side, LANES))
                for tap_row in range(7)
            ]
            for source in range(side):
                cells = padded[source, EDGE - 3 + tap_col : EDGE - 3 + tap_col + side, :]
                for tap_row in range(7):
                    target = source + 3 - tap_row
                    if 0 <= target < side:
                        sums[target] = sums[target] + cells * taps[tap_row]
        for row in range(side):
            conv[row * side : (row + 1) * side, lanes] = sums[row]

    gain = gain_ref[...].reshape(1, feat)
    shift = shift_ref[...].reshape(1, feat)

    @pl.loop(0, side, unroll=4)
    def _(row):
        cells = pl.ds(pl.multiple_of(row * side, side), side)
        values = conv[cells, :]
        centred = values - jnp.mean(values, axis=-1, keepdims=True)
        inv_sigma = lax.rsqrt(jnp.mean(centred * centred, axis=-1, keepdims=True) + 1e-06)
        scaled = centred * inv_sigma
        unit[cells, :] = scaled
        sigma_ref[cells, :] = jnp.broadcast_to(inv_sigma, (side, LANES))
        normed[cells, :] = (scaled * gain + shift).astype(jnp.bfloat16)

    stores = [
        pltpu.make_async_copy(normed, normed_out, out_sems.at[0]),
        pltpu.make_async_copy(unit, unit_out, out_sems.at[1]),
    ]
    for copy in stores:
        copy.start()

    group = order_ref.shape[0]
    rows = turned_ref.shape[3]
    for index in range(feat // group):
        y_lo, pair = divmod(index, 2)
        turned = lax.dot_general(
            order_ref[...],
            normed[:, index * group : (index + 1) * group],
            (((1,), (1,)), ((), ())),
            preferred_element_type=jnp.float32,
        ).astype(jnp.bfloat16)
        for within in range(2):
            for y_hi in range(2):
                first = (within * 2 + y_hi) * rows
                turned_ref[2 * pair + within, y_hi, y_lo] = turned[first : first + rows]

    stores += hidden_grads(
        first_unit, normed, b_ref, sums_ref, loads, weights, cots, grads, away_out, grad_sems
    )
    for copy in stores:
        copy.wait()


def channel_order(rows, along_z):
    width = 4 * rows
    owned = rows // along_z
    target = np.arange(width).reshape(2, along_z, 2, owned).transpose(0, 2, 1, 3).reshape(-1)
    return jnp.asarray(np.eye(width, dtype=np.float32)[target], jnp.bfloat16)


def front(core, image, taps, bias, gain, shift, w_up, b_row, cot, along_z, parts=2):
    side, feat = image.shape[1], image.shape[3]
    cells = side * side
    hid = w_up.shape[1]
    rows = feat // 16
    width = hid // 2 // parts
    whole = pl.BlockSpec(memory_space=pltpu.VMEM)
    remain = pl.BlockSpec(memory_space=pl.ANY)
    return pl.pallas_call(
        front_kernel,
        name="front",
        in_specs=[pl.BlockSpec(memory_space=pltpu.SMEM)] + [whole] * 7 + [remain] * 2,
        out_specs=[remain, whole, whole, remain, remain, whole],
        out_shape=(
            jax.ShapeDtypeStruct((cells, feat), jnp.float32),
            jax.ShapeDtypeStruct((cells, LANES), jnp.float32),
            jax.ShapeDtypeStruct((4, 2, 2, rows, cells), jnp.bfloat16),
            jax.ShapeDtypeStruct((cells, feat), jnp.bfloat16),
            jax.ShapeDtypeStruct((cells, hid // 2), jnp.bfloat16),
            jax.ShapeDtypeStruct((1, hid // 2), jnp.float32),
        ),
        scratch_shapes=[
            pltpu.VMEM((side, side + 2 * EDGE, LANES), jnp.float32),
            pltpu.VMEM((cells, feat), jnp.float32),
            pltpu.VMEM((cells, feat), jnp.float32),
            pltpu.VMEM((cells, feat), jnp.bfloat16),
            pltpu.VMEM((parts, feat, width), jnp.bfloat16),
            pltpu.VMEM((parts, cells, width), jnp.bfloat16),
            pltpu.VMEM((parts, cells, width), jnp.bfloat16),
            pltpu.SemaphoreType.DMA((2 * parts,)),
            pltpu.SemaphoreType.DMA((2,)),
            pltpu.SemaphoreType.DMA((parts,)),
        ],
        compiler_params=pltpu.CompilerParams(vmem_limit_bytes=VMEM_LIMIT),
        cost_estimate=SMALL,
    )(core, image, taps, bias, gain, shift, channel_order(rows, along_z), b_row, w_up, cot)


def product_kernel(place_ref, near_t_ref, far_t_ref, near_ref, far_ref, *refs):
    out_refs, pieces, sems = refs[:5], refs[5], refs[6]
    _, along_y, rows, cells = near_t_ref.shape
    block = (
        jnp.dot(near_t_ref[...].reshape(along_y * rows, cells), near_ref[...], preferred_element_type=jnp.float32)
        + jnp.dot(far_t_ref[...].reshape(along_y * rows, cells), far_ref[...], preferred_element_type=jnp.float32)
    ).astype(jnp.bfloat16)
    columns = out_refs[0].shape[2]
    out_refs[4][...] = block[:, columns:].reshape(out_refs[4].shape)
    step = pl.program_id(0)
    for y in range(along_y):
        pieces[step, lax.rem(y - place_ref[1] + 4, 4)] = block[y * rows : (y + 1) * rows, :columns]
    copies = [pltpu.make_async_copy(pieces.at[i], out_refs[i], sems.at[i]) for i in range(4)]
    for i in range(4):

        @pl.when(step == i)
        def _():
            copies[i].start()

    @pl.when(step == 3)
    def _():
        for copy in copies:
            copy.wait()


def product(place, near_t, far_t, near, far, columns):
    _, _, rows, cells = near_t.shape
    others = near.shape[1] - columns
    left = pl.BlockSpec((1, 4, rows, cells), lambda i, p: (lax.rem(p[0] + i, 4), 0, 0, 0))
    right = pl.BlockSpec((cells, near.shape[1]), lambda i, p: (0, 0))
    return pl.pallas_call(
        product_kernel,
        name="product",
        grid_spec=pltpu.PrefetchScalarGridSpec(
            num_scalar_prefetch=1,
            grid=(4,),
            in_specs=[left, left, right, right],
            out_specs=[pl.BlockSpec(memory_space=pl.ANY)] * 4
            + [pl.BlockSpec((4, 1, rows, others), lambda i, p: (0, i, 0, 0))],
            scratch_shapes=[pltpu.VMEM((4, 4, rows, columns), jnp.bfloat16), pltpu.SemaphoreType.DMA((4,))],
        ),
        out_shape=[jax.ShapeDtypeStruct((4, rows, columns), jnp.bfloat16)] * 4
        + [jax.ShapeDtypeStruct((4, 4, rows, others), jnp.bfloat16)],
        compiler_params=pltpu.CompilerParams(vmem_limit_bytes=VMEM_LIMIT),
        cost_estimate=SMALL,
    )(place, near_t, far_t, near, far)


def sum_kernel(*refs):
    ins, outs = refs[:-4], refs[-4:]
    for index in range(4):
        if len(ins) == 1:
            parts = [ins[0][source, index] for source in range(4)]
        else:
            parts = [ref[index] for ref in ins]
        total = parts[0].astype(jnp.float32)
        for part in parts[1:]:
            total = total + part.astype(jnp.float32)
        outs[index][...] = total.astype(jnp.bfloat16)


def sum_pieces(pieces):
    rows, columns = pieces[0].shape[-2:]
    return pl.pallas_call(
        sum_kernel,
        name="sum_pieces",
        out_shape=[jax.ShapeDtypeStruct((rows, columns), jnp.bfloat16)] * 4,
        compiler_params=pltpu.CompilerParams(vmem_limit_bytes=VMEM_LIMIT),
        cost_estimate=SMALL,
    )(*pieces)


def to_owners(pieces, axes):
    named = range(4) if axes == "x" else [0, 2, 1, 3]
    moved = [
        lax.ppermute(piece, axes, [(named[i], named[(i + d) % 4]) for i in range(4)])
        for d, piece in enumerate(pieces)
        if d
    ]
    return [pieces[0]] + moved


def back_kernel(
    core_ref, away_ref, near_ref, sigma_ref, gain_ref, near_sum_ref, away_sum_ref, image_ref, res_ref, taps_ref,
    unit_hbm, w_hbm, out_ref, sums_ref, weights, unit, total, norm_sums, padded, image, small, sems,
):
    side = image_ref.shape[1]
    feat = total.shape[1]

    @pl.when(pl.program_id(0) == 0)
    def _():
        parts, _, width = weights.shape
        half = parts // 2
        core = core_ref[0]
        loads = []
        for part in range(parts):
            owner = 1 - core if part < half else core
            columns = pl.ds(pl.multiple_of((owner * half + part % half) * width, width), width)
            loads.append(pltpu.make_async_copy(w_hbm.at[:, columns], weights.at[part], sems.at[part]))
        loads.append(pltpu.make_async_copy(unit_hbm, unit, sems.at[parts]))
        for load in loads:
            load.start()
        blank = jnp.zeros((side, EDGE, LANES), jnp.float32)
        padded[:, 0:EDGE, :] = blank
        padded[:, EDGE + side : EDGE + side + EDGE, :] = blank
        for part in range(parts):
            loads[part].wait()
            grad_ref = away_ref if part < half else near_ref
            grad = grad_ref[:, (part % half) * width : (part % half + 1) * width]
            value = lax.dot_general(
                grad, weights[part], (((1,), (1,)), ((), ())), preferred_element_type=jnp.float32
            )
            if part:
                total[...] += value
            else:
                total[...] = value
        loads[parts].wait()
        gain = gain_ref[...].reshape(1, feat)

        def finish(row, carry):
            gain_sum, shift_sum = carry
            cells = pl.ds(pl.multiple_of(row * 32, 32), 32)
            grad = total[cells, :]
            scaled = unit[cells, :]
            gain_sum = gain_sum + jnp.sum((grad * scaled).reshape(4, 8, feat), axis=0)
            shift_sum = shift_sum + jnp.sum(grad.reshape(4, 8, feat), axis=0)
            unit_grad = grad * gain
            first = jnp.sum(unit_grad, axis=-1, keepdims=True) * (1.0 / feat)
            second = jnp.sum(unit_grad * scaled, axis=-1, keepdims=True) * (1.0 / feat)
            total[cells, :] = sigma_ref[cells, 0:1] * (unit_grad - first - scaled * second)
            return gain_sum, shift_sum

        zero = jnp.zeros((8, feat), jnp.float32)
        gain_sum, shift_sum = lax.fori_loop(0, total.shape[0] // 32, finish, (zero, zero))
        norm_sums[0:1, :] = jnp.sum(gain_sum, axis=0, keepdims=True)
        norm_sums[1:2, :] = jnp.sum(shift_sum, axis=0, keepdims=True)

    lanes = pl.ds(pl.multiple_of(pl.program_id(0) * LANES, LANES), LANES)
    image[...] = image_ref[0].astype(jnp.float32)
    bias_sum = jnp.zeros((side, LANES), jnp.float32)
    for row in range(side):
        cells = total[row * side : (row + 1) * side, lanes]
        padded[row, EDGE : EDGE + side, :] = cells
        bias_sum = bias_sum + cells
    tap_sums = [None] * 49
    sums = [res_ref[0, row].astype(jnp.float32) for row in range(side)]
    for turn_col in range(7):
        weights_here = [
            jnp.broadcast_to(taps_ref[pl.ds(7 * (6 - turn_row) + 6 - turn_col, 1), :], (side, LANES))
            for turn_row in range(7)
        ]
        parts_here = [jnp.zeros((8, LANES), jnp.float32) for _ in range(7)]
        for source in range(side):
            cells = padded[source, EDGE - 3 + turn_col : EDGE - 3 + turn_col + side, :]
            for turn_row in range(7):
                target = source + 3 - turn_row
                if 0 <= target < side:
                    sums[target] = sums[target] + cells * weights_here[turn_row]
                    product = cells * image[target]
                    parts_here[turn_row] = parts_here[turn_row] + (product[:8] + product[8:])
        for turn_row in range(7):
            tap = 7 * (6 - turn_row) + 6 - turn_col
            small[tap : tap + 1, :] = jnp.sum(parts_here[turn_row], axis=0, keepdims=True)
    small[49:51, :] = norm_sums[0:2, lanes]
    small[51:52, :] = jnp.sum(bias_sum, axis=0, keepdims=True)
    small[52:53, :] = jnp.where(core_ref[0] == 0, near_sum_ref[...], away_sum_ref[...])
    small[53:54, :] = jnp.where(core_ref[0] == 0, away_sum_ref[...], near_sum_ref[...])
    small[54:, :] = jnp.zeros((SMALL_ROWS - 54, LANES), jnp.float32)
    sums_ref[0] = small[...].astype(jnp.bfloat16)
    for row in range(side):
        out_ref[0, row] = sums[row].astype(jnp.bfloat16)


def back(core, away, near, w_up, unit, sigma, gain, near_sums, away_sums, image, residual, taps, parts=4):
    cells, feat = unit.shape
    side = image.shape[1]
    width = w_up.shape[1] // parts
    whole = pl.BlockSpec(memory_space=pltpu.VMEM)
    remain = pl.BlockSpec(memory_space=pl.ANY)
    picture = pl.BlockSpec((1, side, side, LANES), lambda i: (0, 0, 0, i))
    return pl.pallas_call(
        back_kernel,
        name="back",
        grid=(feat // LANES,),
        in_specs=[pl.BlockSpec(memory_space=pltpu.SMEM)]
        + [whole] * 4
        + [
            pl.BlockSpec((1, LANES), lambda i: (0, i)),
            pl.BlockSpec((1, LANES), lambda i: (0, i)),
            picture,
            picture,
            pl.BlockSpec((49, LANES), lambda i: (0, i)),
            remain,
            remain,
        ],
        out_specs=[picture, pl.BlockSpec((1, SMALL_ROWS, LANES), lambda i: (i, 0, 0))],
        out_shape=(
            jax.ShapeDtypeStruct(image.shape, jnp.bfloat16),
            jax.ShapeDtypeStruct((feat // LANES, SMALL_ROWS, LANES), jnp.bfloat16),
        ),
        scratch_shapes=[
            pltpu.VMEM((parts, feat, width), jnp.bfloat16),
            pltpu.VMEM((cells, feat), jnp.float32),
            pltpu.VMEM((cells, feat), jnp.float32),
            pltpu.VMEM((8, feat), jnp.float32),
            pltpu.VMEM((side, side + 2 * EDGE, LANES), jnp.float32),
            pltpu.VMEM((side, side, LANES), jnp.float32),
            pltpu.VMEM((SMALL_ROWS, LANES), jnp.float32),
            pltpu.SemaphoreType.DMA((1 + parts,)),
        ],
        compiler_params=pltpu.CompilerParams(vmem_limit_bytes=VMEM_LIMIT),
        cost_estimate=SMALL,
    )(core, away, near, sigma, gain, near_sums, away_sums, image, residual, taps, unit, w_up)


def finish_kernel(inverse_count, received_ref, owned_ref, up_ref, gain_ref, shift_ref, taps_ref, bias_ref):
    pieces, height, _ = received_ref.shape
    owned_rows, hid = owned_ref.shape
    blocks = hid // 2 // LANES
    share = height - owned_rows * blocks
    for core in range(2):
        total = received_ref[core, share:, :].astype(jnp.float32)
        for z in range(1, pieces // 2):
            total = total + received_ref[2 * z + core, share:, :].astype(jnp.float32)
        total = total * inverse_count
        for row in range(owned_rows):
            for block in range(blocks):
                first = (core * blocks + block) * LANES
                index = row * blocks + block
                owned_ref[row : row + 1, first : first + LANES] = total[index : index + 1]
    feat = gain_ref.shape[0]
    for block in range(feat // LANES):
        parts = []
        row, end = block * SMALL_ROWS, (block + 1) * SMALL_ROWS
        while row < end:
            stop = min(end, (row // share + 1) * share)
            first = row % share
            parts.append(received_ref[row // share, first : first + stop - row, :].astype(jnp.float32))
            row = stop
        values = jnp.concatenate(parts, axis=0)
        lanes = slice(block * LANES, (block + 1) * LANES)
        taps_ref[:, lanes] = values[:49]
        gain_ref[lanes] = values[49]
        shift_ref[lanes] = values[50]
        bias_ref[lanes] = values[51]
        up_ref[lanes] = values[52]
        up_ref[feat + block * LANES : feat + (block + 1) * LANES] = values[53]


def finish(received, owned_rows, feat, hid, inverse_count):
    row = jax.ShapeDtypeStruct((feat,), jnp.float32)
    return pl.pallas_call(
        functools.partial(finish_kernel, inverse_count),
        name="finish",
        out_shape=(
            jax.ShapeDtypeStruct((owned_rows, hid), jnp.float32),
            jax.ShapeDtypeStruct((hid,), jnp.float32),
            row,
            row,
            jax.ShapeDtypeStruct((49, feat), jnp.float32),
            row,
        ),
        compiler_params=pltpu.CompilerParams(vmem_limit_bytes=VMEM_LIMIT),
        cost_estimate=SMALL,
    )(received)


def swap_pieces(values, axes):
    return lax.all_to_all(values, axes, 0, 0, tiled=True)


def total_of(received):
    return jnp.sum(received.astype(jnp.float32), axis=0)


def per_device(images, hidden_cot, residual_cot, w_up, b_up, ln_gain, ln_bias, dw_weight, dw_bias):
    feat, hid = w_up.shape
    plane = ("x", "y_hi", "y_lo")
    along_z = lax.axis_size("z")
    owned_rows = feat // (32 * along_z)
    inverse_count = 1.0 / (images.shape[0] * 32 * along_z)
    mine = lax.axis_index("core").astype(jnp.int32).reshape(1)
    y_index = 2 * lax.axis_index("y_hi") + lax.axis_index("y_lo")
    place = jnp.stack([lax.axis_index("x"), y_index]).astype(jnp.int32)
    swap = [(0, 1), (1, 0)]

    b_row = b_up.reshape(1, -1)
    unit, sigma, turned, normed, away, away_sums = front(
        mine, images, dw_weight, dw_bias, ln_gain, ln_bias, w_up, b_row, hidden_cot, along_z
    )
    far_turned = lax.ppermute(turned, "core", swap)
    far = lax.ppermute(away, "core", swap)
    near, near_sums = near_half(mine, normed, b_row, w_up, hidden_cot)
    cells = unit.shape[0]
    *part_a, part_b = product(
        place, turned.reshape(4, 4, -1, cells), far_turned.reshape(4, 4, -1, cells), near, far, 7 * hid // 24
    )
    part_b, unit = lax.optimization_barrier((part_b, unit))
    part_a = to_owners(part_a, "x")
    part_b = swap_pieces(part_b, ("y_hi", "y_lo"))

    grad_input, small = back(
        mine, away, near, w_up, unit, sigma, ln_gain, near_sums, away_sums, images, residual_cot, dw_weight
    )
    part_b, small = lax.optimization_barrier((part_b, small))

    around = ("z", "core")
    small = swap_pieces(small.reshape(2 * along_z, -1, LANES), around)
    small = total_of(small).astype(jnp.bfloat16)
    part_b = to_owners(sum_pieces([part_b]), "x")
    part_a, small = lax.optimization_barrier((part_a, small))
    part_b, small = lax.optimization_barrier((part_b, small))
    small = swap_pieces(jnp.broadcast_to(small, (16,) + small.shape), plane)
    part_a = to_owners(sum_pieces(part_a), ("y_lo", "y_hi"))
    last = jnp.concatenate([total_of(jnp.stack(part_a)), total_of(jnp.stack(part_b))], axis=1)
    last = last.astype(jnp.bfloat16).reshape(2 * along_z, -1, LANES)
    small = (total_of(small) * inverse_count).astype(jnp.bfloat16)
    small = jnp.broadcast_to(small, (2 * along_z,) + small.shape)
    last = swap_pieces(jnp.concatenate([small, last], axis=1), around)
    return (grad_input, *finish(last, owned_rows, feat, hid, inverse_count))


def solution(mesh):
    x, z = 4, mesh.devices.size // 32
    split = Mesh(mesh.devices.reshape(2, x, z, 2, 2), ("y_lo", "x", "z", "y_hi", "core"))
    images = P(("y_lo", "x", "z", "y_hi", "core"))
    return jax.shard_map(
        per_device,
        mesh=split,
        in_specs=(images, images, images, P(), P(), P(), P(), P(), P()),
        out_specs=(images, images, P(), P(), P(), P(), P()),
        check_vma=False,
    )
```

```python
import functools

import jax
import jax.numpy as jnp
import numpy as np
from jax import lax
from jax.experimental import pallas as pl
from jax.experimental.pallas import tpu as pltpu
from jax.sharding import Mesh
from jax.sharding import PartitionSpec as P

LANES = 128
EDGE = 8
VMEM_LIMIT = 60 * 1024 * 1024
SMALL = pl.CostEstimate(flops=1000, bytes_accessed=1000, transcendentals=0)
SMALL_ROWS = 64


def front_kernel(
    core_ref, image_ref, taps_ref, bias_ref, gain_ref, shift_ref, order_ref, b_ref, w_hbm, cot_hbm,
    unit_out, sigma_ref, turned_ref, away_out, near_out, sums_ref,
    padded, conv, unit, normed, weights, cots, grads, in_sems, out_sems,
):
    side, feat = image_ref.shape[1], image_ref.shape[3]
    parts, _, width = weights.shape
    half = parts // 2
    core = core_ref[0]

    def column(part):
        owner = 1 - core if part < half else core
        return pl.multiple_of((owner * half + part % half) * width, width)

    loads = []
    for part in range(parts):
        columns = pl.ds(column(part), width)
        loads.append(
            (
                pltpu.make_async_copy(w_hbm.at[:, columns], weights.at[part], in_sems.at[2 * part]),
                pltpu.make_async_copy(cot_hbm.at[0, :, columns], cots.at[part], in_sems.at[2 * part + 1]),
            )
        )
    for pair in loads:
        pair[0].start()
        pair[1].start()

    blank = jnp.zeros((side, EDGE, LANES), jnp.float32)
    padded[:, 0:EDGE, :] = blank
    padded[:, EDGE + side : EDGE + side + EDGE, :] = blank

    @pl.loop(0, feat // LANES)
    def _(block):
        lanes = pl.ds(pl.multiple_of(block * LANES, LANES), LANES)
        padded[:, EDGE : EDGE + side, :] = image_ref[0, :, :, lanes].astype(jnp.float32)
        start = jnp.broadcast_to(bias_ref[lanes].reshape(1, LANES), (side, LANES))
        sums = [start] * side
        for tap_col in range(7):
            taps = [
                jnp.broadcast_to(taps_ref[pl.ds(7 * tap_row + tap_col, 1), lanes], (side, LANES))
                for tap_row in range(7)
            ]
            for source in range(side):
                cells = padded[source, EDGE - 3 + tap_col : EDGE - 3 + tap_col + side, :]
                for tap_row in range(7):
                    target = source + 3 - tap_row
                    if 0 <= target < side:
                        sums[target] = sums[target] + cells * taps[tap_row]
        for row in range(side):
            conv[row * side : (row + 1) * side, lanes] = sums[row]

    gain = gain_ref[...].reshape(1, feat)
    shift = shift_ref[...].reshape(1, feat)

    @pl.loop(0, side, unroll=4)
    def _(row):
        cells = pl.ds(pl.multiple_of(row * side, side), side)
        values = conv[cells, :]
        centred = values - jnp.mean(values, axis=-1, keepdims=True)
        inv_sigma = lax.rsqrt(jnp.mean(centred * centred, axis=-1, keepdims=True) + 1e-06)
        scaled = centred * inv_sigma
        unit[cells, :] = scaled
        sigma_ref[cells, :] = jnp.broadcast_to(inv_sigma, (side, LANES))
        normed[cells, :] = (scaled * gain + shift).astype(jnp.bfloat16)

    unit_copy = pltpu.make_async_copy(unit, unit_out, out_sems.at[0])
    unit_copy.start()

    group = order_ref.shape[0]
    rows = turned_ref.shape[3]
    for index in range(feat // group):
        y_lo, pair = divmod(index, 2)
        turned = lax.dot_general(
            order_ref[...],
            normed[:, index * group : (index + 1) * group],
            (((1,), (1,)), ((), ())),
            preferred_element_type=jnp.float32,
        ).astype(jnp.bfloat16)
        for within in range(2):
            for y_hi in range(2):
                first = (within * 2 + y_hi) * rows
                turned_ref[2 * pair + within, y_hi, y_lo] = turned[first : first + rows]

    stores = [unit_copy]
    for part in range(parts):
        loads[part][0].wait()
        loads[part][1].wait()
        columns = pl.ds(column(part), width)
        pre_act = jnp.dot(normed[...], weights[part], preferred_element_type=jnp.float32)
        pre_act = pre_act + b_ref[:, columns]
        slope = 0.5 * (1.0 + lax.erf(pre_act * 0.7071067811865476)) + pre_act * jnp.exp(
            -0.5 * pre_act * pre_act
        ) * 0.3989422804014327
        grad = (cots[part].astype(jnp.float32) * slope).astype(jnp.bfloat16)
        grads[part] = grad
        sums_ref[:, columns] = jnp.sum(grad.astype(jnp.float32), axis=0, keepdims=True)
        target = away_out if part < half else near_out
        copy = pltpu.make_async_copy(
            grads.at[part], target.at[:, (part % half) * width : (part % half + 1) * width], out_sems.at[1 + part]
        )
        copy.start()
        stores.append(copy)
    for copy in stores:
        copy.wait()


def channel_order(rows, along_z):
    width = 4 * rows
    owned = rows // along_z
    target = np.arange(width).reshape(2, along_z, 2, owned).transpose(0, 2, 1, 3).reshape(-1)
    return jnp.asarray(np.eye(width, dtype=np.float32)[target], jnp.bfloat16)


def front(core, image, taps, bias, gain, shift, w_up, b_row, cot, along_z, parts=4):
    side, feat = image.shape[1], image.shape[3]
    cells = side * side
    hid = w_up.shape[1]
    rows = feat // 16
    width = hid // parts
    whole = pl.BlockSpec(memory_space=pltpu.VMEM)
    remain = pl.BlockSpec(memory_space=pl.ANY)
    return pl.pallas_call(
        front_kernel,
        name="front",
        in_specs=[pl.BlockSpec(memory_space=pltpu.SMEM)] + [whole] * 7 + [remain] * 2,
        out_specs=[remain, whole, whole, remain, remain, whole],
        out_shape=(
            jax.ShapeDtypeStruct((cells, feat), jnp.float32),
            jax.ShapeDtypeStruct((cells, LANES), jnp.float32),
            jax.ShapeDtypeStruct((4, 2, 2, rows, cells), jnp.bfloat16),
            jax.ShapeDtypeStruct((cells, hid // 2), jnp.bfloat16),
            jax.ShapeDtypeStruct((cells, hid // 2), jnp.bfloat16),
            jax.ShapeDtypeStruct((1, hid), jnp.float32),
        ),
        scratch_shapes=[
            pltpu.VMEM((side, side + 2 * EDGE, LANES), jnp.float32),
            pltpu.VMEM((cells, feat), jnp.float32),
            pltpu.VMEM((cells, feat), jnp.float32),
            pltpu.VMEM((cells, feat), jnp.bfloat16),
            pltpu.VMEM((parts, feat, width), jnp.bfloat16),
            pltpu.VMEM((parts, cells, width), jnp.bfloat16),
            pltpu.VMEM((parts, cells, width), jnp.bfloat16),
            pltpu.SemaphoreType.DMA((2 * parts,)),
            pltpu.SemaphoreType.DMA((1 + parts,)),
        ],
        compiler_params=pltpu.CompilerParams(vmem_limit_bytes=VMEM_LIMIT),
        cost_estimate=SMALL,
    )(core, image, taps, bias, gain, shift, channel_order(rows, along_z), b_row, w_up, cot)


def product_kernel(place_ref, near_t_ref, far_t_ref, near_ref, far_ref, *refs):
    out_refs, pieces, others, sems = refs[:5], refs[5], refs[6], refs[7]
    _, along_y, rows, cells = near_t_ref.shape
    columns = pieces.shape[3]
    copies = []
    for step in range(4):
        x = lax.rem(place_ref[0] + step, 4)
        near_t = near_t_ref[x].reshape(along_y * rows, cells)
        far_t = far_t_ref[x].reshape(along_y * rows, cells)
        block = (
            jnp.dot(near_t, near_ref[...], preferred_element_type=jnp.float32)
            + jnp.dot(far_t, far_ref[...], preferred_element_type=jnp.float32)
        ).astype(jnp.bfloat16)
        for y in range(along_y):
            part = block[y * rows : (y + 1) * rows]
            pieces[step, lax.rem(y - place_ref[1] + 4, 4)] = part[:, :columns]
            others[y, step] = part[:, columns:]
        copies.append(pltpu.make_async_copy(pieces.at[step], out_refs[step], sems.at[step]))
        copies.append(pltpu.make_async_copy(others.at[:, step], out_refs[4].at[:, step], sems.at[4 + step]))
        for copy in copies[-2:]:
            copy.start()
    for copy in copies:
        copy.wait()


def product(place, near_t, far_t, near, far, columns):
    _, _, rows, cells = near_t.shape
    rest = near.shape[1] - columns
    whole = pl.BlockSpec(memory_space=pltpu.VMEM)
    return pl.pallas_call(
        product_kernel,
        name="product",
        in_specs=[pl.BlockSpec(memory_space=pltpu.SMEM)] + [whole] * 4,
        out_specs=[pl.BlockSpec(memory_space=pl.ANY)] * 5,
        out_shape=[jax.ShapeDtypeStruct((4, rows, columns), jnp.bfloat16)] * 4
        + [jax.ShapeDtypeStruct((4, 4, rows, rest), jnp.bfloat16)],
        scratch_shapes=[
            pltpu.VMEM((4, 4, rows, columns), jnp.bfloat16),
            pltpu.VMEM((4, 4, rows, rest), jnp.bfloat16),
            pltpu.SemaphoreType.DMA((8,)),
        ],
        compiler_params=pltpu.CompilerParams(vmem_limit_bytes=VMEM_LIMIT),
        cost_estimate=SMALL,
    )(place, near_t, far_t, near, far)


def sum_kernel(*refs):
    ins, outs = refs[:-4], refs[-4:]
    for index in range(4):
        if len(ins) == 1:
            parts = [ins[0][source, index] for source in range(4)]
        else:
            parts = [ref[index] for ref in ins]
        total = parts[0].astype(jnp.float32)
        for part in parts[1:]:
            total = total + part.astype(jnp.float32)
        outs[index][...] = total.astype(jnp.bfloat16)


def sum_pieces(pieces):
    rows, columns = pieces[0].shape[-2:]
    return pl.pallas_call(
        sum_kernel,
        name="sum_pieces",
        out_shape=[jax.ShapeDtypeStruct((rows, columns), jnp.bfloat16)] * 4,
        compiler_params=pltpu.CompilerParams(vmem_limit_bytes=VMEM_LIMIT),
        cost_estimate=SMALL,
    )(*pieces)


def to_owners(pieces, axes):
    named = range(4) if axes == "x" else [0, 2, 1, 3]
    moved = [
        lax.ppermute(piece, axes, [(named[i], named[(i + d) % 4]) for i in range(4)])
        for d, piece in enumerate(pieces)
        if d
    ]
    return [pieces[0]] + moved


def back_kernel(
    core_ref, away_ref, near_ref, sigma_ref, gain_ref, up_first_ref, up_second_ref, image_ref, res_ref, taps_ref,
    unit_hbm, w_hbm, out_ref, sums_ref, weights, unit, total, norm_sums, padded, image, small, sems,
):
    side = image_ref.shape[1]
    feat = total.shape[1]

    @pl.when(pl.program_id(0) == 0)
    def _():
        parts, _, width = weights.shape
        half = parts // 2
        core = core_ref[0]
        loads = []
        for part in range(parts):
            owner = 1 - core if part < half else core
            columns = pl.ds(pl.multiple_of((owner * half + part % half) * width, width), width)
            loads.append(pltpu.make_async_copy(w_hbm.at[:, columns], weights.at[part], sems.at[part]))
        loads.append(pltpu.make_async_copy(unit_hbm, unit, sems.at[parts]))
        for load in loads:
            load.start()
        blank = jnp.zeros((side, EDGE, LANES), jnp.float32)
        padded[:, 0:EDGE, :] = blank
        padded[:, EDGE + side : EDGE + side + EDGE, :] = blank
        for part in range(parts):
            loads[part].wait()
            grad_ref = away_ref if part < half else near_ref
            grad = grad_ref[:, (part % half) * width : (part % half + 1) * width]
            value = lax.dot_general(
                grad, weights[part], (((1,), (1,)), ((), ())), preferred_element_type=jnp.float32
            )
            if part:
                total[...] += value
            else:
                total[...] = value
        loads[parts].wait()
        gain = gain_ref[...].reshape(1, feat)

        def finish(row, carry):
            gain_sum, shift_sum = carry
            cells = pl.ds(pl.multiple_of(row * 32, 32), 32)
            grad = total[cells, :]
            scaled = unit[cells, :]
            gain_sum = gain_sum + jnp.sum((grad * scaled).reshape(4, 8, feat), axis=0)
            shift_sum = shift_sum + jnp.sum(grad.reshape(4, 8, feat), axis=0)
            unit_grad = grad * gain
            first = jnp.sum(unit_grad, axis=-1, keepdims=True) * (1.0 / feat)
            second = jnp.sum(unit_grad * scaled, axis=-1, keepdims=True) * (1.0 / feat)
            total[cells, :] = sigma_ref[cells, 0:1] * (unit_grad - first - scaled * second)
            return gain_sum, shift_sum

        zero = jnp.zeros((8, feat), jnp.float32)
        gain_sum, shift_sum = lax.fori_loop(0, total.shape[0] // 32, finish, (zero, zero))
        norm_sums[0:1, :] = jnp.sum(gain_sum, axis=0, keepdims=True)
        norm_sums[1:2, :] = jnp.sum(shift_sum, axis=0, keepdims=True)

    lanes = pl.ds(pl.multiple_of(pl.program_id(0) * LANES, LANES), LANES)
    image[...] = image_ref[0].astype(jnp.float32)
    bias_sum = jnp.zeros((side, LANES), jnp.float32)
    for row in range(side):
        cells = total[row * side : (row + 1) * side, lanes]
        padded[row, EDGE : EDGE + side, :] = cells
        bias_sum = bias_sum + cells
    tap_sums = [None] * 49
    sums = [res_ref[0, row].astype(jnp.float32) for row in range(side)]
    for turn_col in range(7):
        weights_here = [
            jnp.broadcast_to(taps_ref[pl.ds(7 * (6 - turn_row) + 6 - turn_col, 1), :], (side, LANES))
            for turn_row in range(7)
        ]
        parts_here = [jnp.zeros((8, LANES), jnp.float32) for _ in range(7)]
        for source in range(side):
            cells = padded[source, EDGE - 3 + turn_col : EDGE - 3 + turn_col + side, :]
            for turn_row in range(7):
                target = source + 3 - turn_row
                if 0 <= target < side:
                    sums[target] = sums[target] + cells * weights_here[turn_row]
                    product = cells * image[target]
                    parts_here[turn_row] = parts_here[turn_row] + (product[:8] + product[8:])
        for turn_row in range(7):
            tap = 7 * (6 - turn_row) + 6 - turn_col
            small[tap : tap + 1, :] = jnp.sum(parts_here[turn_row], axis=0, keepdims=True)
    small[49:51, :] = norm_sums[0:2, lanes]
    small[51:52, :] = jnp.sum(bias_sum, axis=0, keepdims=True)
    small[52:53, :] = up_first_ref[...]
    small[53:54, :] = up_second_ref[...]
    small[54:, :] = jnp.zeros((SMALL_ROWS - 54, LANES), jnp.float32)
    sums_ref[0] = small[...].astype(jnp.bfloat16)
    for row in range(side):
        out_ref[0, row] = sums[row].astype(jnp.bfloat16)


def back(core, away, near, w_up, unit, sigma, gain, up_sums, image, residual, taps, parts=4):
    cells, feat = unit.shape
    side = image.shape[1]
    width = w_up.shape[1] // parts
    whole = pl.BlockSpec(memory_space=pltpu.VMEM)
    remain = pl.BlockSpec(memory_space=pl.ANY)
    picture = pl.BlockSpec((1, side, side, LANES), lambda i: (0, 0, 0, i))
    return pl.pallas_call(
        back_kernel,
        name="back",
        grid=(feat // LANES,),
        in_specs=[pl.BlockSpec(memory_space=pltpu.SMEM)]
        + [whole] * 4
        + [
            pl.BlockSpec((1, LANES), lambda i: (0, i)),
            pl.BlockSpec((1, LANES), lambda i: (0, i + feat // LANES)),
            picture,
            picture,
            pl.BlockSpec((49, LANES), lambda i: (0, i)),
            remain,
            remain,
        ],
        out_specs=[picture, pl.BlockSpec((1, SMALL_ROWS, LANES), lambda i: (i, 0, 0))],
        out_shape=(
            jax.ShapeDtypeStruct(image.shape, jnp.bfloat16),
            jax.ShapeDtypeStruct((feat // LANES, SMALL_ROWS, LANES), jnp.bfloat16),
        ),
        scratch_shapes=[
            pltpu.VMEM((parts, feat, width), jnp.bfloat16),
            pltpu.VMEM((cells, feat), jnp.float32),
            pltpu.VMEM((cells, feat), jnp.float32),
            pltpu.VMEM((8, feat), jnp.float32),
            pltpu.VMEM((side, side + 2 * EDGE, LANES), jnp.float32),
            pltpu.VMEM((side, side, LANES), jnp.float32),
            pltpu.VMEM((SMALL_ROWS, LANES), jnp.float32),
            pltpu.SemaphoreType.DMA((1 + parts,)),
        ],
        compiler_params=pltpu.CompilerParams(vmem_limit_bytes=VMEM_LIMIT),
        cost_estimate=SMALL,
    )(core, away, near, sigma, gain, up_sums, up_sums, image, residual, taps, unit, w_up)


def finish_kernel(inverse_count, received_ref, owned_ref, up_ref, gain_ref, shift_ref, taps_ref, bias_ref):
    pieces, height, _ = received_ref.shape
    owned_rows, hid = owned_ref.shape
    blocks = hid // 2 // LANES
    share = height - owned_rows * blocks
    for core in range(2):
        total = received_ref[core, share:, :].astype(jnp.float32)
        for z in range(1, pieces // 2):
            total = total + received_ref[2 * z + core, share:, :].astype(jnp.float32)
        total = total * inverse_count
        for row in range(owned_rows):
            for block in range(blocks):
                first = (core * blocks + block) * LANES
                index = row * blocks + block
                owned_ref[row : row + 1, first : first + LANES] = total[index : index + 1]
    feat = gain_ref.shape[0]
    for block in range(feat // LANES):
        parts = []
        row, end = block * SMALL_ROWS, (block + 1) * SMALL_ROWS
        while row < end:
            stop = min(end, (row // share + 1) * share)
            first = row % share
            parts.append(received_ref[row // share, first : first + stop - row, :].astype(jnp.float32))
            row = stop
        values = jnp.concatenate(parts, axis=0)
        lanes = slice(block * LANES, (block + 1) * LANES)
        taps_ref[:, lanes] = values[:49]
        gain_ref[lanes] = values[49]
        shift_ref[lanes] = values[50]
        bias_ref[lanes] = values[51]
        up_ref[lanes] = values[52]
        up_ref[feat + block * LANES : feat + (block + 1) * LANES] = values[53]


def finish(received, owned_rows, feat, hid, inverse_count):
    row = jax.ShapeDtypeStruct((feat,), jnp.float32)
    return pl.pallas_call(
        functools.partial(finish_kernel, inverse_count),
        name="finish",
        out_shape=(
            jax.ShapeDtypeStruct((owned_rows, hid), jnp.float32),
            jax.ShapeDtypeStruct((hid,), jnp.float32),
            row,
            row,
            jax.ShapeDtypeStruct((49, feat), jnp.float32),
            row,
        ),
        compiler_params=pltpu.CompilerParams(vmem_limit_bytes=VMEM_LIMIT),
        cost_estimate=SMALL,
    )(received)


def swap_pieces(values, axes):
    return lax.all_to_all(values, axes, 0, 0, tiled=True)


def total_of(received):
    return jnp.sum(received.astype(jnp.float32), axis=0)


def per_device(images, hidden_cot, residual_cot, w_up, b_up, ln_gain, ln_bias, dw_weight, dw_bias):
    feat, hid = w_up.shape
    plane = ("x", "y_hi", "y_lo")
    along_z = lax.axis_size("z")
    owned_rows = feat // (32 * along_z)
    inverse_count = 1.0 / (images.shape[0] * 32 * along_z)
    mine = lax.axis_index("core").astype(jnp.int32).reshape(1)
    y_index = 2 * lax.axis_index("y_hi") + lax.axis_index("y_lo")
    place = jnp.stack([lax.axis_index("x"), y_index]).astype(jnp.int32)
    swap = [(0, 1), (1, 0)]

    unit, sigma, turned, away, near, up_sums = front(
        mine, images, dw_weight, dw_bias, ln_gain, ln_bias, w_up, b_up.reshape(1, -1), hidden_cot, along_z
    )
    far = lax.ppermute(away, "core", swap)
    far_turned = lax.ppermute(turned, "core", swap)
    cells = unit.shape[0]
    *part_a, part_b = product(
        place, turned.reshape(4, 4, -1, cells), far_turned.reshape(4, 4, -1, cells), near, far, 7 * hid // 24
    )
    part_b, unit = lax.optimization_barrier((part_b, unit))
    part_a = to_owners(part_a, "x")
    part_b = swap_pieces(part_b, ("y_hi", "y_lo"))

    grad_input, small = back(
        mine, away, near, w_up, unit, sigma, ln_gain, up_sums, images, residual_cot, dw_weight
    )
    part_b, small = lax.optimization_barrier((part_b, small))

    around = ("z", "core")
    small = swap_pieces(small.reshape(2 * along_z, -1, LANES), around)
    small = total_of(small).astype(jnp.bfloat16)
    part_a, small = lax.optimization_barrier((part_a, small))
    small = swap_pieces(jnp.broadcast_to(small, (16,) + small.shape), plane)

    part_b = to_owners(sum_pieces([part_b]), "x")
    part_b[1], part_a = lax.optimization_barrier((part_b[1], part_a))
    part_a = to_owners(sum_pieces(part_a), ("y_lo", "y_hi"))
    last = jnp.concatenate([total_of(jnp.stack(part_a)), total_of(jnp.stack(part_b))], axis=1)
    last = last.astype(jnp.bfloat16).reshape(2 * along_z, -1, LANES)
    small = (total_of(small) * inverse_count).astype(jnp.bfloat16)
    small = jnp.broadcast_to(small, (2 * along_z,) + small.shape)
    last = swap_pieces(jnp.concatenate([small, last], axis=1), around)
    return (grad_input, *finish(last, owned_rows, feat, hid, inverse_count))


def solution(mesh):
    x, z = 4, mesh.devices.size // 32
    split = Mesh(mesh.devices.reshape(2, x, z, 2, 2), ("y_lo", "x", "z", "y_hi", "core"))
    images = P(("y_lo", "x", "z", "y_hi", "core"))
    return jax.shard_map(
        per_device,
        mesh=split,
        in_specs=(images, images, images, P(), P(), P(), P(), P(), P()),
        out_specs=(images, images, P(), P(), P(), P(), P()),
        check_vma=False,
    )
```

```python
import functools

import jax
import jax.numpy as jnp
import numpy as np
from jax import lax
from jax.experimental import pallas as pl
from jax.experimental.pallas import tpu as pltpu
from jax.sharding import Mesh
from jax.sharding import PartitionSpec as P

LANES = 128
EDGE = 8
VMEM_LIMIT = 60 * 1024 * 1024
SMALL = pl.CostEstimate(flops=1000, bytes_accessed=1000, transcendentals=0)
SMALL_ROWS = 64


def front_kernel(
    core_ref, image_ref, taps_ref, bias_ref, gain_ref, shift_ref, order_ref, b_ref, w_hbm, cot_hbm,
    unit_out, sigma_ref, turned_ref, away_out, near_out, sums_ref,
    padded, conv, unit, normed, weights, cots, grads, in_sems, out_sems,
):
    side, feat = image_ref.shape[1], image_ref.shape[3]
    parts, _, width = weights.shape
    half = parts // 2
    core = core_ref[0]

    def column(part):
        owner = 1 - core if part < half else core
        return pl.multiple_of((owner * half + part % half) * width, width)

    loads = []
    for part in range(parts):
        columns = pl.ds(column(part), width)
        loads.append(
            (
                pltpu.make_async_copy(w_hbm.at[:, columns], weights.at[part], in_sems.at[2 * part]),
                pltpu.make_async_copy(cot_hbm.at[0, :, columns], cots.at[part], in_sems.at[2 * part + 1]),
            )
        )
    for pair in loads:
        pair[0].start()
        pair[1].start()

    blank = jnp.zeros((side, EDGE, LANES), jnp.float32)
    padded[:, 0:EDGE, :] = blank
    padded[:, EDGE + side : EDGE + side + EDGE, :] = blank

    @pl.loop(0, feat // LANES)
    def _(block):
        lanes = pl.ds(pl.multiple_of(block * LANES, LANES), LANES)
        padded[:, EDGE : EDGE + side, :] = image_ref[0, :, :, lanes].astype(jnp.float32)
        start = jnp.broadcast_to(bias_ref[lanes].reshape(1, LANES), (side, LANES))
        sums = [start] * side
        for tap_col in range(7):
            taps = [
                jnp.broadcast_to(taps_ref[pl.ds(7 * tap_row + tap_col, 1), lanes], (side, LANES))
                for tap_row in range(7)
            ]
            for source in range(side):
                cells = padded[source, EDGE - 3 + tap_col : EDGE - 3 + tap_col + side, :]
                for tap_row in range(7):
                    target = source + 3 - tap_row
                    if 0 <= target < side:
                        sums[target] = sums[target] + cells * taps[tap_row]
        for row in range(side):
            conv[row * side : (row + 1) * side, lanes] = sums[row]

    gain = gain_ref[...].reshape(1, feat)
    shift = shift_ref[...].reshape(1, feat)

    @pl.loop(0, side, unroll=4)
    def _(row):
        cells = pl.ds(pl.multiple_of(row * side, side), side)
        values = conv[cells, :]
        centred = values - jnp.mean(values, axis=-1, keepdims=True)
        inv_sigma = lax.rsqrt(jnp.mean(centred * centred, axis=-1, keepdims=True) + 1e-06)
        scaled = centred * inv_sigma
        unit[cells, :] = scaled
        sigma_ref[cells, :] = jnp.broadcast_to(inv_sigma, (side, LANES))
        normed[cells, :] = (scaled * gain + shift).astype(jnp.bfloat16)

    unit_copy = pltpu.make_async_copy(unit, unit_out, out_sems.at[0])
    unit_copy.start()

    group = order_ref.shape[0]
    rows = turned_ref.shape[3]
    for index in range(feat // group):
        y_lo, pair = divmod(index, 2)
        turned = lax.dot_general(
            order_ref[...],
            normed[:, index * group : (index + 1) * group],
            (((1,), (1,)), ((), ())),
            preferred_element_type=jnp.float32,
        ).astype(jnp.bfloat16)
        for within in range(2):
            for y_hi in range(2):
                first = (within * 2 + y_hi) * rows
                turned_ref[2 * pair + within, y_hi, y_lo] = turned[first : first + rows]

    stores = [unit_copy]
    for part in range(parts):
        loads[part][0].wait()
        loads[part][1].wait()
        columns = pl.ds(column(part), width)
        pre_act = jnp.dot(normed[...], weights[part], preferred_element_type=jnp.float32)
        pre_act = pre_act + b_ref[:, columns]
        slope = 0.5 * (1.0 + lax.erf(pre_act * 0.7071067811865476)) + pre_act * jnp.exp(
            -0.5 * pre_act * pre_act
        ) * 0.3989422804014327
        grad = (cots[part].astype(jnp.float32) * slope).astype(jnp.bfloat16)
        grads[part] = grad
        sums_ref[:, columns] = jnp.sum(grad.astype(jnp.float32), axis=0, keepdims=True)
        target = away_out if part < half else near_out
        copy = pltpu.make_async_copy(
            grads.at[part], target.at[:, (part % half) * width : (part % half + 1) * width], out_sems.at[1 + part]
        )
        copy.start()
        stores.append(copy)
    for copy in stores:
        copy.wait()


def channel_order(rows, along_z):
    width = 4 * rows
    owned = rows // along_z
    target = np.arange(width).reshape(2, along_z, 2, owned).transpose(0, 2, 1, 3).reshape(-1)
    return jnp.asarray(np.eye(width, dtype=np.float32)[target], jnp.bfloat16)


def front(core, image, taps, bias, gain, shift, w_up, b_row, cot, along_z, parts=4):
    side, feat = image.shape[1], image.shape[3]
    cells = side * side
    hid = w_up.shape[1]
    rows = feat // 16
    width = hid // parts
    whole = pl.BlockSpec(memory_space=pltpu.VMEM)
    remain = pl.BlockSpec(memory_space=pl.ANY)
    return pl.pallas_call(
        front_kernel,
        name="front",
        in_specs=[pl.BlockSpec(memory_space=pltpu.SMEM)] + [whole] * 7 + [remain] * 2,
        out_specs=[remain, whole, whole, remain, remain, whole],
        out_shape=(
            jax.ShapeDtypeStruct((cells, feat), jnp.float32),
            jax.ShapeDtypeStruct((cells, LANES), jnp.float32),
            jax.ShapeDtypeStruct((4, 2, 2, rows, cells), jnp.bfloat16),
            jax.ShapeDtypeStruct((cells, hid // 2), jnp.bfloat16),
            jax.ShapeDtypeStruct((cells, hid // 2), jnp.bfloat16),
            jax.ShapeDtypeStruct((1, hid), jnp.float32),
        ),
        scratch_shapes=[
            pltpu.VMEM((side, side + 2 * EDGE, LANES), jnp.float32),
            pltpu.VMEM((cells, feat), jnp.float32),
            pltpu.VMEM((cells, feat), jnp.float32),
            pltpu.VMEM((cells, feat), jnp.bfloat16),
            pltpu.VMEM((parts, feat, width), jnp.bfloat16),
            pltpu.VMEM((parts, cells, width), jnp.bfloat16),
            pltpu.VMEM((parts, cells, width), jnp.bfloat16),
            pltpu.SemaphoreType.DMA((2 * parts,)),
            pltpu.SemaphoreType.DMA((1 + parts,)),
        ],
        compiler_params=pltpu.CompilerParams(vmem_limit_bytes=VMEM_LIMIT),
        cost_estimate=SMALL,
    )(core, image, taps, bias, gain, shift, channel_order(rows, along_z), b_row, w_up, cot)


def product_kernel(place_ref, near_t_hbm, far_t_hbm, near_hbm, far_hbm, *refs):
    out_refs = refs[:5]
    pieces, others, near_t_ref, far_t_ref, near_ref, far_ref, sems, in_sems = refs[5:]
    _, along_y, rows, cells = near_t_ref.shape
    columns = pieces.shape[3]
    loads = [
        pltpu.make_async_copy(near_hbm, near_ref, in_sems.at[0]),
        pltpu.make_async_copy(far_hbm, far_ref, in_sems.at[1]),
    ]
    for step in range(4):
        x = lax.rem(place_ref[0] + step, 4)
        loads.append(pltpu.make_async_copy(near_t_hbm.at[x], near_t_ref.at[step], in_sems.at[2 + 2 * step]))
        loads.append(pltpu.make_async_copy(far_t_hbm.at[x], far_t_ref.at[step], in_sems.at[3 + 2 * step]))
    for load in loads:
        load.start()
    copies = []
    for step in range(4):
        for load in loads[:4] if step == 0 else loads[2 + 2 * step : 4 + 2 * step]:
            load.wait()
        near_t = near_t_ref[step].reshape(along_y * rows, cells)
        far_t = far_t_ref[step].reshape(along_y * rows, cells)
        block = (
            jnp.dot(near_t, near_ref[...], preferred_element_type=jnp.float32)
            + jnp.dot(far_t, far_ref[...], preferred_element_type=jnp.float32)
        ).astype(jnp.bfloat16)
        for y in range(along_y):
            part = block[y * rows : (y + 1) * rows]
            pieces[step, lax.rem(y - place_ref[1] + 4, 4)] = part[:, :columns]
            others[y, step] = part[:, columns:]
        copies.append(pltpu.make_async_copy(pieces.at[step], out_refs[step], sems.at[step]))
        copies.append(pltpu.make_async_copy(others.at[:, step], out_refs[4].at[:, step], sems.at[4 + step]))
        for copy in copies[-2:]:
            copy.start()
    for copy in copies:
        copy.wait()


def product(place, near_t, far_t, near, far, columns):
    _, _, rows, cells = near_t.shape
    rest = near.shape[1] - columns
    remain = pl.BlockSpec(memory_space=pl.ANY)
    return pl.pallas_call(
        product_kernel,
        name="product",
        in_specs=[pl.BlockSpec(memory_space=pltpu.SMEM)] + [remain] * 4,
        out_specs=[remain] * 5,
        out_shape=[jax.ShapeDtypeStruct((4, rows, columns), jnp.bfloat16)] * 4
        + [jax.ShapeDtypeStruct((4, 4, rows, rest), jnp.bfloat16)],
        scratch_shapes=[
            pltpu.VMEM((4, 4, rows, columns), jnp.bfloat16),
            pltpu.VMEM((4, 4, rows, rest), jnp.bfloat16),
            pltpu.VMEM(near_t.shape, jnp.bfloat16),
            pltpu.VMEM(far_t.shape, jnp.bfloat16),
            pltpu.VMEM(near.shape, jnp.bfloat16),
            pltpu.VMEM(far.shape, jnp.bfloat16),
            pltpu.SemaphoreType.DMA((8,)),
            pltpu.SemaphoreType.DMA((10,)),
        ],
        compiler_params=pltpu.CompilerParams(vmem_limit_bytes=VMEM_LIMIT),
        cost_estimate=SMALL,
    )(place, near_t, far_t, near, far)


def sum_kernel(*refs):
    outs = refs[-8:-4]
    ins, held, sums, in_sems, out_sems = refs[:-8], refs[-4], refs[-3], refs[-2], refs[-1]
    loads, stores = [], []
    for index in range(4):
        for source in range(4):
            piece = ins[0].at[source, index] if len(ins) == 1 else ins[source].at[index]
            loads.append(pltpu.make_async_copy(piece, held.at[index, source], in_sems.at[4 * index + source]))
            loads[-1].start()
    for index in range(4):
        for load in loads[4 * index : 4 * index + 4]:
            load.wait()
        total = held[index, 0].astype(jnp.float32)
        for source in range(1, 4):
            total = total + held[index, source].astype(jnp.float32)
        sums[index] = total.astype(jnp.bfloat16)
        stores.append(pltpu.make_async_copy(sums.at[index], outs[index], out_sems.at[index]))
        stores[-1].start()
    for store in stores:
        store.wait()


def sum_pieces(pieces):
    rows, columns = pieces[0].shape[-2:]
    remain = pl.BlockSpec(memory_space=pl.ANY)
    return pl.pallas_call(
        sum_kernel,
        name="sum_pieces",
        in_specs=[remain] * len(pieces),
        out_specs=[remain] * 4,
        out_shape=[jax.ShapeDtypeStruct((rows, columns), jnp.bfloat16)] * 4,
        scratch_shapes=[
            pltpu.VMEM((4, 4, rows, columns), jnp.bfloat16),
            pltpu.VMEM((4, rows, columns), jnp.bfloat16),
            pltpu.SemaphoreType.DMA((16,)),
            pltpu.SemaphoreType.DMA((4,)),
        ],
        compiler_params=pltpu.CompilerParams(vmem_limit_bytes=VMEM_LIMIT),
        cost_estimate=SMALL,
    )(*pieces)


def to_owners(pieces, axes):
    named = range(4) if axes == "x" else [0, 2, 1, 3]
    moved = [
        lax.ppermute(piece, axes, [(named[i], named[(i + d) % 4]) for i in range(4)])
        for d, piece in enumerate(pieces)
        if d
    ]
    return [pieces[0]] + moved


def back_kernel(
    core_ref, away_ref, near_ref, sigma_ref, gain_ref, up_first_ref, up_second_ref, image_ref, res_ref, taps_ref,
    unit_hbm, w_hbm, out_ref, sums_ref, weights, unit, total, norm_sums, padded, image, small, sems,
):
    side = image_ref.shape[1]
    feat = total.shape[1]

    @pl.when(pl.program_id(0) == 0)
    def _():
        parts, _, width = weights.shape
        half = parts // 2
        core = core_ref[0]
        loads = []
        for part in range(parts):
            owner = 1 - core if part < half else core
            columns = pl.ds(pl.multiple_of((owner * half + part % half) * width, width), width)
            loads.append(pltpu.make_async_copy(w_hbm.at[:, columns], weights.at[part], sems.at[part]))
        loads.append(pltpu.make_async_copy(unit_hbm, unit, sems.at[parts]))
        for load in loads:
            load.start()
        blank = jnp.zeros((side, EDGE, LANES), jnp.float32)
        padded[:, 0:EDGE, :] = blank
        padded[:, EDGE + side : EDGE + side + EDGE, :] = blank
        for part in range(parts):
            loads[part].wait()
            grad_ref = away_ref if part < half else near_ref
            grad = grad_ref[:, (part % half) * width : (part % half + 1) * width]
            value = lax.dot_general(
                grad, weights[part], (((1,), (1,)), ((), ())), preferred_element_type=jnp.float32
            )
            if part:
                total[...] += value
            else:
                total[...] = value
        loads[parts].wait()
        gain = gain_ref[...].reshape(1, feat)

        def finish(row, carry):
            gain_sum, shift_sum = carry
            cells = pl.ds(pl.multiple_of(row * 32, 32), 32)
            grad = total[cells, :]
            scaled = unit[cells, :]
            gain_sum = gain_sum + jnp.sum((grad * scaled).reshape(4, 8, feat), axis=0)
            shift_sum = shift_sum + jnp.sum(grad.reshape(4, 8, feat), axis=0)
            unit_grad = grad * gain
            first = jnp.sum(unit_grad, axis=-1, keepdims=True) * (1.0 / feat)
            second = jnp.sum(unit_grad * scaled, axis=-1, keepdims=True) * (1.0 / feat)
            total[cells, :] = sigma_ref[cells, 0:1] * (unit_grad - first - scaled * second)
            return gain_sum, shift_sum

        zero = jnp.zeros((8, feat), jnp.float32)
        gain_sum, shift_sum = lax.fori_loop(0, total.shape[0] // 32, finish, (zero, zero))
        norm_sums[0:1, :] = jnp.sum(gain_sum, axis=0, keepdims=True)
        norm_sums[1:2, :] = jnp.sum(shift_sum, axis=0, keepdims=True)

    lanes = pl.ds(pl.multiple_of(pl.program_id(0) * LANES, LANES), LANES)
    image[...] = image_ref[0].astype(jnp.float32)
    bias_sum = jnp.zeros((side, LANES), jnp.float32)
    for row in range(side):
        cells = total[row * side : (row + 1) * side, lanes]
        padded[row, EDGE : EDGE + side, :] = cells
        bias_sum = bias_sum + cells
    tap_sums = [None] * 49
    sums = [res_ref[0, row].astype(jnp.float32) for row in range(side)]
    for turn_col in range(7):
        weights_here = [
            jnp.broadcast_to(taps_ref[pl.ds(7 * (6 - turn_row) + 6 - turn_col, 1), :], (side, LANES))
            for turn_row in range(7)
        ]
        parts_here = [jnp.zeros((8, LANES), jnp.float32) for _ in range(7)]
        for source in range(side):
            cells = padded[source, EDGE - 3 + turn_col : EDGE - 3 + turn_col + side, :]
            for turn_row in range(7):
                target = source + 3 - turn_row
                if 0 <= target < side:
                    sums[target] = sums[target] + cells * weights_here[turn_row]
                    product = cells * image[target]
                    parts_here[turn_row] = parts_here[turn_row] + (product[:8] + product[8:])
        for turn_row in range(7):
            tap = 7 * (6 - turn_row) + 6 - turn_col
            small[tap : tap + 1, :] = jnp.sum(parts_here[turn_row], axis=0, keepdims=True)
    small[49:51, :] = norm_sums[0:2, lanes]
    small[51:52, :] = jnp.sum(bias_sum, axis=0, keepdims=True)
    small[52:53, :] = up_first_ref[...]
    small[53:54, :] = up_second_ref[...]
    small[54:, :] = jnp.zeros((SMALL_ROWS - 54, LANES), jnp.float32)
    sums_ref[0] = small[...].astype(jnp.bfloat16)
    for row in range(side):
        out_ref[0, row] = sums[row].astype(jnp.bfloat16)


def back(core, away, near, w_up, unit, sigma, gain, up_sums, image, residual, taps, parts=4):
    cells, feat = unit.shape
    side = image.shape[1]
    width = w_up.shape[1] // parts
    whole = pl.BlockSpec(memory_space=pltpu.VMEM)
    remain = pl.BlockSpec(memory_space=pl.ANY)
    picture = pl.BlockSpec((1, side, side, LANES), lambda i: (0, 0, 0, i))
    return pl.pallas_call(
        back_kernel,
        name="back",
        grid=(feat // LANES,),
        in_specs=[pl.BlockSpec(memory_space=pltpu.SMEM)]
        + [whole] * 4
        + [
            pl.BlockSpec((1, LANES), lambda i: (0, i)),
            pl.BlockSpec((1, LANES), lambda i: (0, i + feat // LANES)),
            picture,
            picture,
            pl.BlockSpec((49, LANES), lambda i: (0, i)),
            remain,
            remain,
        ],
        out_specs=[picture, pl.BlockSpec((1, SMALL_ROWS, LANES), lambda i: (i, 0, 0))],
        out_shape=(
            jax.ShapeDtypeStruct(image.shape, jnp.bfloat16),
            jax.ShapeDtypeStruct((feat // LANES, SMALL_ROWS, LANES), jnp.bfloat16),
        ),
        scratch_shapes=[
            pltpu.VMEM((parts, feat, width), jnp.bfloat16),
            pltpu.VMEM((cells, feat), jnp.float32),
            pltpu.VMEM((cells, feat), jnp.float32),
            pltpu.VMEM((8, feat), jnp.float32),
            pltpu.VMEM((side, side + 2 * EDGE, LANES), jnp.float32),
            pltpu.VMEM((side, side, LANES), jnp.float32),
            pltpu.VMEM((SMALL_ROWS, LANES), jnp.float32),
            pltpu.SemaphoreType.DMA((1 + parts,)),
        ],
        compiler_params=pltpu.CompilerParams(vmem_limit_bytes=VMEM_LIMIT),
        cost_estimate=SMALL,
    )(core, away, near, sigma, gain, up_sums, up_sums, image, residual, taps, unit, w_up)


def finish_kernel(inverse_count, received_ref, owned_ref, up_ref, gain_ref, shift_ref, taps_ref, bias_ref):
    pieces, height, _ = received_ref.shape
    owned_rows, hid = owned_ref.shape
    blocks = hid // 2 // LANES
    share = height - owned_rows * blocks
    for core in range(2):
        total = received_ref[core, share:, :].astype(jnp.float32)
        for z in range(1, pieces // 2):
            total = total + received_ref[2 * z + core, share:, :].astype(jnp.float32)
        total = total * inverse_count
        for row in range(owned_rows):
            for block in range(blocks):
                first = (core * blocks + block) * LANES
                index = row * blocks + block
                owned_ref[row : row + 1, first : first + LANES] = total[index : index + 1]
    feat = gain_ref.shape[0]
    for block in range(feat // LANES):
        parts = []
        row, end = block * SMALL_ROWS, (block + 1) * SMALL_ROWS
        while row < end:
            stop = min(end, (row // share + 1) * share)
            first = row % share
            parts.append(received_ref[row // share, first : first + stop - row, :].astype(jnp.float32))
            row = stop
        values = jnp.concatenate(parts, axis=0)
        lanes = slice(block * LANES, (block + 1) * LANES)
        taps_ref[:, lanes] = values[:49]
        gain_ref[lanes] = values[49]
        shift_ref[lanes] = values[50]
        bias_ref[lanes] = values[51]
        up_ref[lanes] = values[52]
        up_ref[feat + block * LANES : feat + (block + 1) * LANES] = values[53]


def finish(received, owned_rows, feat, hid, inverse_count):
    row = jax.ShapeDtypeStruct((feat,), jnp.float32)
    return pl.pallas_call(
        functools.partial(finish_kernel, inverse_count),
        name="finish",
        out_shape=(
            jax.ShapeDtypeStruct((owned_rows, hid), jnp.float32),
            jax.ShapeDtypeStruct((hid,), jnp.float32),
            row,
            row,
            jax.ShapeDtypeStruct((49, feat), jnp.float32),
            row,
        ),
        compiler_params=pltpu.CompilerParams(vmem_limit_bytes=VMEM_LIMIT),
        cost_estimate=SMALL,
    )(received)


def swap_pieces(values, axes):
    return lax.all_to_all(values, axes, 0, 0, tiled=True)


def total_of(received):
    return jnp.sum(received.astype(jnp.float32), axis=0)


def per_device(images, hidden_cot, residual_cot, w_up, b_up, ln_gain, ln_bias, dw_weight, dw_bias):
    feat, hid = w_up.shape
    plane = ("x", "y_hi", "y_lo")
    along_z = lax.axis_size("z")
    owned_rows = feat // (32 * along_z)
    inverse_count = 1.0 / (images.shape[0] * 32 * along_z)
    mine = lax.axis_index("core").astype(jnp.int32).reshape(1)
    y_index = 2 * lax.axis_index("y_hi") + lax.axis_index("y_lo")
    place = jnp.stack([lax.axis_index("x"), y_index]).astype(jnp.int32)
    swap = [(0, 1), (1, 0)]

    unit, sigma, turned, away, near, up_sums = front(
        mine, images, dw_weight, dw_bias, ln_gain, ln_bias, w_up, b_up.reshape(1, -1), hidden_cot, along_z
    )
    far = lax.ppermute(away, "core", swap)
    far_turned = lax.ppermute(turned, "core", swap)
    cells = unit.shape[0]
    *part_a, part_b = product(
        place, turned.reshape(4, 4, -1, cells), far_turned.reshape(4, 4, -1, cells), near, far, 7 * hid // 24
    )
    part_b, unit = lax.optimization_barrier((part_b, unit))
    part_a = to_owners(part_a, "x")
    part_b = swap_pieces(part_b, ("y_hi", "y_lo"))

    grad_input, small = back(
        mine, away, near, w_up, unit, sigma, ln_gain, up_sums, images, residual_cot, dw_weight
    )
    part_b, small = lax.optimization_barrier((part_b, small))

    around = ("z", "core")
    small = swap_pieces(small.reshape(2 * along_z, -1, LANES), around)
    small = total_of(small).astype(jnp.bfloat16)
    part_a, small = lax.optimization_barrier((part_a, small))
    small = swap_pieces(jnp.broadcast_to(small, (16,) + small.shape), plane)

    part_b = to_owners(sum_pieces([part_b]), "x")
    part_b[1], part_a = lax.optimization_barrier((part_b[1], part_a))
    part_a = to_owners(sum_pieces(part_a), ("y_lo", "y_hi"))
    last = jnp.concatenate([total_of(jnp.stack(part_a)), total_of(jnp.stack(part_b))], axis=1)
    last = last.astype(jnp.bfloat16).reshape(2 * along_z, -1, LANES)
    small = (total_of(small) * inverse_count).astype(jnp.bfloat16)
    small = jnp.broadcast_to(small, (2 * along_z,) + small.shape)
    last = swap_pieces(jnp.concatenate([small, last], axis=1), around)
    return (grad_input, *finish(last, owned_rows, feat, hid, inverse_count))


def solution(mesh):
    x, z = 4, mesh.devices.size // 32
    split = Mesh(mesh.devices.reshape(2, x, z, 2, 2), ("y_lo", "x", "z", "y_hi", "core"))
    images = P(("y_lo", "x", "z", "y_hi", "core"))
    return jax.shard_map(
        per_device,
        mesh=split,
        in_specs=(images, images, images, P(), P(), P(), P(), P(), P()),
        out_specs=(images, images, P(), P(), P(), P(), P()),
        check_vma=False,
    )
```

```python
import functools

import jax
import jax.numpy as jnp
import numpy as np
from jax import lax
from jax.experimental import pallas as pl
from jax.experimental.pallas import tpu as pltpu
from jax.sharding import Mesh
from jax.sharding import PartitionSpec as P

LANES = 128
EDGE = 8
VMEM_LIMIT = 60 * 1024 * 1024
SMALL = pl.CostEstimate(flops=1000, bytes_accessed=1000, transcendentals=0)
SMALL_ROWS = 64


def front_kernel(
    core_ref, image_ref, taps_ref, bias_ref, gain_ref, shift_ref, order_ref, b_ref, w_hbm, cot_hbm,
    unit_out, sigma_ref, turned_ref, away_out, near_out, sums_ref,
    padded, conv, unit, normed, weights, cots, grads, in_sems, out_sems,
):
    side, feat = image_ref.shape[1], image_ref.shape[3]
    parts, _, width = weights.shape
    half = parts // 2
    core = core_ref[0]

    def column(part):
        owner = 1 - core if part < half else core
        return pl.multiple_of((owner * half + part % half) * width, width)

    loads = []
    for part in range(parts):
        columns = pl.ds(column(part), width)
        loads.append(
            (
                pltpu.make_async_copy(w_hbm.at[:, columns], weights.at[part], in_sems.at[2 * part]),
                pltpu.make_async_copy(cot_hbm.at[0, :, columns], cots.at[part], in_sems.at[2 * part + 1]),
            )
        )
    for pair in loads:
        pair[0].start()
        pair[1].start()

    blank = jnp.zeros((side, EDGE, LANES), jnp.float32)
    padded[:, 0:EDGE, :] = blank
    padded[:, EDGE + side : EDGE + side + EDGE, :] = blank

    @pl.loop(0, feat // LANES)
    def _(block):
        lanes = pl.ds(pl.multiple_of(block * LANES, LANES), LANES)
        padded[:, EDGE : EDGE + side, :] = image_ref[0, :, :, lanes].astype(jnp.float32)
        start = jnp.broadcast_to(bias_ref[lanes].reshape(1, LANES), (side, LANES))
        sums = [start] * side
        for tap_col in range(7):
            taps = [
                jnp.broadcast_to(taps_ref[pl.ds(7 * tap_row + tap_col, 1), lanes], (side, LANES))
                for tap_row in range(7)
            ]
            for source in range(side):
                cells = padded[source, EDGE - 3 + tap_col : EDGE - 3 + tap_col + side, :]
                for tap_row in range(7):
                    target = source + 3 - tap_row
                    if 0 <= target < side:
                        sums[target] = sums[target] + cells * taps[tap_row]
        for row in range(side):
            conv[row * side : (row + 1) * side, lanes] = sums[row]

    gain = gain_ref[...].reshape(1, feat)
    shift = shift_ref[...].reshape(1, feat)

    @pl.loop(0, side, unroll=16)
    def _(row):
        cells = pl.ds(pl.multiple_of(row * side, side), side)
        values = conv[cells, :]
        centred = values - jnp.mean(values, axis=-1, keepdims=True)
        inv_sigma = lax.rsqrt(jnp.mean(centred * centred, axis=-1, keepdims=True) + 1e-06)
        scaled = centred * inv_sigma
        unit[cells, :] = scaled
        sigma_ref[cells, :] = jnp.broadcast_to(inv_sigma, (side, LANES))
        normed[cells, :] = (scaled * gain + shift).astype(jnp.bfloat16)

    unit_copy = pltpu.make_async_copy(unit, unit_out, out_sems.at[0])
    unit_copy.start()

    group = order_ref.shape[0]
    rows = turned_ref.shape[3]
    for index in range(feat // group):
        y_lo, pair = divmod(index, 2)
        turned = lax.dot_general(
            order_ref[...],
            normed[:, index * group : (index + 1) * group],
            (((1,), (1,)), ((), ())),
            preferred_element_type=jnp.float32,
        ).astype(jnp.bfloat16)
        for within in range(2):
            for y_hi in range(2):
                first = (within * 2 + y_hi) * rows
                turned_ref[2 * pair + within, y_hi, y_lo] = turned[first : first + rows]

    stores = [unit_copy]
    for part in range(parts):
        loads[part][0].wait()
        loads[part][1].wait()
        columns = pl.ds(column(part), width)
        pre_act = jnp.dot(normed[...], weights[part], preferred_element_type=jnp.float32)
        pre_act = pre_act + b_ref[:, columns]
        slope = 0.5 * (1.0 + lax.erf(pre_act * 0.7071067811865476)) + pre_act * jnp.exp(
            -0.5 * pre_act * pre_act
        ) * 0.3989422804014327
        grad = (cots[part].astype(jnp.float32) * slope).astype(jnp.bfloat16)
        grads[part] = grad
        sums_ref[:, columns] = jnp.sum(grad.astype(jnp.float32), axis=0, keepdims=True)
        target = away_out if part < half else near_out
        copy = pltpu.make_async_copy(
            grads.at[part], target.at[:, (part % half) * width : (part % half + 1) * width], out_sems.at[1 + part]
        )
        copy.start()
        stores.append(copy)
    for copy in stores:
        copy.wait()


def channel_order(rows, along_z):
    width = 4 * rows
    owned = rows // along_z
    target = np.arange(width).reshape(2, along_z, 2, owned).transpose(0, 2, 1, 3).reshape(-1)
    return jnp.asarray(np.eye(width, dtype=np.float32)[target], jnp.bfloat16)


def front(core, image, taps, bias, gain, shift, w_up, b_row, cot, along_z, parts=2):
    side, feat = image.shape[1], image.shape[3]
    cells = side * side
    hid = w_up.shape[1]
    rows = feat // 16
    width = hid // parts
    whole = pl.BlockSpec(memory_space=pltpu.VMEM)
    remain = pl.BlockSpec(memory_space=pl.ANY)
    return pl.pallas_call(
        front_kernel,
        name="front",
        in_specs=[pl.BlockSpec(memory_space=pltpu.SMEM)] + [whole] * 7 + [remain] * 2,
        out_specs=[remain, whole, whole, remain, remain, whole],
        out_shape=(
            jax.ShapeDtypeStruct((cells, feat), jnp.float32),
            jax.ShapeDtypeStruct((cells, LANES), jnp.float32),
            jax.ShapeDtypeStruct((4, 2, 2, rows, cells), jnp.bfloat16),
            jax.ShapeDtypeStruct((cells, hid // 2), jnp.bfloat16),
            jax.ShapeDtypeStruct((cells, hid // 2), jnp.bfloat16),
            jax.ShapeDtypeStruct((1, hid), jnp.float32),
        ),
        scratch_shapes=[
            pltpu.VMEM((side, side + 2 * EDGE, LANES), jnp.float32),
            pltpu.VMEM((cells, feat), jnp.float32),
            pltpu.VMEM((cells, feat), jnp.float32),
            pltpu.VMEM((cells, feat), jnp.bfloat16),
            pltpu.VMEM((parts, feat, width), jnp.bfloat16),
            pltpu.VMEM((parts, cells, width), jnp.bfloat16),
            pltpu.VMEM((parts, cells, width), jnp.bfloat16),
            pltpu.SemaphoreType.DMA((2 * parts,)),
            pltpu.SemaphoreType.DMA((1 + parts,)),
        ],
        compiler_params=pltpu.CompilerParams(vmem_limit_bytes=VMEM_LIMIT),
        cost_estimate=SMALL,
    )(core, image, taps, bias, gain, shift, channel_order(rows, along_z), b_row, w_up, cot)


def product_kernel(place_ref, near_t_ref, far_t_ref, near_ref, far_ref, *refs):
    out_refs, pieces, others, sems = refs[:5], refs[5], refs[6], refs[7]
    _, along_y, rows, cells = near_t_ref.shape
    columns = pieces.shape[3]
    copies = []
    for step in range(4):
        x = lax.rem(place_ref[0] + step, 4)
        near_t = near_t_ref[x].reshape(along_y * rows, cells)
        far_t = far_t_ref[x].reshape(along_y * rows, cells)
        block = (
            jnp.dot(near_t, near_ref[...], preferred_element_type=jnp.float32)
            + jnp.dot(far_t, far_ref[...], preferred_element_type=jnp.float32)
        ).astype(jnp.bfloat16)
        for y in range(along_y):
            part = block[y * rows : (y + 1) * rows]
            pieces[step, lax.rem(y - place_ref[1] + 4, 4)] = part[:, :columns]
            others[y, step] = part[:, columns:]
        copies.append(pltpu.make_async_copy(pieces.at[step], out_refs[step], sems.at[step]))
        copies.append(pltpu.make_async_copy(others.at[:, step], out_refs[4].at[:, step], sems.at[4 + step]))
        for copy in copies[-2:]:
            copy.start()
    for copy in copies:
        copy.wait()


def product(place, near_t, far_t, near, far, columns):
    _, _, rows, cells = near_t.shape
    rest = near.shape[1] - columns
    whole = pl.BlockSpec(memory_space=pltpu.VMEM)
    return pl.pallas_call(
        product_kernel,
        name="product",
        in_specs=[pl.BlockSpec(memory_space=pltpu.SMEM)] + [whole] * 4,
        out_specs=[pl.BlockSpec(memory_space=pl.ANY)] * 5,
        out_shape=[jax.ShapeDtypeStruct((4, rows, columns), jnp.bfloat16)] * 4
        + [jax.ShapeDtypeStruct((4, 4, rows, rest), jnp.bfloat16)],
        scratch_shapes=[
            pltpu.VMEM((4, 4, rows, columns), jnp.bfloat16),
            pltpu.VMEM((4, 4, rows, rest), jnp.bfloat16),
            pltpu.SemaphoreType.DMA((8,)),
        ],
        compiler_params=pltpu.CompilerParams(vmem_limit_bytes=VMEM_LIMIT),
        cost_estimate=SMALL,
    )(place, near_t, far_t, near, far)


def sum_kernel(*refs):
    ins, outs = refs[:-4], refs[-4:]
    for index in range(4):
        if len(ins) == 1:
            parts = [ins[0][source, index] for source in range(4)]
        else:
            parts = [ref[index] for ref in ins]
        total = parts[0].astype(jnp.float32)
        for part in parts[1:]:
            total = total + part.astype(jnp.float32)
        outs[index][...] = total.astype(jnp.bfloat16)


def sum_pieces(pieces):
    rows, columns = pieces[0].shape[-2:]
    return pl.pallas_call(
        sum_kernel,
        name="sum_pieces",
        out_shape=[jax.ShapeDtypeStruct((rows, columns), jnp.bfloat16)] * 4,
        compiler_params=pltpu.CompilerParams(vmem_limit_bytes=VMEM_LIMIT),
        cost_estimate=SMALL,
    )(*pieces)


def to_owners(pieces, axes):
    named = range(4) if axes == "x" else [0, 2, 1, 3]
    moved = [
        lax.ppermute(piece, axes, [(named[i], named[(i + d) % 4]) for i in range(4)])
        for d, piece in enumerate(pieces)
        if d
    ]
    return [pieces[0]] + moved


def back_kernel(
    core_ref, away_ref, near_ref, sigma_ref, gain_ref, up_first_ref, up_second_ref, image_ref, res_ref, taps_ref,
    unit_hbm, w_hbm, out_ref, sums_ref, weights, unit, total, norm_sums, padded, image, small, sems,
):
    side = image_ref.shape[1]
    feat = total.shape[1]

    @pl.when(pl.program_id(0) == 0)
    def _():
        parts, _, width = weights.shape
        half = parts // 2
        core = core_ref[0]
        loads = []
        for part in range(parts):
            owner = 1 - core if part < half else core
            columns = pl.ds(pl.multiple_of((owner * half + part % half) * width, width), width)
            loads.append(pltpu.make_async_copy(w_hbm.at[:, columns], weights.at[part], sems.at[part]))
        loads.append(pltpu.make_async_copy(unit_hbm, unit, sems.at[parts]))
        for load in loads:
            load.start()
        blank = jnp.zeros((side, EDGE, LANES), jnp.float32)
        padded[:, 0:EDGE, :] = blank
        padded[:, EDGE + side : EDGE + side + EDGE, :] = blank
        for part in range(parts):
            loads[part].wait()
            grad_ref = away_ref if part < half else near_ref
            grad = grad_ref[:, (part % half) * width : (part % half + 1) * width]
            value = lax.dot_general(
                grad, weights[part], (((1,), (1,)), ((), ())), preferred_element_type=jnp.float32
            )
            if part:
                total[...] += value
            else:
                total[...] = value
        loads[parts].wait()
        gain = gain_ref[...].reshape(1, feat)

        def finish(row, carry):
            gain_sum, shift_sum = carry
            cells = pl.ds(pl.multiple_of(row * 32, 32), 32)
            grad = total[cells, :]
            scaled = unit[cells, :]
            gain_sum = gain_sum + jnp.sum((grad * scaled).reshape(4, 8, feat), axis=0)
            shift_sum = shift_sum + jnp.sum(grad.reshape(4, 8, feat), axis=0)
            unit_grad = grad * gain
            first = jnp.sum(unit_grad, axis=-1, keepdims=True) * (1.0 / feat)
            second = jnp.sum(unit_grad * scaled, axis=-1, keepdims=True) * (1.0 / feat)
            total[cells, :] = sigma_ref[cells, 0:1] * (unit_grad - first - scaled * second)
            return gain_sum, shift_sum

        zero = jnp.zeros((8, feat), jnp.float32)
        gain_sum, shift_sum = lax.fori_loop(0, total.shape[0] // 32, finish, (zero, zero))
        norm_sums[0:1, :] = jnp.sum(gain_sum, axis=0, keepdims=True)
        norm_sums[1:2, :] = jnp.sum(shift_sum, axis=0, keepdims=True)

    lanes = pl.ds(pl.multiple_of(pl.program_id(0) * LANES, LANES), LANES)
    image[...] = image_ref[0].astype(jnp.float32)
    bias_sum = jnp.zeros((side, LANES), jnp.float32)
    for row in range(side):
        cells = total[row * side : (row + 1) * side, lanes]
        padded[row, EDGE : EDGE + side, :] = cells
        bias_sum = bias_sum + cells
    tap_sums = [None] * 49
    sums = [res_ref[0, row].astype(jnp.float32) for row in range(side)]
    for turn_col in range(7):
        weights_here = [
            jnp.broadcast_to(taps_ref[pl.ds(7 * (6 - turn_row) + 6 - turn_col, 1), :], (side, LANES))
            for turn_row in range(7)
        ]
        parts_here = [jnp.zeros((8, LANES), jnp.float32) for _ in range(7)]
        for source in range(side):
            cells = padded[source, EDGE - 3 + turn_col : EDGE - 3 + turn_col + side, :]
            for turn_row in range(7):
                target = source + 3 - turn_row
                if 0 <= target < side:
                    sums[target] = sums[target] + cells * weights_here[turn_row]
                    product = cells * image[target]
                    parts_here[turn_row] = parts_here[turn_row] + (product[:8] + product[8:])
        for turn_row in range(7):
            tap = 7 * (6 - turn_row) + 6 - turn_col
            small[tap : tap + 1, :] = jnp.sum(parts_here[turn_row], axis=0, keepdims=True)
    small[49:51, :] = norm_sums[0:2, lanes]
    small[51:52, :] = jnp.sum(bias_sum, axis=0, keepdims=True)
    small[52:53, :] = up_first_ref[...]
    small[53:54, :] = up_second_ref[...]
    small[54:, :] = jnp.zeros((SMALL_ROWS - 54, LANES), jnp.float32)
    sums_ref[0] = small[...].astype(jnp.bfloat16)
    for row in range(side):
        out_ref[0, row] = sums[row].astype(jnp.bfloat16)


def back(core, away, near, w_up, unit, sigma, gain, up_sums, image, residual, taps, parts=4):
    cells, feat = unit.shape
    side = image.shape[1]
    width = w_up.shape[1] // parts
    whole = pl.BlockSpec(memory_space=pltpu.VMEM)
    remain = pl.BlockSpec(memory_space=pl.ANY)
    picture = pl.BlockSpec((1, side, side, LANES), lambda i: (0, 0, 0, i))
    return pl.pallas_call(
        back_kernel,
        name="back",
        grid=(feat // LANES,),
        in_specs=[pl.BlockSpec(memory_space=pltpu.SMEM)]
        + [whole] * 4
        + [
            pl.BlockSpec((1, LANES), lambda i: (0, i)),
            pl.BlockSpec((1, LANES), lambda i: (0, i + feat // LANES)),
            picture,
            picture,
            pl.BlockSpec((49, LANES), lambda i: (0, i)),
            remain,
            remain,
        ],
        out_specs=[picture, pl.BlockSpec((1, SMALL_ROWS, LANES), lambda i: (i, 0, 0))],
        out_shape=(
            jax.ShapeDtypeStruct(image.shape, jnp.bfloat16),
            jax.ShapeDtypeStruct((feat // LANES, SMALL_ROWS, LANES), jnp.bfloat16),
        ),
        scratch_shapes=[
            pltpu.VMEM((parts, feat, width), jnp.bfloat16),
            pltpu.VMEM((cells, feat), jnp.float32),
            pltpu.VMEM((cells, feat), jnp.float32),
            pltpu.VMEM((8, feat), jnp.float32),
            pltpu.VMEM((side, side + 2 * EDGE, LANES), jnp.float32),
            pltpu.VMEM((side, side, LANES), jnp.float32),
            pltpu.VMEM((SMALL_ROWS, LANES), jnp.float32),
            pltpu.SemaphoreType.DMA((1 + parts,)),
        ],
        compiler_params=pltpu.CompilerParams(vmem_limit_bytes=VMEM_LIMIT),
        cost_estimate=SMALL,
    )(core, away, near, sigma, gain, up_sums, up_sums, image, residual, taps, unit, w_up)


def finish_kernel(inverse_count, received_ref, owned_ref, up_ref, gain_ref, shift_ref, taps_ref, bias_ref):
    pieces, height, _ = received_ref.shape
    owned_rows, hid = owned_ref.shape
    blocks = hid // 2 // LANES
    share = height - owned_rows * blocks
    for core in range(2):
        total = received_ref[core, share:, :].astype(jnp.float32)
        for z in range(1, pieces // 2):
            total = total + received_ref[2 * z + core, share:, :].astype(jnp.float32)
        total = total * inverse_count
        for row in range(owned_rows):
            for block in range(blocks):
                first = (core * blocks + block) * LANES
                index = row * blocks + block
                owned_ref[row : row + 1, first : first + LANES] = total[index : index + 1]
    feat = gain_ref.shape[0]
    for block in range(feat // LANES):
        parts = []
        row, end = block * SMALL_ROWS, (block + 1) * SMALL_ROWS
        while row < end:
            stop = min(end, (row // share + 1) * share)
            first = row % share
            parts.append(received_ref[row // share, first : first + stop - row, :].astype(jnp.float32))
            row = stop
        values = jnp.concatenate(parts, axis=0)
        lanes = slice(block * LANES, (block + 1) * LANES)
        taps_ref[:, lanes] = values[:49]
        gain_ref[lanes] = values[49]
        shift_ref[lanes] = values[50]
        bias_ref[lanes] = values[51]
        up_ref[lanes] = values[52]
        up_ref[feat + block * LANES : feat + (block + 1) * LANES] = values[53]


def finish(received, owned_rows, feat, hid, inverse_count):
    row = jax.ShapeDtypeStruct((feat,), jnp.float32)
    return pl.pallas_call(
        functools.partial(finish_kernel, inverse_count),
        name="finish",
        out_shape=(
            jax.ShapeDtypeStruct((owned_rows, hid), jnp.float32),
            jax.ShapeDtypeStruct((hid,), jnp.float32),
            row,
            row,
            jax.ShapeDtypeStruct((49, feat), jnp.float32),
            row,
        ),
        compiler_params=pltpu.CompilerParams(vmem_limit_bytes=VMEM_LIMIT),
        cost_estimate=SMALL,
    )(received)


def swap_pieces(values, axes):
    return lax.all_to_all(values, axes, 0, 0, tiled=True)


def total_of(received):
    return jnp.sum(received.astype(jnp.float32), axis=0)


def per_device(images, hidden_cot, residual_cot, w_up, b_up, ln_gain, ln_bias, dw_weight, dw_bias):
    feat, hid = w_up.shape
    plane = ("x", "y_hi", "y_lo")
    along_z = lax.axis_size("z")
    owned_rows = feat // (32 * along_z)
    inverse_count = 1.0 / (images.shape[0] * 32 * along_z)
    mine = lax.axis_index("core").astype(jnp.int32).reshape(1)
    y_index = 2 * lax.axis_index("y_hi") + lax.axis_index("y_lo")
    place = jnp.stack([lax.axis_index("x"), y_index]).astype(jnp.int32)
    swap = [(0, 1), (1, 0)]

    unit, sigma, turned, away, near, up_sums = front(
        mine, images, dw_weight, dw_bias, ln_gain, ln_bias, w_up, b_up.reshape(1, -1), hidden_cot, along_z
    )
    far = lax.ppermute(away, "core", swap)
    far_turned = lax.ppermute(turned, "core", swap)
    cells = unit.shape[0]
    *part_a, part_b = product(
        place, turned.reshape(4, 4, -1, cells), far_turned.reshape(4, 4, -1, cells), near, far, 7 * hid // 24
    )
    part_b, unit = lax.optimization_barrier((part_b, unit))
    part_a = to_owners(part_a, "x")
    part_b = swap_pieces(part_b, ("y_hi", "y_lo"))

    grad_input, small = back(
        mine, away, near, w_up, unit, sigma, ln_gain, up_sums, images, residual_cot, dw_weight
    )
    part_b, small = lax.optimization_barrier((part_b, small))

    around = ("z", "core")
    small = swap_pieces(small.reshape(2 * along_z, -1, LANES), around)
    small = total_of(small).astype(jnp.bfloat16)
    part_a, small = lax.optimization_barrier((part_a, small))
    small = swap_pieces(jnp.broadcast_to(small, (16,) + small.shape), plane)

    part_b = to_owners(sum_pieces([part_b]), "x")
    part_b[1], part_a = lax.optimization_barrier((part_b[1], part_a))
    part_a = to_owners(sum_pieces(part_a), ("y_lo", "y_hi"))
    last = jnp.concatenate([total_of(jnp.stack(part_a)), total_of(jnp.stack(part_b))], axis=1)
    last = last.astype(jnp.bfloat16).reshape(2 * along_z, -1, LANES)
    small = (total_of(small) * inverse_count).astype(jnp.bfloat16)
    small = jnp.broadcast_to(small, (2 * along_z,) + small.shape)
    last = swap_pieces(jnp.concatenate([small, last], axis=1), around)
    return (grad_input, *finish(last, owned_rows, feat, hid, inverse_count))


def solution(mesh):
    x, z = 4, mesh.devices.size // 32
    split = Mesh(mesh.devices.reshape(2, x, z, 2, 2), ("y_lo", "x", "z", "y_hi", "core"))
    images = P(("y_lo", "x", "z", "y_hi", "core"))
    return jax.shard_map(
        per_device,
        mesh=split,
        in_specs=(images, images, images, P(), P(), P(), P(), P(), P()),
        out_specs=(images, images, P(), P(), P(), P(), P()),
        check_vma=False,
    )
```
